256 devices in a mesh: seq: 64 (over y, x, z_hi, core), fs: 4 (over z_lo).
Axes of the slice: x: 4, y: 4, z: 8 (z_hi: 2, z_lo: 4; z = z_hi * 4 + z_lo), core: 2. Of those that a mesh axis runs over, the one named last changes fastest.
Arguments:
- hidden: bfloat16 [16384, 8192], P(('seq', 'fs')), may hold values from -6 to 6
- norm_gain: bfloat16 [8192], replicated, may hold values from 0.099609375 to 1.8984375
- kv_weight: bfloat16 [8192, 1024], P('seq', 'fs'), may hold values from -0.0625 to 0.0625
- queries: bfloat16 [16384, 4096], P('seq', 'fs'), may hold values from -136 to 136
- segment_ids: int32 [16384], P('seq'), may hold values from 0 to 3, never falling along the last dimension, each value on 1 to 8192 neighbouring positions
- page_owner: int32 [4096, 1], P('seq'), may hold values from 0 to 63; in each aligned block of 64 rows (0 to 63, 64 to 127, ...) at most 2 rows name the same one
Outputs:
- attended: bfloat16 [16384, 4096], P('seq', 'fs')
- kv_cache: bfloat16 [64, 64, 2, 4, 1024], P('seq', None, None, None, 'fs')
The draws below stay inside these ranges and needn't reach their ends.
Inputs may be any that keep to these rules, and one draw needn't show every extreme that they name: `segment_ids`: prompt ids never fall along the stream; each of the 4 prompts holds 1 to 8192 tokens and one holds exactly 8192. `page_owner`: among the 64 pages of one block no owner is named more than 2 times, a bound that some block reaches.
All inputs are finite; a program needn't handle non-finite values.
Results may differ from the reference program's by a relative error of at most 0.01.
The reference program's roundings to bfloat16 on the way count: a program that leaves them out, or rounds other values in their place, can miss the bound.
Values may be sent and summed in bfloat16 or wider, within the bound.
A program may use at most 64 MiB of HBM per device.

```python
import math
import jax
import jax.numpy as jnp
import numpy as np
from jax import lax

D = 8192
HD = 128
QH = 32
KVH = 4
PAGE = 4
SEGS = 4
TOKENS = 16384
BLOCK = 256
MAXLEN = 8192
HOPS = 32
NPAGES = 4096
PAGES_BLK = 64
CAP = 2
N_SEQ = 64


def draw_queries(key, part):
    values = jax.random.normal(key, (TOKENS, QH * HD), jnp.float32)
    return jnp.clip(values, -6.0, 6.0).astype(jnp.bfloat16)


def steps_of(rng, shape, cuts, low, top_value):
    factor_of, own = 1.0, jax.random.fold_in(rng, 6)
    for axis_at, blocks in cuts:
        heights = jnp.exp(jax.random.uniform(jax.random.fold_in(own, axis_at), (blocks,), jnp.float32, low / len(cuts), top_value / len(cuts)))
        factor_of = factor_of * jnp.repeat(heights, shape[axis_at] // blocks).reshape([-1 if axis == axis_at else 1 for axis in range(len(shape))])
    return factor_of


def profile(amount, total, most, slope):
    loads = [(1 << 20) // math.isqrt(standing ** slope) + 1 for standing in range(2, amount + 1)]
    spare, given = total - most - (amount - 1), [1] * (amount - 1)
    while spare > 0:
        candidates = [i for i in range(amount - 1) if given[i] < most]
        whole, remaining = sum([loads[i] for i in candidates]), spare
        for i in candidates:
            addition = min(most - given[i], max(1, remaining * loads[i] // whole), spare)
            given[i] = given[i] + addition
            spare = spare - addition
    return np.array([most] + given)


def uneven(own_key, number_of, total, bound, slope):
    if number_of == 2:
        one = jax.random.randint(own_key, (), max(1, total - bound), min(bound, total - 1) + 1)
        return jnp.stack([one, total - one])
    lengths = jnp.asarray(profile(number_of, total, bound, slope), jnp.int32)
    couples = (number_of - 1) // 2
    giver, taker = lengths[1:1 + 2 * couples:2], lengths[2:2 + 2 * couples:2]
    room = jnp.minimum(giver - 1, bound - taker)
    passed = jax.random.randint(jax.random.fold_in(own_key, 1), (couples,), 0, 1 << 20) % (room + 1)
    lengths = lengths.at[1:1 + 2 * couples:2].set(giver - passed).at[2:2 + 2 * couples:2].set(taker + passed)
    return lengths[jax.random.permutation(jax.random.fold_in(own_key, 2), number_of)]


def deal_out(key, own, number, rows, count, top, limit, slope):
    ranking = jax.random.permutation(key, count)
    heavy_load, common = portions_of(count, rows * top, limit, slope, True), portions_of(count, rows * top, limit, slope, False)
    places = jnp.arange(count)

    def named(tallies, offset_by):
        used = int((tallies > 0).sum())
        fixed = max(1, used // 4)
        moved = fixed + (places - fixed + offset_by * (used - fixed)) % max(1, count - fixed)
        return jnp.zeros((count,), jnp.int32).at[ranking[jnp.where(places < fixed, places, moved)]].set(jnp.asarray(tallies, jnp.int32))

    tallies = jnp.where(number % 4 == 0, named(heavy_load, number // 4), named(common, number - number // 4 - 1))
    mixed = jax.random.permutation(jax.random.fold_in(own, 3), count)
    giver, receiver = mixed[0:count // 2 * 2:2], mixed[1:count // 2 * 2:2]
    margin = jnp.minimum(tallies[giver] - 1, limit - tallies[receiver]) // 2
    margin = jnp.where((giver == ranking[0]) | (receiver == ranking[0]) | (tallies[receiver] == 0), 0, jnp.maximum(margin, 0))
    moved = jax.random.randint(jax.random.fold_in(own, 4), (count // 2,), 0, 1 << 20) % (margin + 1)
    tallies = tallies.at[giver].add(-moved).at[receiver].add(moved)
    items = jnp.searchsorted(jnp.cumsum(tallies), jnp.arange(rows * top), side="right").astype(jnp.int32)
    grid = items.reshape(top, rows).T
    grid = grid[jax.random.permutation(jax.random.fold_in(own, 1), rows)]
    offset_by = jax.random.randint(jax.random.fold_in(own, 2), (rows, 1), 0, top)
    return jnp.take_along_axis(grid, (jnp.arange(top)[None, :] + offset_by) % top, axis=1)


def portions_of(number_of, total, most, skew, full):
    weights = [(1 << 20) // math.isqrt(grade ** skew) + 1 for grade in range(1, number_of + 1)]
    largest = most if full else min(most, max(-(-total // number_of), total * weights[0] // sum(weights)))
    least = 1 if total - largest >= number_of - 1 else 0
    given, rest = [largest] + [least] * (number_of - 1), total - largest - least * (number_of - 1)
    while rest > 0:
        free = [i for i in range(1, number_of) if given[i] < largest] or [i for i in range(1, number_of) if given[i] < most]
        pool, left = sum([weights[i] for i in free]), rest
        for i in free:
            more = min(most - given[i], max(1, left * weights[i] // pool), rest)
            given[i] = given[i] + more
            rest = rest - more
    return np.array(given)


def centred(key, extent, deviation, bound, pieces=(), kind=jnp.bfloat16):
    values = deviation * jax.random.normal(key, extent, jnp.float32)
    if pieces:
        values = values * steps_of(key, extent, pieces, -0.22, 0.18)
    return jnp.clip(values, -bound, bound).astype(kind)


def setup_inputs(seed: int = 0) -> dict:
    seeds = jax.random.split(jax.random.key(seed), 7)
    hidden = centred(seeds[0], (TOKENS, D), 1.0, 6.0, ((0, 256),))
    norm_gain = jnp.clip(1.0 + 0.18 * jax.random.normal(seeds[1], (D,), jnp.float32), 0.099609375, 1.8984375).astype(jnp.bfloat16)
    kv_weight = centred(seeds[2], (D, 2 * KVH * HD), D ** -0.5, 0.0625, ((0, 64), (1, 4)))
    queries = draw_queries(jax.random.fold_in(seeds[6], 71), 0)
    segment_ids = jnp.searchsorted(jnp.cumsum(uneven(seeds[4], SEGS, TOKENS, MAXLEN, 2)), jnp.arange(TOKENS), side="right").astype(jnp.int32)
    page_owner_keys = jax.random.split(jax.random.fold_in(seeds[5], 1), NPAGES // PAGES_BLK)
    page_owner_turns = jax.random.permutation(jax.random.fold_in(seeds[5], 3), NPAGES // PAGES_BLK)
    page_owner = jax.vmap(lambda own, number: deal_out(jax.random.fold_in(seeds[5], 2), own, number, PAGES_BLK, N_SEQ, 1, CAP, 2))(page_owner_keys, page_owner_turns).reshape((NPAGES, 1))
    return {"hidden": hidden, "norm_gain": norm_gain, "kv_weight": kv_weight, "queries": queries, "segment_ids": segment_ids, "page_owner": page_owner}


EPSILON = 1e-05
NEGATIVE = -1e+30

def rotate_keys(keys, positions):
    half = keys.shape[-1] // 2
    freq = 10000.0 ** (-jnp.arange(half, dtype=jnp.float32) * 2.0 / keys.shape[-1])
    angle = positions.astype(jnp.float32)[:, None] * freq[None, :]
    cosine = jnp.cos(angle)[:, None, :]
    sine = jnp.sin(angle)[:, None, :]
    first = keys[..., :half]
    second = keys[..., half:]
    return jnp.concatenate([first * cosine - second * sine, second * cosine + first * sine], axis=-1)

def pair_keys(projected, positions, head_size):
    rows = projected.shape[0]
    pairs = projected.reshape(rows, -1, 2, head_size)
    turned = rotate_keys(pairs[:, :, 0], positions)
    return jnp.stack([turned, pairs[:, :, 1]], axis=2).reshape(rows, -1).astype(jnp.bfloat16)

def reference(hidden, norm_gain, kv_weight, queries, segment_ids, page_owner):
    wide = hidden.astype(jnp.float32)
    stat = lax.optimization_barrier(jnp.mean(wide * wide, axis=1, keepdims=True))
    normed = (wide * lax.rsqrt(stat + EPSILON) * norm_gain.astype(jnp.float32)[None, :]).astype(jnp.bfloat16)
    projected = jnp.dot(normed, kv_weight, preferred_element_type=jnp.float32)
    token_index = jnp.arange(TOKENS, dtype=jnp.int32)
    starts = jnp.full((SEGS,), TOKENS, jnp.int32).at[segment_ids].min(token_index)
    query_start = starts[segment_ids]
    positions = token_index - query_start
    kv_rows = pair_keys(projected, positions, HD)
    kv_four = kv_rows.reshape(TOKENS, KVH, 2, HD)
    padding = jnp.zeros((HOPS * BLOCK, KVH, HD), jnp.bfloat16)
    keys_all = jnp.concatenate([padding, kv_four[:, :, 0]], axis=0)
    values_all = jnp.concatenate([padding, kv_four[:, :, 1]], axis=0)
    window = (HOPS + 1) * BLOCK
    group = QH // KVH
    scale = HD ** (-0.5)

    def one_block(block_id):
        anchor = (block_id * BLOCK).astype(jnp.int32)
        query_block = lax.dynamic_slice_in_dim(queries, anchor, BLOCK, 0).reshape(BLOCK, KVH, group, HD).astype(jnp.float32)
        key_block = lax.dynamic_slice_in_dim(keys_all, anchor, window, 0).astype(jnp.float32)
        value_block = lax.dynamic_slice_in_dim(values_all, anchor, window, 0).astype(jnp.float32)
        key_index = anchor - HOPS * BLOCK + jnp.arange(window, dtype=jnp.int32)
        query_index = anchor + jnp.arange(BLOCK, dtype=jnp.int32)
        lower = lax.dynamic_slice_in_dim(query_start, anchor, BLOCK, 0)
        scores = jnp.einsum('qhgd,khd->hgqk', query_block, key_block) * scale
        allowed = (key_index[None, :] >= lower[:, None]) & (key_index[None, :] <= query_index[:, None])
        scores = jnp.where(allowed[None, None], scores, NEGATIVE)
        top = lax.optimization_barrier(jnp.max(scores, axis=-1, keepdims=True))
        weights = jnp.exp(scores - top)
        denominators = lax.optimization_barrier(jnp.sum(weights, axis=-1))
        rounded = lax.optimization_barrier(weights.astype(jnp.bfloat16)).astype(jnp.float32)
        summed = jnp.einsum('hgqk,khd->hgqd', rounded, value_block)
        result = summed / denominators[..., None]
        return result.transpose(2, 0, 1, 3).reshape(BLOCK, QH * HD).astype(jnp.bfloat16)
    attended = lax.map(one_block, jnp.arange(N_SEQ, dtype=jnp.int32)).reshape(TOKENS, QH * HD)
    pages = kv_rows.reshape(N_SEQ, PAGES_BLK, PAGE * 2 * KVH * HD)
    owners = page_owner[:, 0].reshape(N_SEQ, PAGES_BLK)
    order = jnp.arange(PAGES_BLK, dtype=jnp.int32)
    earlier = (owners[:, None, :] == owners[:, :, None]) & (order[None, None, :] < order[None, :, None])
    rank = lax.optimization_barrier(jnp.sum(earlier.astype(jnp.int32), axis=2)).astype(jnp.int32)
    source = jnp.broadcast_to(jnp.arange(N_SEQ, dtype=jnp.int32)[:, None], (N_SEQ, PAGES_BLK))
    cache = jnp.zeros((N_SEQ, N_SEQ, CAP, PAGE * 2 * KVH * HD), jnp.bfloat16)
    cache = cache.at[owners, source, rank].set(pages)
    kv_cache = cache.reshape(N_SEQ, N_SEQ, CAP, PAGE, 2 * KVH * HD)
    return (attended, kv_cache)
```

```python
import functools

import jax
import jax.numpy as jnp
from jax import lax
from jax.experimental import pallas as pl
from jax.experimental.pallas import tpu as pltpu
from jax.sharding import PartitionSpec as P

HD = 128
SEGS = 4
EPSILON = 1e-05
NEGATIVE = -1e30
LOG2E = 1.4426950408889634
MESH = pl.DeviceIdType.MESH
BLK = 256


def rotate_keys(keys, positions):
    half = keys.shape[-1] // 2
    freq = 10000.0 ** (-jnp.arange(half, dtype=jnp.float32) * 2.0 / keys.shape[-1])
    angle = positions.astype(jnp.float32)[:, None] * freq[None, :]
    cosine = jnp.cos(angle)[:, None, :]
    sine = jnp.sin(angle)[:, None, :]
    first = keys[..., :half]
    second = keys[..., half:]
    return jnp.concatenate(
        [first * cosine - second * sine, second * cosine + first * sine], axis=-1
    )


def pair_keys(projected, positions, head_size):
    rows = projected.shape[0]
    pairs = projected.reshape(rows, -1, 2, head_size)
    turned = rotate_keys(pairs[:, :, 0], positions)
    return jnp.stack([turned, pairs[:, :, 1]], axis=2).reshape(rows, -1).astype(jnp.bfloat16)


class Place:
    def __init__(self):
        s = lax.axis_index("seq")
        self.s = s
        self.f = lax.axis_index("fs")
        self.c = lax.rem(s, 2)
        self.z = lax.rem(lax.div(s, 2), 2)
        self.x = lax.rem(lax.div(s, 4), 4)
        self.y = lax.div(s, 16)

    def at(self, dy=0, dx=0, other_z=False, other_core=False):
        y = lax.rem(self.y + dy, 4)
        x = lax.rem(self.x + dx, 4)
        z = 1 - self.z if other_z else self.z
        c = 1 - self.c if other_core else self.c
        return (((y * 4 + x) * 2 + z) * 2 + c, self.f)


def remote(src, dst, send, recv, target):
    return pltpu.make_async_remote_copy(
        src_ref=src, dst_ref=dst, send_sem=send, recv_sem=recv, device_id=target, device_id_type=MESH
    )


def attend_kernel(
    kv_ref, q_ref, qseg_ref, bounds_ref, out_ref, buf, qa, kaug, m_ref, l_ref, acc_ref, ss, rs
):
    me = Place()
    c, z, x = me.c, me.z, me.x
    heads = q_ref.shape[1] // HD
    scale2 = (HD ** (-0.5)) * LOG2E

    core = me.at(other_core=True)
    opposite = me.at(other_z=True)
    partners = [core, opposite] + [me.at(dy=k) for k in (1, 2, 3)] + [me.at(dx=k) for k in (1, 2, 3)]
    barrier = pltpu.get_barrier_semaphore()
    for partner in partners:
        pl.semaphore_signal(barrier, inc=1, device_id=partner, device_id_type=MESH)
    buf[0, 0, z, c] = kv_ref[...]
    pl.semaphore_wait(barrier, len(partners))

    started = []

    def send(index, src, dst, target):
        copy = remote(src, dst, ss.at[index], rs.at[index], target)
        copy.start()
        started.append(copy)

    def arrived(index, dst):
        remote(dst, dst, ss.at[index], rs.at[index], core).wait_recv()

    send(0, kv_ref, buf.at[0, 0, z, c], core)
    send(1, kv_ref, buf.at[0, 0, z, c], opposite)

    for h in range(heads):
        qa[h, :, 0:HD] = q_ref[:, h * HD : (h + 1) * HD]
        qa[h, :, HD : 2 * HD] = qseg_ref[...]
        m_ref[h] = jnp.full((BLK, HD), NEGATIVE, jnp.float32)
        l_ref[h] = jnp.zeros((BLK, HD), jnp.float32)
        acc_ref[h] = jnp.zeros((BLK, HD), jnp.float32)

    low = bounds_ref[0:1, :]
    high = bounds_ref[1:2, :]
    quad_first = (me.y * 4 + x) * 4 * BLK
    token = me.s * BLK + lax.broadcasted_iota(jnp.int32, (BLK, 1), 0)

    def fold(blocks, first_key, causal):
        count = len(blocks) * BLK
        for i, block in enumerate(blocks):
            rows = pl.ds(i * BLK, BLK)
            kaug[rows, 0:HD] = block[:, 0:HD]
            key = first_key + i * BLK + lax.broadcasted_iota(jnp.int32, (BLK, HD), 0)
            inside = (key >= low) & (key < high)
            kaug[rows, HD : 2 * HD] = jnp.where(inside, 0.0, NEGATIVE).astype(jnp.bfloat16)
        values = jnp.concatenate([block[:, HD : 2 * HD] for block in blocks], axis=0)
        key_row = first_key + lax.broadcasted_iota(jnp.int32, (1, count), 1)

        def one_head(h, carry):
            scores = lax.dot_general(
                qa[h],
                kaug[0:count, :],
                (((1,), (1,)), ((), ())),
                preferred_element_type=jnp.float32,
            )
            if causal:
                scores = jnp.where(key_row <= token, scores, NEGATIVE)
            old = m_ref[h]
            new = jnp.maximum(old, jnp.max(scores, axis=1, keepdims=True))
            weights = jnp.exp2(scores * scale2 - new[:, 0:1] * scale2)
            factor = jnp.exp2((old - new) * scale2)
            m_ref[h] = new
            l_ref[h] = l_ref[h] * factor + jnp.sum(weights, axis=1, keepdims=True)
            update = jnp.dot(
                weights.astype(jnp.bfloat16), values, preferred_element_type=jnp.float32
            )
            acc_ref[h] = acc_ref[h] * factor + update
            return carry

        lax.fori_loop(0, heads, one_head, 0, unroll=2)

    def quad(rx, k):
        return [buf.at[rx, k, zz, cc] for zz in range(2) for cc in range(2)]

    arrived(0, buf.at[0, 0, z, 1 - c])
    fold([buf.at[0, 0, z, 0], buf.at[0, 0, z, 1]], quad_first + z * 2 * BLK, True)

    arrived(1, buf.at[0, 0, 1 - z, c])
    mine = lambda rx, k: buf.at[rx, k, :, c]
    send(2, buf.at[0, 0, 1 - z, c], buf.at[0, 0, 1 - z, c], core)
    send(3, mine(0, 0), mine(0, 1), me.at(dy=1))
    send(4, mine(0, 0), mine(0, 2), me.at(dy=2))
    arrived(2, buf.at[0, 0, 1 - z, 1 - c])
    fold([buf.at[0, 0, 1 - z, 0], buf.at[0, 0, 1 - z, 1]], quad_first + (1 - z) * 2 * BLK, True)

    order = (1, 3, 2)
    other = lambda rx, k: buf.at[rx, k, :, 1 - c]
    out_wrap = {rx: lax.div(x + rx, 4) for rx in order}
    in_wrap = {rx: jnp.where(x < rx, 1, 0) for rx in order}

    arrived(3, mine(0, 1))
    send(5, mine(0, 1), mine(0, 1), core)
    for rx in order:
        send(6 + rx, mine(0, 1), mine(rx, 1 - out_wrap[rx]), me.at(dx=rx))
    arrived(4, mine(0, 2))
    send(6, mine(0, 2), mine(0, 2), core)
    for rx in order:
        send(9 + rx, mine(0, 2 * out_wrap[rx]), mine(rx, out_wrap[rx]), me.at(dx=rx))
    arrived(5, other(0, 1))
    fold(quad(0, 1), quad_first - 16 * BLK, False)
    arrived(6, other(0, 2))
    fold(quad(0, 2), quad_first - 32 * BLK, False)

    stages = [(6 + rx, 12 + rx, rx, 1 - in_wrap[rx]) for rx in order]
    stages += [(9 + rx, 15 + rx, rx, in_wrap[rx]) for rx in order]

    def forward(stage):
        first, second, rx, k = stage
        arrived(first, mine(rx, k))
        send(second, mine(rx, k), mine(rx, k), core)

    forward(stages[0])
    for i, (first, second, rx, k) in enumerate(stages):
        if i + 1 < len(stages):
            forward(stages[i + 1])
        arrived(second, other(rx, k))
        fold(quad(rx, k), quad_first - (rx + 4 * k) * 4 * BLK, False)

    for h in range(heads):
        out_ref[:, h * HD : (h + 1) * HD] = (acc_ref[h] / l_ref[h]).astype(out_ref.dtype)
    for copy in started:
        copy.wait_send()


def attend(kv_block, queries, query_onehot, bounds):
    heads = queries.shape[1] // HD
    vmem = pl.BlockSpec(memory_space=pltpu.VMEM)
    return pl.pallas_call(
        attend_kernel,
        out_shape=jax.ShapeDtypeStruct(queries.shape, jnp.bfloat16),
        in_specs=[vmem] * 4,
        out_specs=vmem,
        scratch_shapes=[
            pltpu.VMEM((4, 3, 2, 2, BLK, 2 * HD), jnp.bfloat16),
            pltpu.VMEM((heads, BLK, 2 * HD), jnp.bfloat16),
            pltpu.VMEM((4 * BLK, 2 * HD), jnp.bfloat16),
            pltpu.VMEM((heads, BLK, HD), jnp.float32),
            pltpu.VMEM((heads, BLK, HD), jnp.float32),
            pltpu.VMEM((heads, BLK, HD), jnp.float32),
            pltpu.SemaphoreType.DMA((19,)),
            pltpu.SemaphoreType.DMA((19,)),
        ],
        compiler_params=pltpu.CompilerParams(
            collective_id=0, has_side_effects=True, vmem_limit_bytes=48 << 20
        ),
        cost_estimate=pl.CostEstimate(
            flops=9_000_000_000, bytes_accessed=2_000_000, transcendentals=17_000_000
        ),
    )(kv_block, queries, query_onehot, bounds)


def on_device(hidden, norm_gain, kv_weight, queries, segment_ids, page_owner):
    seq_count = lax.axis_size("seq")
    seq_place = lax.axis_index("seq")
    block_rows = segment_ids.shape[0]
    stream_rows = block_rows * seq_count
    anchor = seq_place * block_rows
    token_index = anchor + jnp.arange(block_rows, dtype=jnp.int32)
    labels = jnp.arange(SEGS, dtype=jnp.int32)
    member = segment_ids[:, None] == labels[None, :]
    firsts = jnp.min(jnp.where(member, token_index[:, None], stream_rows), axis=0)
    starts = lax.pmin(firsts, "seq")
    query_start = jnp.sum(jnp.where(member, starts[None, :], 0), axis=1)
    positions = token_index - query_start
    wide = hidden.astype(jnp.float32)
    stat = jnp.mean(wide * wide, axis=1, keepdims=True)
    normed = (wide * lax.rsqrt(stat + EPSILON) * norm_gain.astype(jnp.float32)[None, :]).astype(
        jnp.bfloat16
    )
    gathered = lax.all_gather(normed, "fs", axis=0, tiled=True)
    projected = jnp.dot(
        gathered,
        lax.all_gather(kv_weight, "seq", axis=0, tiled=True),
        preferred_element_type=jnp.float32,
    )
    kv_block = pair_keys(projected, positions, HD)

    lanes = jnp.arange(HD, dtype=jnp.int32)
    query_onehot = (segment_ids[:, None] == lanes[None, :]).astype(jnp.bfloat16)
    low = jnp.full((HD,), stream_rows, jnp.int32).at[:SEGS].set(starts)
    high = jnp.full((HD,), stream_rows, jnp.int32).at[: SEGS - 1].set(starts[1:])
    bounds = jnp.zeros((8, HD), jnp.int32).at[0].set(low).at[1].set(high)
    attended = attend(kv_block, queries, query_onehot, bounds)

    pages_block = page_owner.shape[0]
    page_rows = block_rows // pages_block
    capacity = max(2, 2 * pages_block // seq_count)
    owners = page_owner[:, 0]
    order = jnp.arange(pages_block, dtype=jnp.int32)
    earlier = (owners[None, :] == owners[:, None]) & (order[None, :] < order[:, None])
    rank = jnp.sum(earlier.astype(jnp.int32), axis=1)
    target = owners * capacity + rank
    select = (jnp.arange(seq_count * capacity, dtype=jnp.int32)[:, None] == target[None, :]).astype(
        jnp.bfloat16
    )
    columns_dev = kv_block.shape[1]
    pages = kv_block.reshape(pages_block, page_rows * columns_dev)
    outgoing = jnp.dot(select, pages, preferred_element_type=jnp.float32).astype(jnp.bfloat16)
    outgoing = outgoing.reshape(seq_count, capacity, page_rows, columns_dev)
    arrived = lax.all_to_all(outgoing, "seq", split_axis=0, concat_axis=0, tiled=True)
    kv_cache = arrived.reshape(1, seq_count, capacity, page_rows, columns_dev)
    return (attended, kv_cache)


def solution(mesh):
    placed = (P(("seq", "fs"), None), P(), P("seq", "fs"), P("seq", "fs"), P("seq"), P("seq", None))
    return jax.shard_map(
        on_device,
        mesh=mesh,
        in_specs=placed,
        out_specs=(P("seq", "fs"), P("seq", None, None, None, "fs")),
        check_vma=False,
    )
```

```python
import functools

import jax
import jax.numpy as jnp
from jax import lax
from jax.experimental import pallas as pl
from jax.experimental.pallas import tpu as pltpu
from jax.sharding import PartitionSpec as P

HD = 128
SEGS = 4
EPSILON = 1e-05
NEGATIVE = -1e30
LOG2E = 1.4426950408889634
MESH = pl.DeviceIdType.MESH
BLK = 256


def rotate_keys(keys, positions):
    half = keys.shape[-1] // 2
    freq = 10000.0 ** (-jnp.arange(half, dtype=jnp.float32) * 2.0 / keys.shape[-1])
    angle = positions.astype(jnp.float32)[:, None] * freq[None, :]
    cosine = jnp.cos(angle)[:, None, :]
    sine = jnp.sin(angle)[:, None, :]
    first = keys[..., :half]
    second = keys[..., half:]
    return jnp.concatenate(
        [first * cosine - second * sine, second * cosine + first * sine], axis=-1
    )


def pair_keys(projected, positions, head_size):
    rows = projected.shape[0]
    pairs = projected.reshape(rows, -1, 2, head_size)
    turned = rotate_keys(pairs[:, :, 0], positions)
    return jnp.stack([turned, pairs[:, :, 1]], axis=2).reshape(rows, -1).astype(jnp.bfloat16)


class Place:
    def __init__(self):
        s = lax.axis_index("seq")
        self.s = s
        self.f = lax.axis_index("fs")
        self.c = lax.rem(s, 2)
        self.z = lax.rem(lax.div(s, 2), 2)
        self.x = lax.rem(lax.div(s, 4), 4)
        self.y = lax.div(s, 16)

    def at(self, dy=0, dx=0, other_z=False, other_core=False):
        y = lax.rem(self.y + dy, 4)
        x = lax.rem(self.x + dx, 4)
        z = 1 - self.z if other_z else self.z
        c = 1 - self.c if other_core else self.c
        return (((y * 4 + x) * 2 + z) * 2 + c, self.f)


def remote(src, dst, send, recv, target):
    return pltpu.make_async_remote_copy(
        src_ref=src, dst_ref=dst, send_sem=send, recv_sem=recv, device_id=target, device_id_type=MESH
    )


def project_kernel(
    hid_ref, gain_ref, w_ref, first_ref, out_ref, starts_ref, nb, wb, fb, acc, res, got, ss, rs
):
    me = Place()
    c, z, x, y, f = me.c, me.z, me.x, me.y, me.f
    parity, group = lax.rem(f, 2), lax.div(f, 2)
    head = parity + 2 * c
    twin = lax.rem(f + 2, 4)
    mate = f + 1 - 2 * parity
    home = c == group
    chunks, rows, cols = nb.shape[2], nb.shape[3], nb.shape[4]

    def near(zz, cc, ff):
        return (((y * 4 + x) * 2 + zz) * 2 + cc, ff)

    core = near(z, 1 - c, f)
    ring_x = {k: me.at(dx=k) for k in (1, 2, 3)}
    ring_y = {k: me.at(dy=k) for k in (1, 2, 3)}
    cube = [near(zz, cc, ff) for ff in (f, twin) for zz in (z, 1 - z) for cc in (c, 1 - c)][1:]
    partners = cube + [near(z, c, mate)] + list(ring_x.values()) + list(ring_y.values())
    barrier = pltpu.get_barrier_semaphore()
    for partner in partners:
        pl.semaphore_signal(barrier, inc=1, device_id=partner, device_id_type=MESH)
    pl.semaphore_wait(barrier, len(partners))

    started = []

    def send(index, src, dst, target, recv=None):
        recv = index if recv is None else recv
        copy = remote(src, dst, ss.at[index], rs.at[recv], target)
        copy.start()
        started.append(copy)

    def arrived(index, dst):
        remote(dst, dst, ss.at[index], rs.at[index], core).wait_recv()

    quad = y * 4 + x
    shard = 2 * z + c
    rows_w = w_ref.shape[0]

    def piece(zz, cc):
        return wb.at[quad, zz, pl.ds(pl.multiple_of(cc * rows_w, rows_w), rows_w)]

    def seed_to_core():
        return remote(w_ref, piece(z, c), ss.at[0], rs.at[shard], core)

    @pl.when(home)
    def _():
        wb[quad, z, pl.ds(pl.multiple_of(c * rows_w, rows_w), rows_w)] = w_ref[...]

    @pl.when(jnp.logical_not(home))
    def _():
        seed_to_core().start()

    send(1, w_ref, piece(z, c), near(z, group, twin), shard)
    send(2, w_ref, piece(z, c), near(1 - z, group, f), shard)
    send(3, w_ref, piece(z, c), near(1 - z, group, twin), shard)
    send(4, first_ref, fb.at[0], core)
    send(5, first_ref, fb.at[1], near(1 - z, c, f))
    send(6, first_ref, fb.at[2], near(1 - z, 1 - c, f))

    total = jnp.zeros((rows, 1), jnp.float32)
    for i in range(chunks):
        wide = hid_ref[:, i * cols : (i + 1) * cols].astype(jnp.float32)
        total = total + jnp.sum(wide * wide, axis=1, keepdims=True)
    factor = lax.rsqrt(total / (chunks * cols) + EPSILON)
    for i in range(chunks):
        wide = hid_ref[:, i * cols : (i + 1) * cols].astype(jnp.float32)
        gain = gain_ref[:, i * cols : (i + 1) * cols].astype(jnp.float32)
        nb[c, parity, i] = (wide * factor * gain).astype(jnp.bfloat16)
        send(13 + i, nb.at[c, parity, i], nb.at[c, parity, i], near(z, c, mate))
        send(17 + i, nb.at[c, parity, i], nb.at[c, parity, i], core)

    def seed_arrived(zz):
        for cc in (0, 1):
            own = jnp.logical_and(home, shard == 2 * zz + cc)

            @pl.when(jnp.logical_not(own))
            def _():
                arrived(2 * zz + cc, piece(zz, cc))

    half = lambda yy, xx, hh: wb.at[yy * 4 + xx, hh]
    back = lambda v, k: lax.rem(v + 4 - k, 4)
    order = (1, 3, 2)
    seed_arrived(0)
    for k in order:
        send(24 + k, half(y, x, 0), half(y, x, 0), ring_x[k])
    seed_arrived(1)
    for k in order:
        send(27 + k, half(y, x, 1), half(y, x, 1), ring_y[k])

    a2 = lambda k, j: 31 + (k - 1) * 4 + j
    b2 = lambda k, j: 43 + (k - 1) * 4 + j

    def spread(j):
        ya, xa = y, back(x, j)
        yb, xb = back(y, j), x
        if j:
            arrived(24 + j, half(ya, xa, 0))
        for k in order:
            send(a2(k, j), half(ya, xa, 0), half(ya, xa, 0), ring_y[k])
        if j:
            arrived(27 + j, half(yb, xb, 1))
        for k in order:
            send(b2(k, j), half(yb, xb, 1), half(yb, xb, 1), ring_x[k])

    def forward(i):
        arrived(13 + i, nb.at[c, 1 - parity, i])
        send(21 + i, nb.at[c, 1 - parity, i], nb.at[c, 1 - parity, i], core)

    spread(0)
    for i in range(3):
        arrived(4 + i, fb.at[i])
    fb[3] = jnp.minimum(jnp.minimum(first_ref[...], fb[0]), jnp.minimum(fb[1], fb[2]))
    for k in order:
        send(6 + k, fb.at[3], fb.at[3 + k], ring_x[k])
    forward(0)
    spread(1)
    spread(3)
    forward(1)
    spread(2)
    for k in order:
        arrived(6 + k, fb.at[3 + k])
    fb[7] = jnp.minimum(jnp.minimum(fb[3], fb[4]), jnp.minimum(fb[5], fb[6]))
    for k in order:
        send(9 + k, fb.at[7], fb.at[7 + k], ring_y[k])
    forward(2)
    forward(3)
    for k in order:
        arrived(9 + k, fb.at[7 + k])
    starts_ref[...] = jnp.minimum(jnp.minimum(fb[7], fb[8]), jnp.minimum(fb[9], fb[10]))
    for i in range(chunks):
        arrived(17 + i, nb.at[1 - c, parity, i])
        arrived(21 + i, nb.at[1 - c, 1 - parity, i])

    acc[...] = jnp.zeros_like(acc)

    def multiply(yy, xx, hh):
        columns = pl.ds(pl.multiple_of(xx * 512 + hh * 256, 256), 256)
        lhs = nb[:, :, yy, :, columns].reshape(4 * rows, 256)
        acc[...] += jnp.dot(lhs, wb[yy * 4 + xx, hh], preferred_element_type=jnp.float32)

    multiply(y, x, 0)
    multiply(y, x, 1)
    for j in order:
        multiply(y, back(x, j), 0)
        multiply(back(y, j), x, 1)
    for j in (0, 1, 3, 2):
        for k in order:
            yy, xx = back(y, k), back(x, j)
            arrived(a2(k, j), half(yy, xx, 0))
            multiply(yy, xx, 0)
            yy, xx = back(y, j), back(x, k)
            arrived(b2(k, j), half(yy, xx, 1))
            multiply(yy, xx, 1)

    res[...] = acc[...].reshape(res.shape)

    def result_to(cc, ff, index):
        return remote(res.at[cc], got.at[group], ss.at[index], rs.at[55 + group], near(z, cc, ff))

    @pl.when(home)
    def _():
        result_to(1 - c, f, 55).start()
        got[group] = res[c]

    @pl.when(jnp.logical_not(home))
    def _():
        result_to(0, twin, 55).start()
        result_to(1, twin, 56).start()

    for g in (0, 1):

        @pl.when(jnp.logical_not(jnp.logical_and(home, group == g)))
        def _():
            arrived(55 + g, got.at[g])

    out_ref[...] = got[...].reshape(out_ref.shape)
    for copy in started:
        copy.wait_send()

    @pl.when(home)
    def _():
        result_to(1 - c, f, 55).wait_send()

    @pl.when(jnp.logical_not(home))
    def _():
        seed_to_core().wait_send()
        result_to(0, twin, 55).wait_send()
        result_to(1, twin, 56).wait_send()


def project(hidden, gain, weight, firsts):
    rows, width = hidden.shape
    columns = weight.shape[1]
    vmem = pl.BlockSpec(memory_space=pltpu.VMEM)
    return pl.pallas_call(
        project_kernel,
        out_shape=(
            jax.ShapeDtypeStruct((4 * rows, columns), jnp.float32),
            jax.ShapeDtypeStruct((8, HD), jnp.int32),
        ),
        in_specs=[vmem] * 4,
        out_specs=(vmem, vmem),
        scratch_shapes=[
            pltpu.VMEM((2, 2, 4, rows, width // 4), jnp.bfloat16),
            pltpu.VMEM((16, 2, width // 32, columns), jnp.bfloat16),
            pltpu.VMEM((11, 8, HD), jnp.int32),
            pltpu.VMEM((4 * rows, columns), jnp.float32),
            pltpu.VMEM((2, 2 * rows, columns), jnp.float32),
            pltpu.VMEM((2, 2 * rows, columns), jnp.float32),
            pltpu.SemaphoreType.DMA((57,)),
            pltpu.SemaphoreType.DMA((57,)),
        ],
        compiler_params=pltpu.CompilerParams(
            collective_id=1, has_side_effects=True, vmem_limit_bytes=48 << 20
        ),
        cost_estimate=pl.CostEstimate(
            flops=1_100_000_000, bytes_accessed=2_000_000, transcendentals=0
        ),
    )(hidden, gain, weight, firsts)


def attend_kernel(
    kv_ref, q_ref, qseg_ref, bounds_ref, out_ref, buf, qa, kaug, m_ref, l_ref, acc_ref, ss, rs
):
    me = Place()
    c, z, x = me.c, me.z, me.x
    heads = q_ref.shape[1] // HD
    scale2 = (HD ** (-0.5)) * LOG2E

    core = me.at(other_core=True)
    opposite = me.at(other_z=True)
    partners = [core, opposite] + [me.at(dy=k) for k in (1, 2, 3)] + [me.at(dx=k) for k in (1, 2, 3)]
    barrier = pltpu.get_barrier_semaphore()
    for partner in partners:
        pl.semaphore_signal(barrier, inc=1, device_id=partner, device_id_type=MESH)
    buf[0, 0, z, c] = kv_ref[...]
    pl.semaphore_wait(barrier, len(partners))

    started = []

    def send(index, src, dst, target):
        copy = remote(src, dst, ss.at[index], rs.at[index], target)
        copy.start()
        started.append(copy)

    def arrived(index, dst):
        remote(dst, dst, ss.at[index], rs.at[index], core).wait_recv()

    send(0, kv_ref, buf.at[0, 0, z, c], core)
    send(1, kv_ref, buf.at[0, 0, z, c], opposite)

    for h in range(heads):
        qa[h, :, 0:HD] = q_ref[:, h * HD : (h + 1) * HD]
        qa[h, :, HD : 2 * HD] = qseg_ref[...]
        m_ref[h] = jnp.full((BLK, HD), NEGATIVE, jnp.float32)
        l_ref[h] = jnp.zeros((BLK, HD), jnp.float32)
        acc_ref[h] = jnp.zeros((BLK, HD), jnp.float32)

    low = bounds_ref[0:1, :]
    high = bounds_ref[1:2, :]
    quad_first = (me.y * 4 + x) * 4 * BLK
    token = me.s * BLK + lax.broadcasted_iota(jnp.int32, (BLK, 1), 0)

    def fold(blocks, first_key, causal):
        count = len(blocks) * BLK
        for i, block in enumerate(blocks):
            rows = pl.ds(i * BLK, BLK)
            kaug[rows, 0:HD] = block[:, 0:HD]
            key = first_key + i * BLK + lax.broadcasted_iota(jnp.int32, (BLK, HD), 0)
            inside = (key >= low) & (key < high)
            kaug[rows, HD : 2 * HD] = jnp.where(inside, 0.0, NEGATIVE).astype(jnp.bfloat16)
        values = jnp.concatenate([block[:, HD : 2 * HD] for block in blocks], axis=0)
        key_row = first_key + lax.broadcasted_iota(jnp.int32, (1, count), 1)

        def one_head(h, carry):
            scores = lax.dot_general(
                qa[h],
                kaug[0:count, :],
                (((1,), (1,)), ((), ())),
                preferred_element_type=jnp.float32,
            )
            if causal:
                scores = jnp.where(key_row <= token, scores, NEGATIVE)
            old = m_ref[h]
            new = jnp.maximum(old, jnp.max(scores, axis=1, keepdims=True))
            weights = jnp.exp2(scores * scale2 - new[:, 0:1] * scale2)
            factor = jnp.exp2((old - new) * scale2)
            m_ref[h] = new
            l_ref[h] = l_ref[h] * factor + jnp.sum(weights, axis=1, keepdims=True)
            update = jnp.dot(
                weights.astype(jnp.bfloat16), values, preferred_element_type=jnp.float32
            )
            acc_ref[h] = acc_ref[h] * factor + update
            return carry

        lax.fori_loop(0, heads, one_head, 0, unroll=2)

    def quad(rx, k):
        return [buf.at[rx, k, zz, cc] for zz in range(2) for cc in range(2)]

    arrived(0, buf.at[0, 0, z, 1 - c])
    fold([buf.at[0, 0, z, 0], buf.at[0, 0, z, 1]], quad_first + z * 2 * BLK, True)

    arrived(1, buf.at[0, 0, 1 - z, c])
    mine = lambda rx, k: buf.at[rx, k, :, c]
    send(2, buf.at[0, 0, 1 - z, c], buf.at[0, 0, 1 - z, c], core)
    send(3, mine(0, 0), mine(0, 1), me.at(dy=1))
    send(4, mine(0, 0), mine(0, 2), me.at(dy=2))
    arrived(2, buf.at[0, 0, 1 - z, 1 - c])
    fold([buf.at[0, 0, 1 - z, 0], buf.at[0, 0, 1 - z, 1]], quad_first + (1 - z) * 2 * BLK, True)

    order = (1, 3, 2)
    other = lambda rx, k: buf.at[rx, k, :, 1 - c]
    out_wrap = {rx: lax.div(x + rx, 4) for rx in order}
    in_wrap = {rx: jnp.where(x < rx, 1, 0) for rx in order}

    arrived(3, mine(0, 1))
    send(5, mine(0, 1), mine(0, 1), core)
    for rx in order:
        send(6 + rx, mine(0, 1), mine(rx, 1 - out_wrap[rx]), me.at(dx=rx))
    arrived(4, mine(0, 2))
    send(6, mine(0, 2), mine(0, 2), core)
    for rx in order:
        send(9 + rx, mine(0, 2 * out_wrap[rx]), mine(rx, out_wrap[rx]), me.at(dx=rx))
    arrived(5, other(0, 1))
    fold(quad(0, 1), quad_first - 16 * BLK, False)
    arrived(6, other(0, 2))
    fold(quad(0, 2), quad_first - 32 * BLK, False)

    stages = [(6 + rx, 12 + rx, rx, 1 - in_wrap[rx]) for rx in order]
    stages += [(9 + rx, 15 + rx, rx, in_wrap[rx]) for rx in order]

    def forward(stage):
        first, second, rx, k = stage
        arrived(first, mine(rx, k))
        send(second, mine(rx, k), mine(rx, k), core)

    forward(stages[0])
    for i, (first, second, rx, k) in enumerate(stages):
        if i + 1 < len(stages):
            forward(stages[i + 1])
        arrived(second, other(rx, k))
        fold(quad(rx, k), quad_first - (rx + 4 * k) * 4 * BLK, False)

    for h in range(heads):
        out_ref[:, h * HD : (h + 1) * HD] = (acc_ref[h] / l_ref[h]).astype(out_ref.dtype)
    for copy in started:
        copy.wait_send()


def attend(kv_block, queries, query_onehot, bounds):
    heads = queries.shape[1] // HD
    vmem = pl.BlockSpec(memory_space=pltpu.VMEM)
    return pl.pallas_call(
        attend_kernel,
        out_shape=jax.ShapeDtypeStruct(queries.shape, jnp.bfloat16),
        in_specs=[vmem] * 4,
        out_specs=vmem,
        scratch_shapes=[
            pltpu.VMEM((4, 3, 2, 2, BLK, 2 * HD), jnp.bfloat16),
            pltpu.VMEM((heads, BLK, 2 * HD), jnp.bfloat16),
            pltpu.VMEM((4 * BLK, 2 * HD), jnp.bfloat16),
            pltpu.VMEM((heads, BLK, HD), jnp.float32),
            pltpu.VMEM((heads, BLK, HD), jnp.float32),
            pltpu.VMEM((heads, BLK, HD), jnp.float32),
            pltpu.SemaphoreType.DMA((19,)),
            pltpu.SemaphoreType.DMA((19,)),
        ],
        compiler_params=pltpu.CompilerParams(
            collective_id=0, has_side_effects=True, vmem_limit_bytes=48 << 20
        ),
        cost_estimate=pl.CostEstimate(
            flops=9_000_000_000, bytes_accessed=2_000_000, transcendentals=17_000_000
        ),
    )(kv_block, queries, query_onehot, bounds)


def on_device(hidden, norm_gain, kv_weight, queries, segment_ids, page_owner):
    seq_count = lax.axis_size("seq")
    seq_place = lax.axis_index("seq")
    block_rows = segment_ids.shape[0]
    stream_rows = block_rows * seq_count
    anchor = seq_place * block_rows
    token_index = anchor + jnp.arange(block_rows, dtype=jnp.int32)
    labels = jnp.arange(SEGS, dtype=jnp.int32)
    member = segment_ids[:, None] == labels[None, :]
    firsts = jnp.min(jnp.where(member, token_index[:, None], stream_rows), axis=0)
    first_tile = jnp.broadcast_to(jnp.pad(firsts, (0, HD - SEGS))[None, :], (8, HD))
    projected, start_tile = project(hidden, norm_gain[None, :], kv_weight, first_tile)
    starts = start_tile[0, :SEGS]
    query_start = jnp.sum(jnp.where(member, starts[None, :], 0), axis=1)
    positions = token_index - query_start
    kv_block = pair_keys(projected, positions, HD)

    lanes = jnp.arange(HD, dtype=jnp.int32)
    query_onehot = (segment_ids[:, None] == lanes[None, :]).astype(jnp.bfloat16)
    low = jnp.full((HD,), stream_rows, jnp.int32).at[:SEGS].set(starts)
    high = jnp.full((HD,), stream_rows, jnp.int32).at[: SEGS - 1].set(starts[1:])
    bounds = jnp.zeros((8, HD), jnp.int32).at[0].set(low).at[1].set(high)
    attended = attend(kv_block, queries, query_onehot, bounds)

    pages_block = page_owner.shape[0]
    page_rows = block_rows // pages_block
    capacity = max(2, 2 * pages_block // seq_count)
    owners = page_owner[:, 0]
    order = jnp.arange(pages_block, dtype=jnp.int32)
    earlier = (owners[None, :] == owners[:, None]) & (order[None, :] < order[:, None])
    rank = jnp.sum(earlier.astype(jnp.int32), axis=1)
    target = owners * capacity + rank
    select = (jnp.arange(seq_count * capacity, dtype=jnp.int32)[:, None] == target[None, :]).astype(
        jnp.bfloat16
    )
    columns_dev = kv_block.shape[1]
    pages = kv_block.reshape(pages_block, page_rows * columns_dev)
    outgoing = jnp.dot(select, pages, preferred_element_type=jnp.float32).astype(jnp.bfloat16)
    outgoing = outgoing.reshape(seq_count, capacity, page_rows, columns_dev)
    arrived = lax.all_to_all(outgoing, "seq", split_axis=0, concat_axis=0, tiled=True)
    kv_cache = arrived.reshape(1, seq_count, capacity, page_rows, columns_dev)
    return (attended, kv_cache)


def solution(mesh):
    placed = (P(("seq", "fs"), None), P(), P("seq", "fs"), P("seq", "fs"), P("seq"), P("seq", None))
    return jax.shard_map(
        on_device,
        mesh=mesh,
        in_specs=placed,
        out_specs=(P("seq", "fs"), P("seq", None, None, None, "fs")),
        check_vma=False,
    )
```

```python
import functools

import jax
import jax.numpy as jnp
from jax import lax
from jax.experimental import pallas as pl
from jax.experimental.pallas import tpu as pltpu
from jax.sharding import PartitionSpec as P

HD = 128
SEGS = 4
EPSILON = 1e-05
NEGATIVE = -1e30
LOG2E = 1.4426950408889634
MESH = pl.DeviceIdType.MESH
BLK = 256


def rotate_keys(keys, positions):
    half = keys.shape[-1] // 2
    freq = 10000.0 ** (-jnp.arange(half, dtype=jnp.float32) * 2.0 / keys.shape[-1])
    angle = positions.astype(jnp.float32)[:, None] * freq[None, :]
    cosine = jnp.cos(angle)[:, None, :]
    sine = jnp.sin(angle)[:, None, :]
    first = keys[..., :half]
    second = keys[..., half:]
    return jnp.concatenate(
        [first * cosine - second * sine, second * cosine + first * sine], axis=-1
    )


def pair_keys(projected, positions, head_size):
    rows = projected.shape[0]
    pairs = projected.reshape(rows, -1, 2, head_size)
    turned = rotate_keys(pairs[:, :, 0], positions)
    return jnp.stack([turned, pairs[:, :, 1]], axis=2).reshape(rows, -1).astype(jnp.bfloat16)


def wrap(value, count):
    return value - count * (value >= count).astype(jnp.int32)


class Place:
    def __init__(self):
        s = lax.axis_index("seq")
        self.s = s
        self.f = lax.axis_index("fs")
        self.c = lax.rem(s, 2)
        self.z = lax.rem(lax.div(s, 2), 2)
        self.x = lax.rem(lax.div(s, 4), 4)
        self.y = lax.div(s, 16)

    def at(self, dy=0, dx=0, other_z=False, other_core=False):
        y = wrap(self.y + dy, 4)
        x = wrap(self.x + dx, 4)
        z = 1 - self.z if other_z else self.z
        c = 1 - self.c if other_core else self.c
        return (((y * 4 + x) * 2 + z) * 2 + c, self.f)


def remote(src, dst, send, recv, target):
    return pltpu.make_async_remote_copy(
        src_ref=src, dst_ref=dst, send_sem=send, recv_sem=recv, device_id=target, device_id_type=MESH
    )


def project_kernel(
    hid_ref, gain_ref, w_ref, first_ref, out_ref, starts_ref, nb, wb, fb, acc, res, got, ss, rs
):
    me = Place()
    c, z, x, y, f = me.c, me.z, me.x, me.y, me.f
    parity, group = lax.rem(f, 2), lax.div(f, 2)
    head = parity + 2 * c
    twin = lax.rem(f + 2, 4)
    mate = f + 1 - 2 * parity
    home = c == group
    chunks, rows, cols = nb.shape[2], nb.shape[3], nb.shape[4]

    def near(zz, cc, ff):
        return (((y * 4 + x) * 2 + zz) * 2 + cc, ff)

    core = near(z, 1 - c, f)
    ring_x = {k: me.at(dx=k) for k in (1, 2, 3)}
    ring_y = {k: me.at(dy=k) for k in (1, 2, 3)}
    cube = [near(zz, cc, ff) for ff in (f, twin) for zz in (z, 1 - z) for cc in (c, 1 - c)][1:]
    partners = cube + [near(z, c, mate)] + list(ring_x.values()) + list(ring_y.values())
    barrier = pltpu.get_barrier_semaphore()
    for partner in partners:
        pl.semaphore_signal(barrier, inc=1, device_id=partner, device_id_type=MESH)
    pl.semaphore_wait(barrier, len(partners))

    started = []

    def send(index, src, dst, target, recv=None):
        recv = index if recv is None else recv
        copy = remote(src, dst, ss.at[index], rs.at[recv], target)
        copy.start()
        started.append(copy)

    def arrived(index, dst):
        remote(dst, dst, ss.at[index], rs.at[index], core).wait_recv()

    quad = y * 4 + x
    shard = 2 * z + c
    rows_w = w_ref.shape[0]

    def piece(zz, cc):
        return wb.at[quad, zz, pl.ds(pl.multiple_of(cc * rows_w, rows_w), rows_w)]

    def seed_to_core():
        return remote(w_ref, piece(z, c), ss.at[0], rs.at[shard], core)

    @pl.when(home)
    def _():
        wb[quad, z, pl.ds(pl.multiple_of(c * rows_w, rows_w), rows_w)] = w_ref[...]

    @pl.when(jnp.logical_not(home))
    def _():
        seed_to_core().start()

    send(1, w_ref, piece(z, c), near(z, group, twin), shard)
    send(2, w_ref, piece(z, c), near(1 - z, group, f), shard)
    send(3, w_ref, piece(z, c), near(1 - z, group, twin), shard)
    send(4, first_ref, fb.at[0], core)
    send(5, first_ref, fb.at[1], near(1 - z, c, f))
    send(6, first_ref, fb.at[2], near(1 - z, 1 - c, f))

    total = jnp.zeros((rows, 1), jnp.float32)
    for i in range(chunks):
        wide = hid_ref[:, i * cols : (i + 1) * cols].astype(jnp.float32)
        total = total + jnp.sum(wide * wide, axis=1, keepdims=True)
    factor = lax.rsqrt(total / (chunks * cols) + EPSILON)
    for i in range(chunks):
        wide = hid_ref[:, i * cols : (i + 1) * cols].astype(jnp.float32)
        gain = gain_ref[:, i * cols : (i + 1) * cols].astype(jnp.float32)
        nb[c, parity, i] = (wide * factor * gain).astype(jnp.bfloat16)
        send(13 + i, nb.at[c, parity, i], nb.at[c, parity, i], near(z, c, mate))
        send(17 + i, nb.at[c, parity, i], nb.at[c, parity, i], core)

    def seed_arrived(zz):
        for cc in (0, 1):
            own = jnp.logical_and(home, shard == 2 * zz + cc)

            @pl.when(jnp.logical_not(own))
            def _():
                arrived(2 * zz + cc, piece(zz, cc))

    half = lambda yy, xx, hh: wb.at[yy * 4 + xx, hh]
    back = lambda v, k: lax.rem(v + 4 - k, 4)
    order = (1, 3, 2)
    seed_arrived(0)
    for k in order:
        send(24 + k, half(y, x, 0), half(y, x, 0), ring_x[k])
    seed_arrived(1)
    for k in order:
        send(27 + k, half(y, x, 1), half(y, x, 1), ring_y[k])

    a2 = lambda k, j: 31 + (k - 1) * 4 + j
    b2 = lambda k, j: 43 + (k - 1) * 4 + j

    def spread(j):
        ya, xa = y, back(x, j)
        yb, xb = back(y, j), x
        if j:
            arrived(24 + j, half(ya, xa, 0))
        for k in order:
            send(a2(k, j), half(ya, xa, 0), half(ya, xa, 0), ring_y[k])
        if j:
            arrived(27 + j, half(yb, xb, 1))
        for k in order:
            send(b2(k, j), half(yb, xb, 1), half(yb, xb, 1), ring_x[k])

    def forward(i):
        arrived(13 + i, nb.at[c, 1 - parity, i])
        send(21 + i, nb.at[c, 1 - parity, i], nb.at[c, 1 - parity, i], core)

    spread(0)
    for i in range(3):
        arrived(4 + i, fb.at[i])
    fb[3] = jnp.minimum(jnp.minimum(first_ref[...], fb[0]), jnp.minimum(fb[1], fb[2]))
    for k in order:
        send(6 + k, fb.at[3], fb.at[3 + k], ring_x[k])
    forward(0)
    spread(1)
    spread(3)
    forward(1)
    spread(2)
    for k in order:
        arrived(6 + k, fb.at[3 + k])
    fb[7] = jnp.minimum(jnp.minimum(fb[3], fb[4]), jnp.minimum(fb[5], fb[6]))
    for k in order:
        send(9 + k, fb.at[7], fb.at[7 + k], ring_y[k])
    forward(2)
    forward(3)
    for k in order:
        arrived(9 + k, fb.at[7 + k])
    starts_ref[...] = jnp.minimum(jnp.minimum(fb[7], fb[8]), jnp.minimum(fb[9], fb[10]))
    for i in range(chunks):
        arrived(17 + i, nb.at[1 - c, parity, i])
        arrived(21 + i, nb.at[1 - c, 1 - parity, i])

    acc[...] = jnp.zeros_like(acc)

    def multiply(yy, xx, hh):
        columns = pl.ds(pl.multiple_of(xx * 512 + hh * 256, 256), 256)
        lhs = nb[:, :, yy, :, columns].reshape(4 * rows, 256)
        acc[...] += jnp.dot(lhs, wb[yy * 4 + xx, hh], preferred_element_type=jnp.float32)

    multiply(y, x, 0)
    multiply(y, x, 1)
    for j in order:
        multiply(y, back(x, j), 0)
        multiply(back(y, j), x, 1)
    for j in (0, 1, 3, 2):
        for k in order:
            yy, xx = back(y, k), back(x, j)
            arrived(a2(k, j), half(yy, xx, 0))
            multiply(yy, xx, 0)
            yy, xx = back(y, j), back(x, k)
            arrived(b2(k, j), half(yy, xx, 1))
            multiply(yy, xx, 1)

    res[...] = acc[...].reshape(res.shape)

    def result_to(cc, ff, index):
        return remote(res.at[cc], got.at[group], ss.at[index], rs.at[55 + group], near(z, cc, ff))

    @pl.when(home)
    def _():
        result_to(1 - c, f, 55).start()
        got[group] = res[c]

    @pl.when(jnp.logical_not(home))
    def _():
        result_to(0, twin, 55).start()
        result_to(1, twin, 56).start()

    for g in (0, 1):

        @pl.when(jnp.logical_not(jnp.logical_and(home, group == g)))
        def _():
            arrived(55 + g, got.at[g])

    out_ref[...] = got[...].reshape(out_ref.shape)
    for copy in started:
        copy.wait_send()

    @pl.when(home)
    def _():
        result_to(1 - c, f, 55).wait_send()

    @pl.when(jnp.logical_not(home))
    def _():
        seed_to_core().wait_send()
        result_to(0, twin, 55).wait_send()
        result_to(1, twin, 56).wait_send()


def project(hidden, gain, weight, firsts):
    rows, width = hidden.shape
    columns = weight.shape[1]
    vmem = pl.BlockSpec(memory_space=pltpu.VMEM)
    return pl.pallas_call(
        project_kernel,
        out_shape=(
            jax.ShapeDtypeStruct((4 * rows, columns), jnp.float32),
            jax.ShapeDtypeStruct((8, HD), jnp.int32),
        ),
        in_specs=[vmem] * 4,
        out_specs=(vmem, vmem),
        scratch_shapes=[
            pltpu.VMEM((2, 2, 4, rows, width // 4), jnp.bfloat16),
            pltpu.VMEM((16, 2, width // 32, columns), jnp.bfloat16),
            pltpu.VMEM((11, 8, HD), jnp.int32),
            pltpu.VMEM((4 * rows, columns), jnp.float32),
            pltpu.VMEM((2, 2 * rows, columns), jnp.float32),
            pltpu.VMEM((2, 2 * rows, columns), jnp.float32),
            pltpu.SemaphoreType.DMA((57,)),
            pltpu.SemaphoreType.DMA((57,)),
        ],
        compiler_params=pltpu.CompilerParams(
            collective_id=1, has_side_effects=True, vmem_limit_bytes=48 << 20
        ),
        cost_estimate=pl.CostEstimate(
            flops=1_100_000_000, bytes_accessed=2_000_000, transcendentals=0
        ),
    )(hidden, gain, weight, firsts)


def attend_kernel(
    kv_ref, q_ref, qseg_ref, bounds_ref, pages_ref, out_ref, cache_ref,
    buf, pages, qa, m_ref, l_ref, acc_ref, ss, rs
):
    me = Place()
    c, z, x = me.c, me.z, me.x
    heads = q_ref.shape[1] // HD
    owners = pages_ref.shape[0]
    scale2 = (HD ** (-0.5)) * LOG2E
    core = me.at(other_core=True)
    opposite = me.at(other_z=True)

    def peer(distance):
        return (wrap(me.s + distance, owners), me.f)

    barrier = pltpu.get_barrier_semaphore()

    def greet(distance, carry):
        pl.semaphore_signal(barrier, inc=1, device_id=peer(distance), device_id_type=MESH)
        return carry

    lax.fori_loop(1, owners, greet, 0)
    buf[0, 0, z, c] = kv_ref[...]
    pages[me.s] = pages_ref[me.s]
    pl.semaphore_wait(barrier, owners - 1)

    def send(index, src, dst, target):
        remote(src, dst, ss.at[index], rs.at[index], target).start()

    def arrived(index, dst):
        remote(dst, dst, ss.at[index], rs.at[index], core).wait_recv()

    def block(rx, k, zi, cc):
        return buf.at[rx, k, wrap(z + zi, 2), cc]

    def mine(rx, k, zi):
        return block(rx, k, zi, c)

    order = (1, 3, 2)
    out_wrap = {rx: (x + rx >= 4).astype(jnp.int32) for rx in order}
    in_wrap = {rx: (x < rx).astype(jnp.int32) for rx in order}
    x1 = lambda rx, zi: 11 + 2 * (rx - 1) + zi
    x2 = lambda rx, zi: 17 + 2 * (rx - 1) + zi

    def second(rx, zi):
        w = out_wrap[rx]
        return remote(
            mine(0, 2 * w, zi), mine(rx, w, zi), ss.at[x2(rx, zi)], rs.at[x2(rx, zi)], me.at(dx=rx)
        )

    def send_second(zi, wraps):
        for rx in order:

            @pl.when(out_wrap[rx] == wraps)
            def _():
                second(rx, zi).start()

    def send_y(zi):
        send(3 + zi, mine(0, 0, zi), mine(0, 1, zi), me.at(dy=1))
        send(5 + zi, mine(0, 0, zi), mine(0, 2, zi), me.at(dy=2))
        send_second(zi, 0)

    def send_first(zi):
        for rx in order:
            send(x1(rx, zi), mine(0, 1, zi), mine(rx, 1 - out_wrap[rx], zi), me.at(dx=rx))

    def forward(first, then, rx, k, zi):
        arrived(first, mine(rx, k, zi))
        send(then, mine(rx, k, zi), mine(rx, k, zi), core)

    units = [
        (0, 0, 0, None, 0),
        (0, 1, 0, 3, 7),
        (0, 2, 0, 5, 9),
        (0, 0, 1, 1, 2),
        (0, 1, 1, 4, 8),
        (0, 2, 1, 6, 10),
    ]
    for zi in (0, 1):
        units += [(rx, 1 - in_wrap[rx], zi, x1(rx, zi), x1(rx, zi) + 12) for rx in order]
        units += [(rx, in_wrap[rx], zi, x2(rx, zi), x2(rx, zi) + 12) for rx in order]
    turn = [0, 1, 2, 3, 6, 7, 8, 4, 5, 9, 10, 11, 12, 13, 14, 15, 16, 17]
    units = [units[i] for i in turn]

    send(0, kv_ref, block(0, 0, 0, c), core)
    send(1, kv_ref, block(0, 0, 0, c), opposite)
    send_y(0)

    for h in range(heads):
        qa[h * BLK : (h + 1) * BLK, 0:HD] = q_ref[:, h * HD : (h + 1) * HD]
        qa[h * BLK : (h + 1) * BLK, HD : 2 * HD] = qseg_ref[...]
    m_ref[...] = jnp.full_like(m_ref, NEGATIVE)
    l_ref[...] = jnp.zeros_like(l_ref)
    acc_ref[...] = jnp.zeros_like(acc_ref)
    low = bounds_ref[0:1, :]
    high = bounds_ref[1:2, :]
    quad_first = (me.y * 4 + x) * 4 * BLK
    place = 2 * z + c

    def step(source, first_key, causal):
        key = first_key + lax.broadcasted_iota(jnp.int32, (BLK, HD), 0)
        inside = (key >= low) & (key < high)
        bias = jnp.where(inside, 0.0, NEGATIVE).astype(jnp.bfloat16)
        keys = jnp.concatenate([source[:, 0:HD], bias], axis=1)
        scores = lax.dot_general(
            qa[...], keys, (((1,), (1,)), ((), ())), preferred_element_type=jnp.float32
        )
        if causal:
            row = lax.broadcasted_iota(jnp.int32, scores.shape, 0) & (BLK - 1)
            column = lax.broadcasted_iota(jnp.int32, scores.shape, 1)
            scores = jnp.where(column <= row, scores, NEGATIVE)
        old = m_ref[...]
        new = jnp.maximum(old, jnp.max(scores, axis=1, keepdims=True))
        offset = new * scale2
        weights = jnp.exp2(scores * scale2 - jnp.concatenate([offset, offset], axis=1))
        factor = jnp.exp2((old - new) * scale2)
        m_ref[...] = new
        l_ref[...] = l_ref[...] * factor + (weights[:, 0:HD] + weights[:, HD : 2 * HD])
        update = jnp.dot(
            weights.astype(jnp.bfloat16), source[:, HD : 2 * HD], preferred_element_type=jnp.float32
        )
        acc_ref[...] = acc_ref[...] * factor + update

    step(block(0, 0, 0, c), quad_first + place * BLK, True)

    def chosen(n, field):
        value = 0
        for i, unit in enumerate(units):
            value = value + (n == i).astype(jnp.int32) * unit[field]
        return value

    def serve(i):
        rx, k, zi, first, then = units[i]
        forward(first, then, rx, k, zi)
        if (rx, k) == (0, 1):
            send_first(zi)
        if (rx, k) == (0, 2):
            send_second(zi, 1)
        if (rx, k) == (0, 0):
            send_y(1)

    def one_unit(n, carry):
        for i in range(1, len(units)):

            @pl.when(n == i - 1)
            def _():
                serve(i)

        rx, k, zi, then = (chosen(n, field) for field in (0, 1, 2, 4))

        @pl.when(n < 8)
        def _():
            for i in range(8):

                @pl.when(n * 8 + i > 0)
                def _():
                    to = peer(n * 8 + i)
                    remote(pages_ref.at[to[0]], pages.at[me.s], ss.at[35], rs.at[35], to).start()

        def one_core(j, inner):
            cc = wrap(c + j, 2)
            source = block(rx, k, zi, cc)
            where = 2 * wrap(z + zi, 2) + cc

            @pl.when(j == 1)
            def _():
                arrived(then, source)

            distance = rx + 4 * k
            first_key = quad_first - distance * 4 * BLK + where * BLK
            skip = ((distance == 0) & (where >= place)) | ((distance == 8) & (where < place))

            @pl.when(jnp.logical_not(skip) & (first_key >= 0))
            def _():
                step(source, first_key, False)

            return inner

        return lax.fori_loop(0, 2, one_core, carry)

    lax.fori_loop(0, len(units), one_unit, 0)

    for h in range(heads):
        rows = slice(h * BLK, (h + 1) * BLK)
        total = jnp.sum(l_ref[rows, :], axis=1, keepdims=True)
        out_ref[:, h * HD : (h + 1) * HD] = (acc_ref[rows, :] / total).astype(out_ref.dtype)

    others = pl.ds(0, owners - 1)
    exchange = remote(pages_ref.at[others], pages.at[others], ss.at[35], rs.at[35], core)
    exchange.wait_recv()
    cache_ref[...] = pages[...]
    exchange.wait_send()
    for index in range(35):
        remote(kv_ref, block(0, 0, 0, c), ss.at[index], rs.at[index], core).wait_send()


def attend(kv_block, queries, query_onehot, bounds, outgoing):
    heads = queries.shape[1] // HD
    vmem = pl.BlockSpec(memory_space=pltpu.VMEM)
    return pl.pallas_call(
        attend_kernel,
        out_shape=(
            jax.ShapeDtypeStruct(queries.shape, jnp.bfloat16),
            jax.ShapeDtypeStruct(outgoing.shape, jnp.bfloat16),
        ),
        in_specs=[vmem] * 5,
        out_specs=(vmem, vmem),
        scratch_shapes=[
            pltpu.VMEM((4, 3, 2, 2, BLK, 2 * HD), jnp.bfloat16),
            pltpu.VMEM(outgoing.shape, jnp.bfloat16),
            pltpu.VMEM((heads * BLK, 2 * HD), jnp.bfloat16),
            pltpu.VMEM((heads * BLK, HD), jnp.float32),
            pltpu.VMEM((heads * BLK, HD), jnp.float32),
            pltpu.VMEM((heads * BLK, HD), jnp.float32),
            pltpu.SemaphoreType.DMA((36,)),
            pltpu.SemaphoreType.DMA((36,)),
        ],
        compiler_params=pltpu.CompilerParams(
            collective_id=0, has_side_effects=True, vmem_limit_bytes=48 << 20
        ),
        cost_estimate=pl.CostEstimate(
            flops=9_000_000_000, bytes_accessed=2_000_000, transcendentals=17_000_000
        ),
    )(kv_block, queries, query_onehot, bounds, outgoing)


def on_device(hidden, norm_gain, kv_weight, queries, segment_ids, page_owner):
    seq_count = lax.axis_size("seq")
    seq_place = lax.axis_index("seq")
    block_rows = segment_ids.shape[0]
    stream_rows = block_rows * seq_count
    anchor = seq_place * block_rows
    token_index = anchor + jnp.arange(block_rows, dtype=jnp.int32)
    labels = jnp.arange(SEGS, dtype=jnp.int32)
    member = segment_ids[:, None] == labels[None, :]
    firsts = jnp.min(jnp.where(member, token_index[:, None], stream_rows), axis=0)
    first_tile = jnp.broadcast_to(jnp.pad(firsts, (0, HD - SEGS))[None, :], (8, HD))
    projected, start_tile = project(hidden, norm_gain[None, :], kv_weight, first_tile)
    starts = start_tile[0, :SEGS]
    query_start = jnp.sum(jnp.where(member, starts[None, :], 0), axis=1)
    positions = token_index - query_start
    kv_block = pair_keys(projected, positions, HD)

    lanes = jnp.arange(HD, dtype=jnp.int32)
    query_onehot = (segment_ids[:, None] == lanes[None, :]).astype(jnp.bfloat16)
    low = jnp.full((HD,), stream_rows, jnp.int32).at[:SEGS].set(starts)
    high = jnp.full((HD,), stream_rows, jnp.int32).at[: SEGS - 1].set(starts[1:])
    bounds = jnp.zeros((8, HD), jnp.int32).at[0].set(low).at[1].set(high)

    pages_block = page_owner.shape[0]
    page_rows = block_rows // pages_block
    capacity = max(2, 2 * pages_block // seq_count)
    owners = page_owner[:, 0]
    order = jnp.arange(pages_block, dtype=jnp.int32)
    earlier = (owners[None, :] == owners[:, None]) & (order[None, :] < order[:, None])
    rank = jnp.sum(earlier.astype(jnp.int32), axis=1)
    target = owners * capacity + rank
    select = (jnp.arange(seq_count * capacity, dtype=jnp.int32)[:, None] == target[None, :]).astype(
        jnp.bfloat16
    )
    columns_dev = kv_block.shape[1]
    pages = kv_block.reshape(pages_block, page_rows * columns_dev)
    outgoing = jnp.dot(select, pages, preferred_element_type=jnp.float32).astype(jnp.bfloat16)
    outgoing = outgoing.reshape(seq_count, capacity * page_rows * columns_dev // HD, HD)
    attended, arrived = attend(kv_block, queries, query_onehot, bounds, outgoing)
    kv_cache = arrived.reshape(1, seq_count, capacity, page_rows, columns_dev)
    return (attended, kv_cache)


def solution(mesh):
    placed = (P(("seq", "fs"), None), P(), P("seq", "fs"), P("seq", "fs"), P("seq"), P("seq", None))
    return jax.shard_map(
        on_device,
        mesh=mesh,
        in_specs=placed,
        out_specs=(P("seq", "fs"), P("seq", None, None, None, "fs")),
        check_vma=False,
    )
```

```python
import functools

import jax
import jax.numpy as jnp
from jax import lax
from jax.experimental import pallas as pl
from jax.experimental.pallas import tpu as pltpu
from jax.sharding import PartitionSpec as P

HD = 128
SEGS = 4
EPSILON = 1e-05
NEGATIVE = -1e30
LOG2E = 1.4426950408889634
MESH = pl.DeviceIdType.MESH
BLK = 256


def wrap(value, count):
    return value - count * (value >= count).astype(jnp.int32)


class Place:
    def __init__(self):
        s = lax.axis_index("seq")
        self.s = s
        self.f = lax.axis_index("fs")
        self.c = lax.rem(s, 2)
        self.z = lax.rem(lax.div(s, 2), 2)
        self.x = lax.rem(lax.div(s, 4), 4)
        self.y = lax.div(s, 16)

    def at(self, dy=0, dx=0, other_z=False, other_core=False):
        y = wrap(self.y + dy, 4)
        x = wrap(self.x + dx, 4)
        z = 1 - self.z if other_z else self.z
        c = 1 - self.c if other_core else self.c
        return (((y * 4 + x) * 2 + z) * 2 + c, self.f)


def remote(src, dst, send, recv, target):
    return pltpu.make_async_remote_copy(
        src_ref=src, dst_ref=dst, send_sem=send, recv_sem=recv, device_id=target, device_id_type=MESH
    )


def project_part(me, hid_ref, gain_ref, w_ref, first_ref, nb, wb, fb, acc, res, got, ss, rs, enter):
    c, z, x, y, f = me.c, me.z, me.x, me.y, me.f
    parity, group = lax.rem(f, 2), lax.div(f, 2)
    head = parity + 2 * c
    twin = lax.rem(f + 2, 4)
    mate = f + 1 - 2 * parity
    home = c == group
    chunks, rows, cols = nb.shape[2], nb.shape[3], nb.shape[4]

    def near(zz, cc, ff):
        return (((y * 4 + x) * 2 + zz) * 2 + cc, ff)

    core = near(z, 1 - c, f)
    ring_x = {k: me.at(dx=k) for k in (1, 2, 3)}
    ring_y = {k: me.at(dy=k) for k in (1, 2, 3)}
    enter([near(zz, cc, twin) for zz in (z, 1 - z) for cc in (c, 1 - c)] + [near(z, c, mate)])

    started = []

    def send(index, src, dst, target, recv=None):
        recv = index if recv is None else recv
        copy = remote(src, dst, ss.at[index], rs.at[recv], target)
        copy.start()
        started.append(copy)

    def arrived(index, dst):
        remote(dst, dst, ss.at[index], rs.at[index], core).wait_recv()

    quad = y * 4 + x
    shard = 2 * z + c
    rows_w = w_ref.shape[0]

    def piece(zz, cc):
        return wb.at[quad, zz, pl.ds(pl.multiple_of(cc * rows_w, rows_w), rows_w)]

    def seed_to_core():
        return remote(w_ref, piece(z, c), ss.at[0], rs.at[shard], core)

    @pl.when(home)
    def _():
        wb[quad, z, pl.ds(pl.multiple_of(c * rows_w, rows_w), rows_w)] = w_ref[...]

    @pl.when(jnp.logical_not(home))
    def _():
        seed_to_core().start()

    send(1, w_ref, piece(z, c), near(z, group, twin), shard)
    send(2, w_ref, piece(z, c), near(1 - z, group, f), shard)
    send(3, w_ref, piece(z, c), near(1 - z, group, twin), shard)
    send(4, first_ref, fb.at[0], core)
    send(5, first_ref, fb.at[1], near(1 - z, c, f))
    send(6, first_ref, fb.at[2], near(1 - z, 1 - c, f))

    total = jnp.zeros((rows, 1), jnp.float32)
    for i in range(chunks):
        wide = hid_ref[:, i * cols : (i + 1) * cols].astype(jnp.float32)
        total = total + jnp.sum(wide * wide, axis=1, keepdims=True)
    factor = lax.rsqrt(total / (chunks * cols) + EPSILON)
    for i in range(chunks):
        wide = hid_ref[:, i * cols : (i + 1) * cols].astype(jnp.float32)
        gain = gain_ref[:, i * cols : (i + 1) * cols].astype(jnp.float32)
        nb[c, parity, i] = (wide * factor * gain).astype(jnp.bfloat16)
        send(13 + i, nb.at[c, parity, i], nb.at[c, parity, i], near(z, c, mate))
        send(17 + i, nb.at[c, parity, i], nb.at[c, parity, i], core)

    def seed_arrived(zz):
        for cc in (0, 1):
            own = jnp.logical_and(home, shard == 2 * zz + cc)

            @pl.when(jnp.logical_not(own))
            def _():
                arrived(2 * zz + cc, piece(zz, cc))

    half = lambda yy, xx, hh: wb.at[yy * 4 + xx, hh]
    back = lambda v, k: lax.rem(v + 4 - k, 4)
    order = (1, 3, 2)
    seed_arrived(0)
    for k in order:
        send(24 + k, half(y, x, 0), half(y, x, 0), ring_x[k])
    seed_arrived(1)
    for k in order:
        send(27 + k, half(y, x, 1), half(y, x, 1), ring_y[k])

    a2 = lambda k, j: 31 + (k - 1) * 4 + j
    b2 = lambda k, j: 43 + (k - 1) * 4 + j

    def spread(j):
        ya, xa = y, back(x, j)
        yb, xb = back(y, j), x
        if j:
            arrived(24 + j, half(ya, xa, 0))
        for k in order:
            send(a2(k, j), half(ya, xa, 0), half(ya, xa, 0), ring_y[k])
        if j:
            arrived(27 + j, half(yb, xb, 1))
        for k in order:
            send(b2(k, j), half(yb, xb, 1), half(yb, xb, 1), ring_x[k])

    def forward(i):
        arrived(13 + i, nb.at[c, 1 - parity, i])
        send(21 + i, nb.at[c, 1 - parity, i], nb.at[c, 1 - parity, i], core)

    spread(0)
    for i in range(3):
        arrived(4 + i, fb.at[i])
    fb[3] = jnp.minimum(jnp.minimum(first_ref[...], fb[0]), jnp.minimum(fb[1], fb[2]))
    for k in order:
        send(6 + k, fb.at[3], fb.at[3 + k], ring_x[k])
    forward(0)
    spread(1)
    spread(3)
    forward(1)
    spread(2)
    for k in order:
        arrived(6 + k, fb.at[3 + k])
    fb[7] = jnp.minimum(jnp.minimum(fb[3], fb[4]), jnp.minimum(fb[5], fb[6]))
    for k in order:
        send(9 + k, fb.at[7], fb.at[7 + k], ring_y[k])
    forward(2)
    forward(3)
    for k in order:
        arrived(9 + k, fb.at[7 + k])
    fb[11] = jnp.minimum(jnp.minimum(fb[7], fb[8]), jnp.minimum(fb[9], fb[10]))
    for i in range(chunks):
        arrived(17 + i, nb.at[1 - c, parity, i])
        arrived(21 + i, nb.at[1 - c, 1 - parity, i])

    acc[...] = jnp.zeros_like(acc)

    def multiply(yy, xx, hh):
        columns = pl.ds(pl.multiple_of(xx * 512 + hh * 256, 256), 256)
        lhs = nb[:, :, yy, :, columns].reshape(4 * rows, 256)
        acc[...] += jnp.dot(lhs, wb[yy * 4 + xx, hh], preferred_element_type=jnp.float32)

    multiply(y, x, 0)
    multiply(y, x, 1)
    for j in order:
        multiply(y, back(x, j), 0)
        multiply(back(y, j), x, 1)
    for j in (0, 1, 3, 2):
        for k in order:
            yy, xx = back(y, k), back(x, j)
            arrived(a2(k, j), half(yy, xx, 0))
            multiply(yy, xx, 0)
            yy, xx = back(y, j), back(x, k)
            arrived(b2(k, j), half(yy, xx, 1))
            multiply(yy, xx, 1)

    res[...] = acc[...].reshape(res.shape)

    def result_to(cc, ff, index):
        return remote(res.at[cc], got.at[group], ss.at[index], rs.at[55 + group], near(z, cc, ff))

    @pl.when(home)
    def _():
        result_to(1 - c, f, 55).start()
        got[group] = res[c]

    @pl.when(jnp.logical_not(home))
    def _():
        result_to(0, twin, 55).start()
        result_to(1, twin, 56).start()

    for g in (0, 1):

        @pl.when(jnp.logical_not(jnp.logical_and(home, group == g)))
        def _():
            arrived(55 + g, got.at[g])


    def finish():
        for copy in started:
            copy.wait_send()

        @pl.when(home)
        def _():
            result_to(1 - c, f, 55).wait_send()

        @pl.when(jnp.logical_not(home))
        def _():
            seed_to_core().wait_send()
            result_to(0, twin, 55).wait_send()
            result_to(1, twin, 56).wait_send()

    return finish


def layer_kernel(
    hid_ref, gain_ref, w_ref, first_ref, q_ref, qseg_ref, freq_ref, target_ref,
    out_ref, cache_ref,
    nb, wb, fb, proj, res, got, ass, ars,
    buf, pages, pages_ref, qa, m_ref, l_ref, acc_ref, ss, rs
):
    me = Place()
    c, z, x = me.c, me.z, me.x
    heads = q_ref.shape[1] // HD
    owners = pages_ref.shape[0]
    scale2 = (HD ** (-0.5)) * LOG2E
    core = me.at(other_core=True)
    opposite = me.at(other_z=True)

    def peer(distance):
        return (wrap(me.s + distance, owners), me.f)

    def enter(others):
        barrier = pltpu.get_barrier_semaphore()

        def greet(distance, carry):
            pl.semaphore_signal(barrier, inc=1, device_id=peer(distance), device_id_type=MESH)
            return carry

        for other in others:
            pl.semaphore_signal(barrier, inc=1, device_id=other, device_id_type=MESH)
        lax.fori_loop(1, owners, greet, 0)
        for h in range(heads):
            qa[h * BLK : (h + 1) * BLK, 0:HD] = q_ref[:, h * HD : (h + 1) * HD]
            qa[h * BLK : (h + 1) * BLK, HD : 2 * HD] = qseg_ref[...]
        m_ref[...] = jnp.full_like(m_ref, NEGATIVE)
        l_ref[...] = jnp.zeros_like(l_ref)
        acc_ref[...] = jnp.zeros_like(acc_ref)
        pl.semaphore_wait(barrier, owners - 1 + len(others))

    finish = project_part(
        me, hid_ref, gain_ref, w_ref, first_ref, nb, wb, fb, proj, res, got, ass, ars, enter
    )

    bounds = fb[11]
    low = bounds[0:1, :]
    high = bounds[1:2, :]
    begin = jnp.sum(
        qseg_ref[...].astype(jnp.float32) * low.astype(jnp.float32), axis=1, keepdims=True
    )
    token = (me.s * BLK + lax.broadcasted_iota(jnp.int32, (BLK, HD), 0)).astype(jnp.float32)
    angle = (token - begin) * freq_ref[0:1, :]
    lane = lax.broadcasted_iota(jnp.int32, (BLK, HD), 1)
    sine = jnp.sin(angle)
    sine = jnp.where(lane < HD // 2, -sine, sine)
    projected = got[...].reshape(BLK, 2 * HD)
    keys = projected[:, 0:HD]
    swapped = jnp.concatenate([keys[:, HD // 2 :], keys[:, : HD // 2]], axis=1)
    turned = keys * jnp.cos(angle) + swapped * sine
    kv = jnp.concatenate([turned, projected[:, HD:]], axis=1).astype(jnp.bfloat16)
    kv_ref = buf.at[0, 0, z, c]
    kv_ref[...] = kv

    def send(index, src, dst, target):
        remote(src, dst, ss.at[index], rs.at[index], target).start()

    def arrived(index, dst):
        remote(dst, dst, ss.at[index], rs.at[index], core).wait_recv()

    def block(rx, k, zi, cc):
        return buf.at[rx, k, wrap(z + zi, 2), cc]

    def mine(rx, k, zi):
        return block(rx, k, zi, c)

    order = (1, 3, 2)
    out_wrap = {rx: (x + rx >= 4).astype(jnp.int32) for rx in order}
    in_wrap = {rx: (x < rx).astype(jnp.int32) for rx in order}
    x1 = lambda rx, zi: 11 + 2 * (rx - 1) + zi
    x2 = lambda rx, zi: 17 + 2 * (rx - 1) + zi

    def second(rx, zi):
        w = out_wrap[rx]
        return remote(
            mine(0, 2 * w, zi), mine(rx, w, zi), ss.at[x2(rx, zi)], rs.at[x2(rx, zi)], me.at(dx=rx)
        )

    def send_second(zi, wraps):
        for rx in order:

            @pl.when(out_wrap[rx] == wraps)
            def _():
                second(rx, zi).start()

    def send_y(zi):
        send(3 + zi, mine(0, 0, zi), mine(0, 1, zi), me.at(dy=1))
        send(5 + zi, mine(0, 0, zi), mine(0, 2, zi), me.at(dy=2))
        send_second(zi, 0)

    def send_first(zi):
        for rx in order:
            send(x1(rx, zi), mine(0, 1, zi), mine(rx, 1 - out_wrap[rx], zi), me.at(dx=rx))

    def forward(first, then, rx, k, zi):
        arrived(first, mine(rx, k, zi))
        send(then, mine(rx, k, zi), mine(rx, k, zi), core)

    units = [
        (0, 0, 0, None, 0),
        (0, 1, 0, 3, 7),
        (0, 2, 0, 5, 9),
        (0, 0, 1, 1, 2),
        (0, 1, 1, 4, 8),
        (0, 2, 1, 6, 10),
    ]
    for zi in (0, 1):
        units += [(rx, 1 - in_wrap[rx], zi, x1(rx, zi), x1(rx, zi) + 12) for rx in order]
        units += [(rx, in_wrap[rx], zi, x2(rx, zi), x2(rx, zi) + 12) for rx in order]
    turn = [0, 1, 2, 3, 6, 7, 8, 4, 5, 9, 10, 11, 12, 13, 14, 15, 16, 17]
    units = [units[i] for i in turn]

    send(0, kv_ref, block(0, 0, 0, c), core)
    send(1, kv_ref, block(0, 0, 0, c), opposite)
    send_y(0)

    row = lax.broadcasted_iota(jnp.int32, (owners * 8, BLK), 0)
    select = (row == target_ref[0:1, :]).astype(jnp.bfloat16)
    chosen_pages = jnp.dot(select, kv, preferred_element_type=jnp.float32)
    pages_ref[...] = chosen_pages.astype(jnp.bfloat16).reshape(pages_ref.shape)
    pages[me.s] = pages_ref[me.s]

    quad_first = (me.y * 4 + x) * 4 * BLK
    place = 2 * z + c

    def step(source, first_key, causal):
        key = first_key + lax.broadcasted_iota(jnp.int32, (BLK, HD), 0)
        inside = (key >= low) & (key < high)
        bias = jnp.where(inside, 0.0, NEGATIVE).astype(jnp.bfloat16)
        keys = jnp.concatenate([source[:, 0:HD], bias], axis=1)
        scores = lax.dot_general(
            qa[...], keys, (((1,), (1,)), ((), ())), preferred_element_type=jnp.float32
        )
        if causal:
            row = lax.broadcasted_iota(jnp.int32, scores.shape, 0) & (BLK - 1)
            column = lax.broadcasted_iota(jnp.int32, scores.shape, 1)
            scores = jnp.where(column <= row, scores, NEGATIVE)
        old = m_ref[...]
        new = jnp.maximum(old, jnp.max(scores, axis=1, keepdims=True))
        offset = new * scale2
        weights = jnp.exp2(scores * scale2 - jnp.concatenate([offset, offset], axis=1))
        factor = jnp.exp2((old - new) * scale2)
        m_ref[...] = new
        l_ref[...] = l_ref[...] * factor + (weights[:, 0:HD] + weights[:, HD : 2 * HD])
        update = jnp.dot(
            weights.astype(jnp.bfloat16), source[:, HD : 2 * HD], preferred_element_type=jnp.float32
        )
        acc_ref[...] = acc_ref[...] * factor + update

    step(block(0, 0, 0, c), quad_first + place * BLK, True)

    def chosen(n, field):
        value = 0
        for i, unit in enumerate(units):
            value = value + (n == i).astype(jnp.int32) * unit[field]
        return value

    def serve(i):
        rx, k, zi, first, then = units[i]
        forward(first, then, rx, k, zi)
        if (rx, k) == (0, 1):
            send_first(zi)
        if (rx, k) == (0, 2):
            send_second(zi, 1)
        if (rx, k) == (0, 0):
            send_y(1)

    def one_unit(n, carry):
        for i in range(1, len(units)):

            @pl.when(n == i - 1)
            def _():
                serve(i)

        rx, k, zi, then = (chosen(n, field) for field in (0, 1, 2, 4))

        @pl.when(n < 8)
        def _():
            for i in range(8):

                @pl.when(n * 8 + i > 0)
                def _():
                    to = peer(n * 8 + i)
                    remote(pages_ref.at[to[0]], pages.at[me.s], ss.at[35], rs.at[35], to).start()

        def one_core(j, inner):
            cc = wrap(c + j, 2)
            source = block(rx, k, zi, cc)
            where = 2 * wrap(z + zi, 2) + cc

            @pl.when(j == 1)
            def _():
                arrived(then, source)

            distance = rx + 4 * k
            first_key = quad_first - distance * 4 * BLK + where * BLK
            skip = ((distance == 0) & (where >= place)) | ((distance == 8) & (where < place))

            @pl.when(jnp.logical_not(skip) & (first_key >= 0))
            def _():
                step(source, first_key, False)

            return inner

        return lax.fori_loop(0, 2, one_core, carry)

    lax.fori_loop(0, len(units), one_unit, 0)

    for h in range(heads):
        rows = slice(h * BLK, (h + 1) * BLK)
        total = jnp.sum(l_ref[rows, :], axis=1, keepdims=True)
        out_ref[:, h * HD : (h + 1) * HD] = (acc_ref[rows, :] / total).astype(out_ref.dtype)

    others = pl.ds(0, owners - 1)
    exchange = remote(pages_ref.at[others], pages.at[others], ss.at[35], rs.at[35], core)
    exchange.wait_recv()
    cache_ref[...] = pages[...]
    exchange.wait_send()
    for index in range(35):
        remote(kv_ref, block(0, 0, 0, c), ss.at[index], rs.at[index], core).wait_send()
    finish()


def layer(hidden, gain, weight, firsts, queries, query_onehot, freq, target):
    heads = queries.shape[1] // HD
    rows, width = hidden.shape
    columns = weight.shape[1]
    owners = lax.axis_size("seq")
    vmem = pl.BlockSpec(memory_space=pltpu.VMEM)
    return pl.pallas_call(
        layer_kernel,
        out_shape=(
            jax.ShapeDtypeStruct(queries.shape, jnp.bfloat16),
            jax.ShapeDtypeStruct((owners, 8, columns), jnp.bfloat16),
        ),
        in_specs=[vmem] * 8,
        out_specs=(vmem, vmem),
        scratch_shapes=[
            pltpu.VMEM((2, 2, 4, rows, width // 4), jnp.bfloat16),
            pltpu.VMEM((16, 2, width // 32, columns), jnp.bfloat16),
            pltpu.VMEM((12, 8, HD), jnp.int32),
            pltpu.VMEM((4 * rows, columns), jnp.float32),
            pltpu.VMEM((2, 2 * rows, columns), jnp.float32),
            pltpu.VMEM((2, 2 * rows, columns), jnp.float32),
            pltpu.SemaphoreType.DMA((57,)),
            pltpu.SemaphoreType.DMA((57,)),
            pltpu.VMEM((4, 3, 2, 2, BLK, 2 * HD), jnp.bfloat16),
            pltpu.VMEM((owners, 8, columns), jnp.bfloat16),
            pltpu.VMEM((owners, 8, columns), jnp.bfloat16),
            pltpu.VMEM((heads * BLK, 2 * HD), jnp.bfloat16),
            pltpu.VMEM((heads * BLK, HD), jnp.float32),
            pltpu.VMEM((heads * BLK, HD), jnp.float32),
            pltpu.VMEM((heads * BLK, HD), jnp.float32),
            pltpu.SemaphoreType.DMA((36,)),
            pltpu.SemaphoreType.DMA((36,)),
        ],
        compiler_params=pltpu.CompilerParams(
            collective_id=0, has_side_effects=True, vmem_limit_bytes=52 << 20
        ),
        cost_estimate=pl.CostEstimate(
            flops=10_000_000_000, bytes_accessed=4_000_000, transcendentals=17_000_000
        ),
    )(hidden, gain, weight, firsts, queries, query_onehot, freq, target)


def on_device(hidden, norm_gain, kv_weight, queries, segment_ids, page_owner):
    seq_count = lax.axis_size("seq")
    seq_place = lax.axis_index("seq")
    block_rows = segment_ids.shape[0]
    stream_rows = block_rows * seq_count
    token_index = seq_place * block_rows + jnp.arange(block_rows, dtype=jnp.int32)
    lanes = jnp.arange(HD, dtype=jnp.int32)
    member = segment_ids[:, None] == lanes[None, :]
    wanted = jnp.stack([lanes, lanes + 1])
    hit = segment_ids[None, None, :] == wanted[:, :, None]
    firsts = jnp.min(jnp.where(hit, token_index[None, None, :], stream_rows), axis=2)
    first_tile = jnp.pad(firsts, ((0, 6), (0, 0)))
    freq = 10000.0 ** (-jnp.arange(HD // 2, dtype=jnp.float32) * 2.0 / HD)
    freq_tile = jnp.broadcast_to(jnp.concatenate([freq, freq])[None, :], (8, HD))

    pages_block = page_owner.shape[0]
    page_rows = block_rows // pages_block
    capacity = max(2, 2 * pages_block // seq_count)
    owners = page_owner[:, 0]
    order = jnp.arange(pages_block, dtype=jnp.int32)
    earlier = (owners[None, :] == owners[:, None]) & (order[None, :] < order[:, None])
    rank = jnp.sum(earlier.astype(jnp.int32), axis=1)
    slot = (owners * capacity + rank) * page_rows
    target = (slot[:, None] + jnp.arange(page_rows, dtype=jnp.int32)[None, :]).reshape(1, block_rows)
    target_tile = jnp.broadcast_to(target, (8, block_rows))

    attended, arrived = layer(
        hidden,
        norm_gain[None, :],
        kv_weight,
        first_tile,
        queries,
        member.astype(jnp.bfloat16),
        freq_tile,
        target_tile,
    )
    kv_cache = arrived.reshape(1, seq_count, capacity, page_rows, arrived.shape[2])
    return (attended, kv_cache)


def solution(mesh):
    placed = (P(("seq", "fs"), None), P(), P("seq", "fs"), P("seq", "fs"), P("seq"), P("seq", None))
    return jax.shard_map(
        on_device,
        mesh=mesh,
        in_specs=placed,
        out_specs=(P("seq", "fs"), P("seq", None, None, None, "fs")),
        check_vma=False,
    )
```

```python
import functools

import jax
import jax.numpy as jnp
from jax import lax
from jax.experimental import pallas as pl
from jax.experimental.pallas import tpu as pltpu
from jax.sharding import PartitionSpec as P

HD = 128
SEGS = 4
EPSILON = 1e-05
NEGATIVE = -1e30
LOG2E = 1.4426950408889634
MESH = pl.DeviceIdType.MESH
BLK = 256


def wrap(value, count):
    return value - count * (value >= count).astype(jnp.int32)


class Place:
    def __init__(self):
        s = lax.axis_index("seq")
        self.s = s
        self.f = lax.axis_index("fs")
        self.c = lax.rem(s, 2)
        self.z = lax.rem(lax.div(s, 2), 2)
        self.x = lax.rem(lax.div(s, 4), 4)
        self.y = lax.div(s, 16)

    def at(self, dy=0, dx=0, other_z=False, other_core=False):
        y = wrap(self.y + dy, 4)
        x = wrap(self.x + dx, 4)
        z = 1 - self.z if other_z else self.z
        c = 1 - self.c if other_core else self.c
        return (((y * 4 + x) * 2 + z) * 2 + c, self.f)


def remote(src, dst, send, recv, target):
    return pltpu.make_async_remote_copy(
        src_ref=src, dst_ref=dst, send_sem=send, recv_sem=recv, device_id=target, device_id_type=MESH
    )


def project_part(
    me, hid_ref, gain_ref, w_ref, first_ref, qseg_ref, freq_ref,
    nb, wb, fb, acc, res, begins, buf, ss, rs, local, enter, idle
):
    c, z, x, y, f = me.c, me.z, me.x, me.y, me.f
    parity, group = lax.rem(f, 2), lax.div(f, 2)
    head = parity + 2 * c
    twin = lax.rem(f + 2, 4)
    mate = f + 1 - 2 * parity
    home = c == group
    chunks, rows, cols = nb.shape[2], nb.shape[3], nb.shape[4]

    def near(zz, cc, ff):
        return (((y * 4 + x) * 2 + zz) * 2 + cc, ff)

    core = near(z, 1 - c, f)
    ring_x = {k: me.at(dx=k) for k in (1, 2, 3)}
    ring_y = {k: me.at(dy=k) for k in (1, 2, 3)}
    enter([near(zz, cc, twin) for zz in (z, 1 - z) for cc in (c, 1 - c)] + [near(z, c, mate)])

    started = []

    def send(index, src, dst, target, recv=None):
        recv = index if recv is None else recv
        copy = remote(src, dst, ss.at[index], rs.at[recv], target)
        copy.start()
        started.append(copy)

    def arrived(index, dst):
        remote(dst, dst, ss.at[index], rs.at[index], core).wait_recv()

    quad = y * 4 + x
    shard = 2 * z + c
    rows_w = w_ref.shape[0]

    def piece(zz, cc):
        return wb.at[quad, zz, pl.ds(pl.multiple_of(cc * rows_w, rows_w), rows_w)]

    def seed_to_core():
        return remote(w_ref, piece(z, c), ss.at[0], rs.at[shard], core)

    @pl.when(home)
    def _():
        pltpu.make_async_copy(w_ref, piece(z, c), local).start()

    @pl.when(jnp.logical_not(home))
    def _():
        seed_to_core().start()

    send(1, w_ref, piece(z, c), near(z, group, twin), shard)
    send(2, w_ref, piece(z, c), near(1 - z, group, f), shard)
    send(3, w_ref, piece(z, c), near(1 - z, group, twin), shard)
    send(4, first_ref, fb.at[0], core)
    send(5, first_ref, fb.at[1], near(1 - z, c, f))
    send(6, first_ref, fb.at[2], near(1 - z, 1 - c, f))

    total = jnp.zeros((rows, 1), jnp.float32)
    for i in range(chunks):
        wide = hid_ref[:, i * cols : (i + 1) * cols].astype(jnp.float32)
        total = total + jnp.sum(wide * wide, axis=1, keepdims=True)
    factor = lax.rsqrt(total / (chunks * cols) + EPSILON)
    for i in range(chunks):
        wide = hid_ref[:, i * cols : (i + 1) * cols].astype(jnp.float32)
        gain = gain_ref[:, i * cols : (i + 1) * cols].astype(jnp.float32)
        nb[c, parity, i] = (wide * factor * gain).astype(jnp.bfloat16)
        send(13 + i, nb.at[c, parity, i], nb.at[c, parity, i], near(z, c, mate))
        send(17 + i, nb.at[c, parity, i], nb.at[c, parity, i], core)

    def seed_arrived(zz):
        for cc in (0, 1):
            own = jnp.logical_and(home, shard == 2 * zz + cc)

            @pl.when(own)
            def _():
                pltpu.make_async_copy(w_ref, piece(zz, cc), local).wait()

            @pl.when(jnp.logical_not(own))
            def _():
                arrived(2 * zz + cc, piece(zz, cc))

    half = lambda yy, xx, hh: wb.at[yy * 4 + xx, hh]
    back = lambda v, k: lax.rem(v + 4 - k, 4)
    order = (1, 3, 2)
    seed_arrived(0)
    for k in order:
        send(24 + k, half(y, x, 0), half(y, x, 0), ring_x[k])
    seed_arrived(1)
    for k in order:
        send(27 + k, half(y, x, 1), half(y, x, 1), ring_y[k])

    a2 = lambda k, j: 31 + (k - 1) * 4 + j
    b2 = lambda k, j: 43 + (k - 1) * 4 + j

    def spread(j):
        ya, xa = y, back(x, j)
        yb, xb = back(y, j), x
        if j:
            arrived(24 + j, half(ya, xa, 0))
        for k in order:
            send(a2(k, j), half(ya, xa, 0), half(ya, xa, 0), ring_y[k])
        if j:
            arrived(27 + j, half(yb, xb, 1))
        for k in order:
            send(b2(k, j), half(yb, xb, 1), half(yb, xb, 1), ring_x[k])

    def forward(i):
        arrived(13 + i, nb.at[c, 1 - parity, i])
        send(21 + i, nb.at[c, 1 - parity, i], nb.at[c, 1 - parity, i], core)

    spread(0)
    idle()
    for i in range(3):
        arrived(4 + i, fb.at[i])
    fb[3] = jnp.minimum(jnp.minimum(first_ref[...], fb[0]), jnp.minimum(fb[1], fb[2]))
    for k in order:
        send(6 + k, fb.at[3], fb.at[3 + k], ring_x[k])
    forward(0)
    spread(1)
    spread(3)
    forward(1)
    spread(2)
    for k in order:
        arrived(6 + k, fb.at[3 + k])
    fb[7] = jnp.minimum(jnp.minimum(fb[3], fb[4]), jnp.minimum(fb[5], fb[6]))
    for k in order:
        send(9 + k, fb.at[7], fb.at[7 + k], ring_y[k])
    forward(2)
    forward(3)
    for k in order:
        arrived(9 + k, fb.at[7 + k])
    fb[11] = jnp.minimum(jnp.minimum(fb[7], fb[8]), jnp.minimum(fb[9], fb[10]))
    first_row = fb[11][0:1, :].astype(jnp.float32)
    begin = jnp.sum(qseg_ref[...].astype(jnp.float32) * first_row, axis=1, keepdims=True)
    begins[c] = jnp.broadcast_to(begin, begins.shape[1:])
    send(59, begins.at[c], begins.at[c], core)
    for i in range(chunks):
        arrived(17 + i, nb.at[1 - c, parity, i])
        arrived(21 + i, nb.at[1 - c, 1 - parity, i])

    acc[...] = jnp.zeros_like(acc)

    def multiply(yy, xx, hh):
        columns = pl.ds(pl.multiple_of(xx * 512 + hh * 256, 256), 256)
        lhs = nb[:, :, yy, :, columns].reshape(4 * rows, 256)
        acc[...] += jnp.dot(lhs, wb[yy * 4 + xx, hh], preferred_element_type=jnp.float32)

    multiply(y, x, 0)
    multiply(y, x, 1)
    for j in order:
        multiply(y, back(x, j), 0)
        multiply(back(y, j), x, 1)
    for j in (0, 1, 3, 2):
        for k in order:
            yy, xx = back(y, k), back(x, j)
            arrived(a2(k, j), half(yy, xx, 0))
            multiply(yy, xx, 0)
            yy, xx = back(y, j), back(x, k)
            arrived(b2(k, j), half(yy, xx, 1))
            multiply(yy, xx, 1)

    arrived(59, begins.at[1 - c])
    pair = 2 * rows
    rows_g = pl.ds(pl.multiple_of(group * pair, pair), pair)
    lane = lax.broadcasted_iota(jnp.int32, (pair, HD), 1)
    for cc in (0, 1):
        first_token = (me.s - c + cc) * BLK + group * pair
        token = first_token + lax.broadcasted_iota(jnp.int32, (pair, HD), 0)
        angle = (token.astype(jnp.float32) - begins[cc, rows_g, :]) * freq_ref[0:1, :]
        sine = jnp.sin(angle)
        sine = jnp.where(lane < HD // 2, -sine, sine)
        keys = acc[cc * pair : (cc + 1) * pair, 0:HD]
        swapped = jnp.concatenate([keys[:, HD // 2 :], keys[:, : HD // 2]], axis=1)
        turned = keys * jnp.cos(angle) + swapped * sine
        res[cc, :, 0:HD] = turned.astype(jnp.bfloat16)
        res[cc, :, HD:] = acc[cc * pair : (cc + 1) * pair, HD:].astype(jnp.bfloat16)

    def part(zz, cc, g):
        return buf.at[0, 0, zz, cc, pl.ds(pl.multiple_of(g * pair, pair), pair)]

    def result_to(zz, cc, ff, index, recv):
        return remote(
            res.at[cc], part(z, cc, group), ss.at[index], rs.at[recv + group], near(zz, cc, ff)
        )

    @pl.when(home)
    def _():
        result_to(z, 1 - c, f, 55, 55).start()
        result_to(1 - z, 0, f, 57, 57).start()
        result_to(1 - z, 1, f, 58, 57).start()
        buf[0, 0, z, c, rows_g, :] = res[c]

    @pl.when(jnp.logical_not(home))
    def _():
        result_to(z, 0, twin, 55, 55).start()
        result_to(z, 1, twin, 56, 55).start()
        result_to(1 - z, 0, twin, 57, 57).start()
        result_to(1 - z, 1, twin, 58, 57).start()

    for g in (0, 1):

        @pl.when(jnp.logical_not(jnp.logical_and(home, group == g)))
        def _():
            arrived(55 + g, part(z, c, g))

    def opposite_arrived():
        for g in (0, 1):
            arrived(57 + g, part(1 - z, c, g))

    def finish():
        for copy in started:
            copy.wait_send()

        @pl.when(home)
        def _():
            result_to(z, 1 - c, f, 55, 55).wait_send()

        @pl.when(jnp.logical_not(home))
        def _():
            seed_to_core().wait_send()
            result_to(z, 0, twin, 55, 55).wait_send()
            result_to(z, 1, twin, 56, 55).wait_send()

        result_to(1 - z, 0, f, 57, 57).wait_send()
        result_to(1 - z, 1, f, 58, 57).wait_send()

    return finish, opposite_arrived


def layer_kernel(
    hid_hbm, gain_ref, w_ref, first_ref, q_hbm, qseg_ref, freq_ref, target_ref,
    out_ref, cache_ref,
    hid, q, nb, wb, fb, proj, res, begins, ass, ars, local,
    buf, pages, pages_ref, qa, m_ref, l_ref, acc_ref, ss, rs
):
    me = Place()
    c, z, x = me.c, me.z, me.x
    heads = q.shape[1] // HD
    owners = pages_ref.shape[0]
    scale2 = (HD ** (-0.5)) * LOG2E
    core = me.at(other_core=True)
    load_hidden = pltpu.make_async_copy(hid_hbm, hid, local.at[0])
    load_queries = pltpu.make_async_copy(q_hbm, q, local.at[1])
    load_hidden.start()
    load_queries.start()

    def peer(distance):
        return (wrap(me.s + distance, owners), me.f)

    def enter(others):
        barrier = pltpu.get_barrier_semaphore()

        def greet(distance, carry):
            pl.semaphore_signal(barrier, inc=1, device_id=peer(distance), device_id_type=MESH)
            return carry

        for other in others:
            pl.semaphore_signal(barrier, inc=1, device_id=other, device_id_type=MESH)
        lax.fori_loop(1, owners, greet, 0)
        pl.semaphore_wait(barrier, owners - 1 + len(others))
        load_hidden.wait()

    def idle():
        load_queries.wait()
        for h in range(heads):
            qa[h * BLK : (h + 1) * BLK, 0:HD] = q[:, h * HD : (h + 1) * HD]
            qa[h * BLK : (h + 1) * BLK, HD : 2 * HD] = qseg_ref[...]
        m_ref[...] = jnp.full_like(m_ref, NEGATIVE)
        l_ref[...] = jnp.zeros_like(l_ref)
        acc_ref[...] = jnp.zeros_like(acc_ref)

    finish, opposite_arrived = project_part(
        me, hid, gain_ref, w_ref, first_ref, qseg_ref, freq_ref,
        nb, wb, fb, proj, res, begins, buf, ass, ars, local.at[2], enter, idle,
    )
    bounds = fb[11]
    low = bounds[0:1, :]
    high = bounds[1:2, :]
    kv_ref = buf.at[0, 0, z, c]

    def send(index, src, dst, target):
        remote(src, dst, ss.at[index], rs.at[index], target).start()

    def arrived(index, dst):
        remote(dst, dst, ss.at[index], rs.at[index], core).wait_recv()

    def block(rx, k, zi, cc):
        return buf.at[rx, k, wrap(z + zi, 2), cc]

    def mine(rx, k, zi):
        return block(rx, k, zi, c)

    order = (1, 3, 2)
    out_wrap = {rx: (x + rx >= 4).astype(jnp.int32) for rx in order}
    in_wrap = {rx: (x < rx).astype(jnp.int32) for rx in order}
    x1 = lambda rx, zi: 11 + 2 * (rx - 1) + zi
    x2 = lambda rx, zi: 17 + 2 * (rx - 1) + zi

    def second(rx, zi):
        w = out_wrap[rx]
        return remote(
            mine(0, 2 * w, zi), mine(rx, w, zi), ss.at[x2(rx, zi)], rs.at[x2(rx, zi)], me.at(dx=rx)
        )

    def send_second(zi, wraps):
        for rx in order:

            @pl.when(out_wrap[rx] == wraps)
            def _():
                second(rx, zi).start()

    def send_y(zi):
        send(3 + zi, mine(0, 0, zi), mine(0, 1, zi), me.at(dy=1))
        send(5 + zi, mine(0, 0, zi), mine(0, 2, zi), me.at(dy=2))
        send_second(zi, 0)

    def send_first(zi):
        for rx in order:
            send(x1(rx, zi), mine(0, 1, zi), mine(rx, 1 - out_wrap[rx], zi), me.at(dx=rx))

    def forward(first, then, rx, k, zi):
        arrived(first, mine(rx, k, zi))
        send(then, mine(rx, k, zi), mine(rx, k, zi), core)

    units = [
        (0, 0, 0, None, 0),
        (0, 1, 0, 3, 7),
        (0, 2, 0, 5, 9),
        (0, 0, 1, None, 2),
        (0, 1, 1, 4, 8),
        (0, 2, 1, 6, 10),
    ]
    for zi in (0, 1):
        units += [(rx, 1 - in_wrap[rx], zi, x1(rx, zi), x1(rx, zi) + 12) for rx in order]
        units += [(rx, in_wrap[rx], zi, x2(rx, zi), x2(rx, zi) + 12) for rx in order]
    turn = [0, 1, 2, 3, 6, 7, 8, 4, 5, 9, 10, 11, 12, 13, 14, 15, 16, 17]
    units = [units[i] for i in turn]

    send(0, kv_ref, block(0, 0, 0, c), core)
    send_y(0)

    row = lax.broadcasted_iota(jnp.int32, (owners * 8, BLK), 0)
    select = (row == target_ref[0:1, :]).astype(jnp.bfloat16)
    chosen_pages = jnp.dot(select, kv_ref[...], preferred_element_type=jnp.float32)
    pages_ref[...] = chosen_pages.astype(jnp.bfloat16).reshape(pages_ref.shape)
    pages[me.s] = pages_ref[me.s]

    quad_first = (me.y * 4 + x) * 4 * BLK
    place = 2 * z + c

    def step(source, first_key, causal):
        key = first_key + lax.broadcasted_iota(jnp.int32, (BLK, HD), 0)
        inside = (key >= low) & (key < high)
        bias = jnp.where(inside, 0.0, NEGATIVE).astype(jnp.bfloat16)
        keys = jnp.concatenate([source[:, 0:HD], bias], axis=1)
        scores = lax.dot_general(
            qa[...], keys, (((1,), (1,)), ((), ())), preferred_element_type=jnp.float32
        )
        if causal:
            row = lax.broadcasted_iota(jnp.int32, scores.shape, 0) & (BLK - 1)
            column = lax.broadcasted_iota(jnp.int32, scores.shape, 1)
            scores = jnp.where(column <= row, scores, NEGATIVE)
        old = m_ref[...]
        new = jnp.maximum(old, jnp.max(scores, axis=1, keepdims=True))
        offset = new * scale2
        weights = jnp.exp2(scores * scale2 - jnp.concatenate([offset, offset], axis=1))
        factor = jnp.exp2((old - new) * scale2)
        m_ref[...] = new
        l_ref[...] = l_ref[...] * factor + (weights[:, 0:HD] + weights[:, HD : 2 * HD])
        update = jnp.dot(
            weights.astype(jnp.bfloat16), source[:, HD : 2 * HD], preferred_element_type=jnp.float32
        )
        acc_ref[...] = acc_ref[...] * factor + update

    step(block(0, 0, 0, c), quad_first + place * BLK, True)

    def chosen(n, field):
        value = 0
        for i, unit in enumerate(units):
            value = value + (n == i).astype(jnp.int32) * unit[field]
        return value

    def serve(i):
        rx, k, zi, first, then = units[i]
        if first is None:
            opposite_arrived()
            send(then, mine(rx, k, zi), mine(rx, k, zi), core)
        else:
            forward(first, then, rx, k, zi)
        if (rx, k) == (0, 1):
            send_first(zi)
        if (rx, k) == (0, 2):
            send_second(zi, 1)
        if (rx, k) == (0, 0):
            send_y(1)

    def one_unit(n, carry):
        for i in range(1, len(units)):

            @pl.when(n == i - 1)
            def _():
                serve(i)

        rx, k, zi, then = (chosen(n, field) for field in (0, 1, 2, 4))

        @pl.when(n < 8)
        def _():
            for i in range(8):

                @pl.when(n * 8 + i > 0)
                def _():
                    to = peer(n * 8 + i)
                    remote(pages_ref.at[to[0]], pages.at[me.s], ss.at[35], rs.at[35], to).start()

        def one_core(j, inner):
            cc = wrap(c + j, 2)
            source = block(rx, k, zi, cc)
            where = 2 * wrap(z + zi, 2) + cc

            @pl.when(j == 1)
            def _():
                arrived(then, source)

            distance = rx + 4 * k
            first_key = quad_first - distance * 4 * BLK + where * BLK
            skip = ((distance == 0) & (where >= place)) | ((distance == 8) & (where < place))

            @pl.when(jnp.logical_not(skip) & (first_key >= 0))
            def _():
                step(source, first_key, False)

            return inner

        return lax.fori_loop(0, 2, one_core, carry)

    lax.fori_loop(0, len(units), one_unit, 0)

    for h in range(heads):
        rows = slice(h * BLK, (h + 1) * BLK)
        total = jnp.sum(l_ref[rows, :], axis=1, keepdims=True)
        out_ref[:, h * HD : (h + 1) * HD] = (acc_ref[rows, :] / total).astype(out_ref.dtype)

    others = pl.ds(0, owners - 1)
    exchange = remote(pages_ref.at[others], pages.at[others], ss.at[35], rs.at[35], core)
    exchange.wait_recv()
    cache_ref[...] = pages[...]
    exchange.wait_send()
    for index in [0] + list(range(2, 35)):
        remote(kv_ref, block(0, 0, 0, c), ss.at[index], rs.at[index], core).wait_send()
    finish()


def layer(hidden, gain, weight, firsts, queries, query_onehot, freq, target):
    heads = queries.shape[1] // HD
    rows, width = hidden.shape
    columns = weight.shape[1]
    owners = lax.axis_size("seq")
    away = pl.BlockSpec(memory_space=pl.ANY)
    vmem = pl.BlockSpec(memory_space=pltpu.VMEM)
    return pl.pallas_call(
        layer_kernel,
        out_shape=(
            jax.ShapeDtypeStruct(queries.shape, jnp.bfloat16),
            jax.ShapeDtypeStruct((owners, 8, columns), jnp.bfloat16),
        ),
        in_specs=[away, vmem, away, vmem, away, vmem, vmem, vmem],
        out_specs=(vmem, vmem),
        scratch_shapes=[
            pltpu.VMEM(hidden.shape, jnp.bfloat16),
            pltpu.VMEM(queries.shape, jnp.bfloat16),
            pltpu.VMEM((2, 2, 4, rows, width // 4), jnp.bfloat16),
            pltpu.VMEM((16, 2, width // 32, columns), jnp.bfloat16),
            pltpu.VMEM((12, 8, HD), jnp.int32),
            pltpu.VMEM((4 * rows, columns), jnp.float32),
            pltpu.VMEM((2, 2 * rows, columns), jnp.bfloat16),
            pltpu.VMEM((2, 4 * rows, HD), jnp.float32),
            pltpu.SemaphoreType.DMA((60,)),
            pltpu.SemaphoreType.DMA((60,)),
            pltpu.SemaphoreType.DMA((3,)),
            pltpu.VMEM((4, 3, 2, 2, BLK, 2 * HD), jnp.bfloat16),
            pltpu.VMEM((owners, 8, columns), jnp.bfloat16),
            pltpu.VMEM((owners, 8, columns), jnp.bfloat16),
            pltpu.VMEM((heads * BLK, 2 * HD), jnp.bfloat16),
            pltpu.VMEM((heads * BLK, HD), jnp.float32),
            pltpu.VMEM((heads * BLK, HD), jnp.float32),
            pltpu.VMEM((heads * BLK, HD), jnp.float32),
            pltpu.SemaphoreType.DMA((36,)),
            pltpu.SemaphoreType.DMA((36,)),
        ],
        compiler_params=pltpu.CompilerParams(
            collective_id=0, has_side_effects=True, vmem_limit_bytes=52 << 20
        ),
        cost_estimate=pl.CostEstimate(
            flops=10_000_000_000, bytes_accessed=4_000_000, transcendentals=17_000_000
        ),
    )(hidden, gain, weight, firsts, queries, query_onehot, freq, target)


def on_device(hidden, norm_gain, kv_weight, queries, segment_ids, page_owner):
    seq_count = lax.axis_size("seq")
    seq_place = lax.axis_index("seq")
    block_rows = segment_ids.shape[0]
    stream_rows = block_rows * seq_count
    token_index = seq_place * block_rows + jnp.arange(block_rows, dtype=jnp.int32)
    lanes = jnp.arange(HD, dtype=jnp.int32)
    member = segment_ids[:, None] == lanes[None, :]
    wanted = jnp.stack([lanes, lanes + 1])
    hit = segment_ids[None, None, :] == wanted[:, :, None]
    firsts = jnp.min(jnp.where(hit, token_index[None, None, :], stream_rows), axis=2)
    first_tile = jnp.pad(firsts, ((0, 6), (0, 0)))
    freq = 10000.0 ** (-jnp.arange(HD // 2, dtype=jnp.float32) * 2.0 / HD)
    freq_tile = jnp.broadcast_to(jnp.concatenate([freq, freq])[None, :], (8, HD))

    pages_block = page_owner.shape[0]
    page_rows = block_rows // pages_block
    capacity = max(2, 2 * pages_block // seq_count)
    owners = page_owner[:, 0]
    order = jnp.arange(pages_block, dtype=jnp.int32)
    earlier = (owners[None, :] == owners[:, None]) & (order[None, :] < order[:, None])
    rank = jnp.sum(earlier.astype(jnp.int32), axis=1)
    slot = (owners * capacity + rank) * page_rows
    target = (slot[:, None] + jnp.arange(page_rows, dtype=jnp.int32)[None, :]).reshape(1, block_rows)
    target_tile = jnp.broadcast_to(target, (8, block_rows))

    attended, arrived = layer(
        hidden,
        norm_gain[None, :],
        kv_weight,
        first_tile,
        queries,
        member.astype(jnp.bfloat16),
        freq_tile,
        target_tile,
    )
    kv_cache = arrived.reshape(1, seq_count, capacity, page_rows, arrived.shape[2])
    return (attended, kv_cache)


def solution(mesh):
    placed = (P(("seq", "fs"), None), P(), P("seq", "fs"), P("seq", "fs"), P("seq"), P("seq", None))
    return jax.shard_map(
        on_device,
        mesh=mesh,
        in_specs=placed,
        out_specs=(P("seq", "fs"), P("seq", None, None, None, "fs")),
        check_vma=False,
    )
```

```python
import functools

import jax
import jax.numpy as jnp
from jax import lax
from jax.experimental import pallas as pl
from jax.experimental.pallas import tpu as pltpu
from jax.sharding import PartitionSpec as P

HD = 128
SEGS = 4
EPSILON = 1e-05
NEGATIVE = -1e30
LOG2E = 1.4426950408889634
MESH = pl.DeviceIdType.MESH
BLK = 256


def wrap(value, count):
    return value - count * (value >= count).astype(jnp.int32)


class Place:
    def __init__(self):
        s = lax.axis_index("seq")
        self.s = s
        self.f = lax.axis_index("fs")
        self.c = lax.rem(s, 2)
        self.z = lax.rem(lax.div(s, 2), 2)
        self.x = lax.rem(lax.div(s, 4), 4)
        self.y = lax.div(s, 16)

    def at(self, dy=0, dx=0, other_z=False, other_core=False):
        y = wrap(self.y + dy, 4)
        x = wrap(self.x + dx, 4)
        z = 1 - self.z if other_z else self.z
        c = 1 - self.c if other_core else self.c
        return (((y * 4 + x) * 2 + z) * 2 + c, self.f)


def remote(src, dst, send, recv, target):
    return pltpu.make_async_remote_copy(
        src_ref=src, dst_ref=dst, send_sem=send, recv_sem=recv, device_id=target, device_id_type=MESH
    )


def project_part(
    me, hid_ref, gain_ref, w_ref, first_ref, qseg_ref, freq_ref,
    nb, wb, fb, acc, res, begins, buf, ss, rs, local, enter, idle
):
    c, z, x, y, f = me.c, me.z, me.x, me.y, me.f
    parity, group = lax.rem(f, 2), lax.div(f, 2)
    head = parity + 2 * c
    twin = lax.rem(f + 2, 4)
    mate = f + 1 - 2 * parity
    home = c == group
    chunks, rows, cols = nb.shape[2], nb.shape[3], nb.shape[4]

    def near(zz, cc, ff):
        return (((y * 4 + x) * 2 + zz) * 2 + cc, ff)

    core = near(z, 1 - c, f)
    ring_x = {k: me.at(dx=k) for k in (1, 2, 3)}
    ring_y = {k: me.at(dy=k) for k in (1, 2, 3)}
    enter([near(zz, cc, twin) for zz in (z, 1 - z) for cc in (c, 1 - c)] + [near(z, c, mate)])

    started = []

    def send(index, src, dst, target, recv=None):
        recv = index if recv is None else recv
        copy = remote(src, dst, ss.at[index], rs.at[recv], target)
        copy.start()
        started.append(copy)

    def arrived(index, dst):
        remote(dst, dst, ss.at[index], rs.at[index], core).wait_recv()

    quad = y * 4 + x
    shard = 2 * z + c
    rows_w = w_ref.shape[0]

    def piece(zz, cc):
        return wb.at[quad, zz, pl.ds(pl.multiple_of(cc * rows_w, rows_w), rows_w)]

    def seed_to_core():
        return remote(w_ref, piece(z, c), ss.at[0], rs.at[shard], core)

    @pl.when(home)
    def _():
        pltpu.make_async_copy(w_ref, piece(z, c), local).start()

    @pl.when(jnp.logical_not(home))
    def _():
        seed_to_core().start()

    send(1, w_ref, piece(z, c), near(z, group, twin), shard)
    send(2, w_ref, piece(z, c), near(1 - z, group, f), shard)
    send(3, w_ref, piece(z, c), near(1 - z, group, twin), shard)
    send(4, first_ref, fb.at[0], core)
    send(5, first_ref, fb.at[1], near(1 - z, c, f))
    send(6, first_ref, fb.at[2], near(1 - z, 1 - c, f))

    total = jnp.zeros((rows, 1), jnp.float32)
    for i in range(chunks):
        wide = hid_ref[:, i * cols : (i + 1) * cols].astype(jnp.float32)
        total = total + jnp.sum(wide * wide, axis=1, keepdims=True)
    factor = lax.rsqrt(total / (chunks * cols) + EPSILON)
    for i in range(chunks):
        wide = hid_ref[:, i * cols : (i + 1) * cols].astype(jnp.float32)
        gain = gain_ref[:, i * cols : (i + 1) * cols].astype(jnp.float32)
        nb[c, parity, i] = (wide * factor * gain).astype(jnp.bfloat16)
        send(13 + i, nb.at[c, parity, i], nb.at[c, parity, i], near(z, c, mate))
        send(17 + i, nb.at[c, parity, i], nb.at[c, parity, i], core)

    def seed_arrived(zz):
        for cc in (0, 1):
            own = jnp.logical_and(home, shard == 2 * zz + cc)

            @pl.when(own)
            def _():
                pltpu.make_async_copy(w_ref, piece(zz, cc), local).wait()

            @pl.when(jnp.logical_not(own))
            def _():
                arrived(2 * zz + cc, piece(zz, cc))

    half = lambda yy, xx, hh: wb.at[yy * 4 + xx, hh]
    back = lambda v, k: lax.rem(v + 4 - k, 4)
    order = (1, 3, 2)
    seed_arrived(0)
    for k in order:
        send(24 + k, half(y, x, 0), half(y, x, 0), ring_x[k])
    seed_arrived(1)
    for k in order:
        send(27 + k, half(y, x, 1), half(y, x, 1), ring_y[k])

    a2 = lambda k, j: 31 + (k - 1) * 4 + j
    b2 = lambda k, j: 43 + (k - 1) * 4 + j

    def spread(j):
        ya, xa = y, back(x, j)
        yb, xb = back(y, j), x
        if j:
            arrived(24 + j, half(ya, xa, 0))
        for k in order:
            send(a2(k, j), half(ya, xa, 0), half(ya, xa, 0), ring_y[k])
        if j:
            arrived(27 + j, half(yb, xb, 1))
        for k in order:
            send(b2(k, j), half(yb, xb, 1), half(yb, xb, 1), ring_x[k])

    def forward(i):
        arrived(13 + i, nb.at[c, 1 - parity, i])
        send(21 + i, nb.at[c, 1 - parity, i], nb.at[c, 1 - parity, i], core)

    spread(0)
    idle()
    for i in range(3):
        arrived(4 + i, fb.at[i])
    fb[3] = jnp.minimum(jnp.minimum(first_ref[...], fb[0]), jnp.minimum(fb[1], fb[2]))
    for k in order:
        send(6 + k, fb.at[3], fb.at[3 + k], ring_x[k])
    forward(0)
    spread(1)
    spread(3)
    forward(1)
    spread(2)
    for k in order:
        arrived(6 + k, fb.at[3 + k])
    fb[7] = jnp.minimum(jnp.minimum(fb[3], fb[4]), jnp.minimum(fb[5], fb[6]))
    for k in order:
        send(9 + k, fb.at[7], fb.at[7 + k], ring_y[k])
    forward(2)
    forward(3)
    for k in order:
        arrived(9 + k, fb.at[7 + k])
    fb[11] = jnp.minimum(jnp.minimum(fb[7], fb[8]), jnp.minimum(fb[9], fb[10]))
    first_row = fb[11][0:1, :].astype(jnp.float32)
    begin = jnp.sum(qseg_ref[...].astype(jnp.float32) * first_row, axis=1, keepdims=True)
    begins[c] = jnp.broadcast_to(begin, begins.shape[1:])
    send(59, begins.at[c], begins.at[c], core)
    for i in range(chunks):
        arrived(17 + i, nb.at[1 - c, parity, i])
        arrived(21 + i, nb.at[1 - c, 1 - parity, i])

    acc[...] = jnp.zeros_like(acc)

    def multiply(yy, xx, hh):
        columns = pl.ds(pl.multiple_of(xx * 512 + hh * 256, 256), 256)
        lhs = nb[:, :, yy, :, columns].reshape(4 * rows, 256)
        acc[...] += jnp.dot(lhs, wb[yy * 4 + xx, hh], preferred_element_type=jnp.float32)

    multiply(y, x, 0)
    multiply(y, x, 1)
    for j in order:
        multiply(y, back(x, j), 0)
        multiply(back(y, j), x, 1)
    for j in (0, 1, 3, 2):
        for k in order:
            yy, xx = back(y, k), back(x, j)
            arrived(a2(k, j), half(yy, xx, 0))
            multiply(yy, xx, 0)
            yy, xx = back(y, j), back(x, k)
            arrived(b2(k, j), half(yy, xx, 1))
            multiply(yy, xx, 1)

    arrived(59, begins.at[1 - c])
    pair = 2 * rows
    rows_g = pl.ds(pl.multiple_of(group * pair, pair), pair)
    lane = lax.broadcasted_iota(jnp.int32, (pair, HD), 1)
    for cc in (0, 1):
        first_token = (me.s - c + cc) * BLK + group * pair
        token = first_token + lax.broadcasted_iota(jnp.int32, (pair, HD), 0)
        angle = (token.astype(jnp.float32) - begins[cc, rows_g, :]) * freq_ref[0:1, :]
        sine = jnp.sin(angle)
        sine = jnp.where(lane < HD // 2, -sine, sine)
        keys = acc[cc * pair : (cc + 1) * pair, 0:HD]
        swapped = jnp.concatenate([keys[:, HD // 2 :], keys[:, : HD // 2]], axis=1)
        turned = keys * jnp.cos(angle) + swapped * sine
        res[cc, :, 0:HD] = turned.astype(jnp.bfloat16)
        res[cc, :, HD:] = acc[cc * pair : (cc + 1) * pair, HD:].astype(jnp.bfloat16)

    def part(zz, cc, g):
        return buf.at[0, 0, zz, cc, pl.ds(pl.multiple_of(g * pair, pair), pair)]

    def result_to(zz, cc, ff, index, recv):
        return remote(
            res.at[cc], part(z, cc, group), ss.at[index], rs.at[recv + group], near(zz, cc, ff)
        )

    @pl.when(home)
    def _():
        result_to(z, 1 - c, f, 55, 55).start()
        result_to(1 - z, 0, f, 57, 57).start()
        result_to(1 - z, 1, f, 58, 57).start()
        buf[0, 0, z, c, rows_g, :] = res[c]

    @pl.when(jnp.logical_not(home))
    def _():
        result_to(z, 0, twin, 55, 55).start()
        result_to(z, 1, twin, 56, 55).start()
        result_to(1 - z, 0, twin, 57, 57).start()
        result_to(1 - z, 1, twin, 58, 57).start()

    for g in (0, 1):

        @pl.when(jnp.logical_not(jnp.logical_and(home, group == g)))
        def _():
            arrived(55 + g, part(z, c, g))

    def opposite_arrived():
        for g in (0, 1):
            arrived(57 + g, part(1 - z, c, g))

    def finish():
        for copy in started:
            copy.wait_send()

        @pl.when(home)
        def _():
            result_to(z, 1 - c, f, 55, 55).wait_send()

        @pl.when(jnp.logical_not(home))
        def _():
            seed_to_core().wait_send()
            result_to(z, 0, twin, 55, 55).wait_send()
            result_to(z, 1, twin, 56, 55).wait_send()

        result_to(1 - z, 0, f, 57, 57).wait_send()
        result_to(1 - z, 1, f, 58, 57).wait_send()

    return finish, opposite_arrived


def layer_kernel(
    hid_hbm, gain_ref, w_ref, first_ref, q_hbm, qseg_ref, freq_ref, target_ref,
    out_ref, cache_ref,
    hid, q, nb, wb, fb, proj, res, begins, ass, ars, local,
    buf, pages, pages_ref, qa, m_ref, l_ref, acc_ref, ss, rs
):
    me = Place()
    c, z, x = me.c, me.z, me.x
    heads = q.shape[1] // HD
    owners = pages_ref.shape[0]
    scale2 = (HD ** (-0.5)) * LOG2E
    core = me.at(other_core=True)
    load_hidden = pltpu.make_async_copy(hid_hbm, hid, local.at[0])
    load_queries = pltpu.make_async_copy(q_hbm, q, local.at[1])
    load_hidden.start()
    load_queries.start()

    def peer(distance):
        return (wrap(me.s + distance, owners), me.f)

    def enter(others):
        barrier = pltpu.get_barrier_semaphore()

        def greet(distance, carry):
            pl.semaphore_signal(barrier, inc=1, device_id=peer(distance), device_id_type=MESH)
            return carry

        for other in others:
            pl.semaphore_signal(barrier, inc=1, device_id=other, device_id_type=MESH)
        lax.fori_loop(1, owners, greet, 0)
        pl.semaphore_wait(barrier, owners - 1 + len(others))
        load_hidden.wait()

    def idle():
        load_queries.wait()
        for h in range(heads):
            qa[h * BLK : (h + 1) * BLK, 0:HD] = q[:, h * HD : (h + 1) * HD]
            qa[h * BLK : (h + 1) * BLK, HD : 2 * HD] = qseg_ref[...]
        m_ref[...] = jnp.full_like(m_ref, NEGATIVE)
        l_ref[...] = jnp.zeros_like(l_ref)
        acc_ref[...] = jnp.zeros_like(acc_ref)

    finish, opposite_arrived = project_part(
        me, hid, gain_ref, w_ref, first_ref, qseg_ref, freq_ref,
        nb, wb, fb, proj, res, begins, buf, ass, ars, local.at[2], enter, idle,
    )
    bounds = fb[11]
    low = bounds[0:1, :]
    high = bounds[1:2, :]
    kv_ref = buf.at[0, 0, z, c]

    def send(index, src, dst, target):
        remote(src, dst, ss.at[index], rs.at[index], target).start()

    def arrived(index, dst):
        remote(dst, dst, ss.at[index], rs.at[index], core).wait_recv()

    def block(rx, k, zi, cc):
        return buf.at[rx, k, wrap(z + zi, 2), cc]

    def mine(rx, k, zi):
        return block(rx, k, zi, c)

    order = (1, 3, 2)
    out_wrap = {rx: (x + rx >= 4).astype(jnp.int32) for rx in order}
    in_wrap = {rx: (x < rx).astype(jnp.int32) for rx in order}
    x1 = lambda rx, zi: 11 + 2 * (rx - 1) + zi
    x2 = lambda rx, zi: 17 + 2 * (rx - 1) + zi

    def second(rx, zi):
        w = out_wrap[rx]
        return remote(
            mine(0, 2 * w, zi), mine(rx, w, zi), ss.at[x2(rx, zi)], rs.at[x2(rx, zi)], me.at(dx=rx)
        )

    def send_second(zi, wraps):
        for rx in order:

            @pl.when(out_wrap[rx] == wraps)
            def _():
                second(rx, zi).start()

    def send_y(zi):
        send(3 + zi, mine(0, 0, zi), mine(0, 1, zi), me.at(dy=1))
        send(5 + zi, mine(0, 0, zi), mine(0, 2, zi), me.at(dy=2))
        send_second(zi, 0)

    def send_first(zi):
        for rx in order:
            send(x1(rx, zi), mine(0, 1, zi), mine(rx, 1 - out_wrap[rx], zi), me.at(dx=rx))

    def forward(first, then, rx, k, zi):
        arrived(first, mine(rx, k, zi))
        send(then, mine(rx, k, zi), mine(rx, k, zi), core)

    units = [
        (0, 0, 0, None, 0),
        (0, 1, 0, 3, 7),
        (0, 2, 0, 5, 9),
        (0, 0, 1, None, 2),
        (0, 1, 1, 4, 8),
        (0, 2, 1, 6, 10),
    ]
    for zi in (0, 1):
        units += [(rx, 1 - in_wrap[rx], zi, x1(rx, zi), x1(rx, zi) + 12) for rx in order]
        units += [(rx, in_wrap[rx], zi, x2(rx, zi), x2(rx, zi) + 12) for rx in order]
    turn = [0, 3, 1, 2, 4, 5, 6, 7, 8, 9, 10, 11, 12, 13, 14, 15, 16, 17]
    units = [units[i] for i in turn]

    send(0, kv_ref, block(0, 0, 0, c), core)
    send_y(0)

    row = lax.broadcasted_iota(jnp.int32, (owners * 8, BLK), 0)
    select = (row == target_ref[0:1, :]).astype(jnp.bfloat16)
    chosen_pages = jnp.dot(select, kv_ref[...], preferred_element_type=jnp.float32)
    pages_ref[...] = chosen_pages.astype(jnp.bfloat16).reshape(pages_ref.shape)
    pages[me.s] = pages_ref[me.s]

    quad_first = (me.y * 4 + x) * 4 * BLK
    place = 2 * z + c

    def step(source, first_key, causal):
        key = first_key + lax.broadcasted_iota(jnp.int32, (BLK, HD), 0)
        inside = (key >= low) & (key < high)
        bias = jnp.where(inside, 0.0, NEGATIVE).astype(jnp.bfloat16)
        keys = jnp.concatenate([source[:, 0:HD], bias], axis=1)
        scores = lax.dot_general(
            qa[...], keys, (((1,), (1,)), ((), ())), preferred_element_type=jnp.float32
        )
        if causal:
            row = lax.broadcasted_iota(jnp.int32, scores.shape, 0) & (BLK - 1)
            column = lax.broadcasted_iota(jnp.int32, scores.shape, 1)
            scores = jnp.where(column <= row, scores, NEGATIVE)
        old = m_ref[...]
        new = jnp.maximum(old, jnp.max(scores, axis=1, keepdims=True))
        offset = new * scale2
        weights = jnp.exp2(scores * scale2 - jnp.concatenate([offset, offset], axis=1))
        factor = jnp.exp2((old - new) * scale2)
        m_ref[...] = new
        l_ref[...] = l_ref[...] * factor + (weights[:, 0:HD] + weights[:, HD : 2 * HD])
        update = jnp.dot(
            weights.astype(jnp.bfloat16), source[:, HD : 2 * HD], preferred_element_type=jnp.float32
        )
        acc_ref[...] = acc_ref[...] * factor + update

    step(block(0, 0, 0, c), quad_first + place * BLK, True)

    def chosen(n, field):
        value = 0
        for i, unit in enumerate(units):
            value = value + (n == i).astype(jnp.int32) * unit[field]
        return value

    def serve(i):
        rx, k, zi, first, then = units[i]
        if first is None:
            opposite_arrived()
            send(then, mine(rx, k, zi), mine(rx, k, zi), core)
        else:
            forward(first, then, rx, k, zi)
        if (rx, k) == (0, 1):
            send_first(zi)
        if (rx, k) == (0, 2):
            send_second(zi, 1)
        if (rx, k) == (0, 0):
            send_y(1)

    def one_unit(n, carry):
        for i in range(1, len(units)):

            @pl.when(n == i - 1)
            def _():
                serve(i)

        rx, k, zi, then = (chosen(n, field) for field in (0, 1, 2, 4))

        @pl.when(n < 8)
        def _():
            for i in range(8):

                @pl.when(n * 8 + i > 0)
                def _():
                    to = peer(n * 8 + i)
                    remote(pages_ref.at[to[0]], pages.at[me.s], ss.at[35], rs.at[35], to).start()

        def one_core(j, inner):
            cc = wrap(c + j, 2)
            source = block(rx, k, zi, cc)
            where = 2 * wrap(z + zi, 2) + cc

            @pl.when(j == 1)
            def _():
                arrived(then, source)

            distance = rx + 4 * k
            first_key = quad_first - distance * 4 * BLK + where * BLK
            skip = ((distance == 0) & (where >= place)) | ((distance == 8) & (where < place))

            @pl.when(jnp.logical_not(skip) & (first_key >= 0))
            def _():
                step(source, first_key, False)

            return inner

        return lax.fori_loop(0, 2, one_core, carry)

    lax.fori_loop(0, len(units), one_unit, 0)

    for h in range(heads):
        rows = slice(h * BLK, (h + 1) * BLK)
        total = jnp.sum(l_ref[rows, :], axis=1, keepdims=True)
        out_ref[:, h * HD : (h + 1) * HD] = (acc_ref[rows, :] / total).astype(out_ref.dtype)

    others = pl.ds(0, owners - 1)
    exchange = remote(pages_ref.at[others], pages.at[others], ss.at[35], rs.at[35], core)
    exchange.wait_recv()
    cache_ref[...] = pages[...]
    exchange.wait_send()
    for index in [0] + list(range(2, 35)):
        remote(kv_ref, block(0, 0, 0, c), ss.at[index], rs.at[index], core).wait_send()
    finish()


def layer(hidden, gain, weight, firsts, queries, query_onehot, freq, target):
    heads = queries.shape[1] // HD
    rows, width = hidden.shape
    columns = weight.shape[1]
    owners = lax.axis_size("seq")
    away = pl.BlockSpec(memory_space=pl.ANY)
    vmem = pl.BlockSpec(memory_space=pltpu.VMEM)
    return pl.pallas_call(
        layer_kernel,
        out_shape=(
            jax.ShapeDtypeStruct(queries.shape, jnp.bfloat16),
            jax.ShapeDtypeStruct((owners, 8, columns), jnp.bfloat16),
        ),
        in_specs=[away, vmem, away, vmem, away, vmem, vmem, vmem],
        out_specs=(vmem, vmem),
        scratch_shapes=[
            pltpu.VMEM(hidden.shape, jnp.bfloat16),
            pltpu.VMEM(queries.shape, jnp.bfloat16),
            pltpu.VMEM((2, 2, 4, rows, width // 4), jnp.bfloat16),
            pltpu.VMEM((16, 2, width // 32, columns), jnp.bfloat16),
            pltpu.VMEM((12, 8, HD), jnp.int32),
            pltpu.VMEM((4 * rows, columns), jnp.float32),
            pltpu.VMEM((2, 2 * rows, columns), jnp.bfloat16),
            pltpu.VMEM((2, 4 * rows, HD), jnp.float32),
            pltpu.SemaphoreType.DMA((60,)),
            pltpu.SemaphoreType.DMA((60,)),
            pltpu.SemaphoreType.DMA((3,)),
            pltpu.VMEM((4, 3, 2, 2, BLK, 2 * HD), jnp.bfloat16),
            pltpu.VMEM((owners, 8, columns), jnp.bfloat16),
            pltpu.VMEM((owners, 8, columns), jnp.bfloat16),
            pltpu.VMEM((heads * BLK, 2 * HD), jnp.bfloat16),
            pltpu.VMEM((heads * BLK, HD), jnp.float32),
            pltpu.VMEM((heads * BLK, HD), jnp.float32),
            pltpu.VMEM((heads * BLK, HD), jnp.float32),
            pltpu.SemaphoreType.DMA((36,)),
            pltpu.SemaphoreType.DMA((36,)),
        ],
        compiler_params=pltpu.CompilerParams(
            collective_id=0, has_side_effects=True, vmem_limit_bytes=52 << 20
        ),
        cost_estimate=pl.CostEstimate(
            flops=10_000_000_000, bytes_accessed=4_000_000, transcendentals=17_000_000
        ),
    )(hidden, gain, weight, firsts, queries, query_onehot, freq, target)


def on_device(hidden, norm_gain, kv_weight, queries, segment_ids, page_owner):
    seq_count = lax.axis_size("seq")
    seq_place = lax.axis_index("seq")
    block_rows = segment_ids.shape[0]
    stream_rows = block_rows * seq_count
    token_index = seq_place * block_rows + jnp.arange(block_rows, dtype=jnp.int32)
    lanes = jnp.arange(HD, dtype=jnp.int32)
    member = segment_ids[:, None] == lanes[None, :]
    wanted = jnp.stack([lanes, lanes + 1])
    hit = segment_ids[None, None, :] == wanted[:, :, None]
    firsts = jnp.min(jnp.where(hit, token_index[None, None, :], stream_rows), axis=2)
    first_tile = jnp.pad(firsts, ((0, 6), (0, 0)))
    freq = 10000.0 ** (-jnp.arange(HD // 2, dtype=jnp.float32) * 2.0 / HD)
    freq_tile = jnp.broadcast_to(jnp.concatenate([freq, freq])[None, :], (8, HD))

    pages_block = page_owner.shape[0]
    page_rows = block_rows // pages_block
    capacity = max(2, 2 * pages_block // seq_count)
    owners = page_owner[:, 0]
    order = jnp.arange(pages_block, dtype=jnp.int32)
    earlier = (owners[None, :] == owners[:, None]) & (order[None, :] < order[:, None])
    rank = jnp.sum(earlier.astype(jnp.int32), axis=1)
    slot = (owners * capacity + rank) * page_rows
    target = (slot[:, None] + jnp.arange(page_rows, dtype=jnp.int32)[None, :]).reshape(1, block_rows)
    target_tile = jnp.broadcast_to(target, (8, block_rows))

    attended, arrived = layer(
        hidden,
        norm_gain[None, :],
        kv_weight,
        first_tile,
        queries,
        member.astype(jnp.bfloat16),
        freq_tile,
        target_tile,
    )
    kv_cache = arrived.reshape(1, seq_count, capacity, page_rows, arrived.shape[2])
    return (attended, kv_cache)


def solution(mesh):
    placed = (P(("seq", "fs"), None), P(), P("seq", "fs"), P("seq", "fs"), P("seq"), P("seq", None))
    return jax.shard_map(
        on_device,
        mesh=mesh,
        in_specs=placed,
        out_specs=(P("seq", "fs"), P("seq", None, None, None, "fs")),
        check_vma=False,
    )
```

```python
import functools

import jax
import jax.numpy as jnp
from jax import lax
from jax.experimental import pallas as pl
from jax.experimental.pallas import tpu as pltpu
from jax.sharding import PartitionSpec as P

HD = 128
SEGS = 4
EPSILON = 1e-05
NEGATIVE = -1e30
LOG2E = 1.4426950408889634
MESH = pl.DeviceIdType.MESH
BLK = 256


def wrap(value, count):
    return value - count * (value >= count).astype(jnp.int32)


class Place:
    def __init__(self):
        s = lax.axis_index("seq")
        self.s = s
        self.f = lax.axis_index("fs")
        self.c = lax.rem(s, 2)
        self.z = lax.rem(lax.div(s, 2), 2)
        self.x = lax.rem(lax.div(s, 4), 4)
        self.y = lax.div(s, 16)

    def at(self, dy=0, dx=0, other_z=False, other_core=False):
        y = wrap(self.y + dy, 4)
        x = wrap(self.x + dx, 4)
        z = 1 - self.z if other_z else self.z
        c = 1 - self.c if other_core else self.c
        return (((y * 4 + x) * 2 + z) * 2 + c, self.f)


def remote(src, dst, send, recv, target):
    return pltpu.make_async_remote_copy(
        src_ref=src, dst_ref=dst, send_sem=send, recv_sem=recv, device_id=target, device_id_type=MESH
    )


def project_part(
    me, hid_ref, gain_ref, w_ref, first_ref, qseg_ref, freq_ref,
    nb, wb, fb, acc, res, begins, buf, ss, rs, local, enter, idle
):
    c, z, x, y, f = me.c, me.z, me.x, me.y, me.f
    parity, group = lax.rem(f, 2), lax.div(f, 2)
    head = parity + 2 * c
    twin = lax.rem(f + 2, 4)
    mate = f + 1 - 2 * parity
    home = c == group
    chunks, rows, cols = nb.shape[2], nb.shape[3], nb.shape[4]

    def near(zz, cc, ff):
        return (((y * 4 + x) * 2 + zz) * 2 + cc, ff)

    core = near(z, 1 - c, f)
    ring_x = {k: me.at(dx=k) for k in (1, 2, 3)}
    ring_y = {k: me.at(dy=k) for k in (1, 2, 3)}
    enter([near(zz, cc, twin) for zz in (z, 1 - z) for cc in (c, 1 - c)] + [near(z, c, mate)])

    started = []

    def send(index, src, dst, target, recv=None):
        recv = index if recv is None else recv
        copy = remote(src, dst, ss.at[index], rs.at[recv], target)
        copy.start()
        started.append(copy)

    def arrived(index, dst):
        remote(dst, dst, ss.at[index], rs.at[index], core).wait_recv()

    quad = y * 4 + x
    shard = 2 * z + c
    rows_w = w_ref.shape[0]

    def piece(zz, cc):
        return wb.at[quad, zz, pl.ds(pl.multiple_of(cc * rows_w, rows_w), rows_w)]

    def seed_to_core():
        return remote(w_ref, piece(z, c), ss.at[0], rs.at[shard], core)

    @pl.when(home)
    def _():
        pltpu.make_async_copy(w_ref, piece(z, c), local).start()

    @pl.when(jnp.logical_not(home))
    def _():
        seed_to_core().start()

    send(1, w_ref, piece(z, c), near(z, group, twin), shard)
    send(2, w_ref, piece(z, c), near(1 - z, group, f), shard)
    send(3, w_ref, piece(z, c), near(1 - z, group, twin), shard)
    send(4, first_ref, fb.at[0], core)
    send(5, first_ref, fb.at[1], near(1 - z, c, f))
    send(6, first_ref, fb.at[2], near(1 - z, 1 - c, f))

    total = jnp.zeros((rows, 1), jnp.float32)
    for i in range(chunks):
        wide = hid_ref[:, i * cols : (i + 1) * cols].astype(jnp.float32)
        total = total + jnp.sum(wide * wide, axis=1, keepdims=True)
    factor = lax.rsqrt(total / (chunks * cols) + EPSILON)
    for i in range(chunks):
        wide = hid_ref[:, i * cols : (i + 1) * cols].astype(jnp.float32)
        gain = gain_ref[:, i * cols : (i + 1) * cols].astype(jnp.float32)
        nb[c, parity, i] = (wide * factor * gain).astype(jnp.bfloat16)
        send(13 + i, nb.at[c, parity, i], nb.at[c, parity, i], near(z, c, mate))
        send(17 + i, nb.at[c, parity, i], nb.at[c, parity, i], core)

    def seed_arrived(zz):
        for cc in (0, 1):
            own = jnp.logical_and(home, shard == 2 * zz + cc)

            @pl.when(own)
            def _():
                pltpu.make_async_copy(w_ref, piece(zz, cc), local).wait()

            @pl.when(jnp.logical_not(own))
            def _():
                arrived(2 * zz + cc, piece(zz, cc))

    half = lambda yy, xx, hh: wb.at[yy * 4 + xx, hh]
    back = lambda v, k: lax.rem(v + 4 - k, 4)
    order = (1, 3, 2)
    seed_arrived(0)
    for k in (1, 3):
        send(24 + k, half(y, x, 0), half(y, x, 0), ring_x[k])
    seed_arrived(1)
    for k in (1, 3):
        send(27 + k, half(y, x, 1), half(y, x, 1), ring_y[k])

    a2 = lambda k, j: 31 + (k - 1) * 4 + j
    b2 = lambda k, j: 43 + (k - 1) * 4 + j

    cut = wb.shape[2] // 2
    lower = lambda yy, xx, hh: wb.at[yy * 4 + xx, hh, 0:cut]
    upper = lambda yy, xx, hh: wb.at[yy * 4 + xx, hh, cut : 2 * cut]

    def spread(j):
        ya, xa = y, back(x, j)
        yb, xb = back(y, j), x
        for k in (1, 3):
            send(a2(k, j), half(ya, xa, 0), half(ya, xa, 0), ring_y[k])
            send(b2(k, j), half(yb, xb, 1), half(yb, xb, 1), ring_x[k])

    def pass_on(firsts, halves, near_by, ring):
        arrived(firsts[0], half(*near_by(1)))
        send(halves[0], lower(*near_by(1)), lower(*near_by(1)), ring[1])
        arrived(firsts[1], half(*near_by(3)))
        send(halves[1], upper(*near_by(3)), upper(*near_by(3)), ring[3])

    def far_arrived(halves, at):
        arrived(halves[0], lower(*at))
        arrived(halves[1], upper(*at))

    def relay_first():
        pass_on((25, 27), (26, 60), lambda k: (y, back(x, k), 0), ring_x)
        pass_on((28, 30), (29, 61), lambda k: (back(y, k), x, 1), ring_y)

    def relay(j):
        pass_on(
            (a2(1, j), a2(3, j)), (a2(2, j), 62 + j), lambda k: (back(y, k), back(x, j), 0), ring_y
        )
        pass_on(
            (b2(1, j), b2(3, j)), (b2(2, j), 66 + j), lambda k: (back(y, j), back(x, k), 1), ring_x
        )

    def forward(i):
        arrived(13 + i, nb.at[c, 1 - parity, i])
        send(21 + i, nb.at[c, 1 - parity, i], nb.at[c, 1 - parity, i], core)

    spread(0)
    idle()
    for i in range(3):
        arrived(4 + i, fb.at[i])
    fb[3] = jnp.minimum(jnp.minimum(first_ref[...], fb[0]), jnp.minimum(fb[1], fb[2]))
    for k in order:
        send(6 + k, fb.at[3], fb.at[3 + k], ring_x[k])
    forward(0)
    relay_first()
    spread(1)
    spread(3)
    far_arrived((26, 60), (y, back(x, 2), 0))
    far_arrived((29, 61), (back(y, 2), x, 1))
    spread(2)
    forward(1)
    relay(0)
    for k in order:
        arrived(6 + k, fb.at[3 + k])
    fb[7] = jnp.minimum(jnp.minimum(fb[3], fb[4]), jnp.minimum(fb[5], fb[6]))
    for k in order:
        send(9 + k, fb.at[7], fb.at[7 + k], ring_y[k])
    relay(1)
    forward(2)
    relay(3)
    relay(2)
    forward(3)
    for k in order:
        arrived(9 + k, fb.at[7 + k])
    fb[11] = jnp.minimum(jnp.minimum(fb[7], fb[8]), jnp.minimum(fb[9], fb[10]))
    first_row = fb[11][0:1, :].astype(jnp.float32)
    begin = jnp.sum(qseg_ref[...].astype(jnp.float32) * first_row, axis=1, keepdims=True)
    begins[c] = jnp.broadcast_to(begin, begins.shape[1:])
    send(59, begins.at[c], begins.at[c], core)
    for i in range(chunks):
        arrived(17 + i, nb.at[1 - c, parity, i])
        arrived(21 + i, nb.at[1 - c, 1 - parity, i])

    acc[...] = jnp.zeros_like(acc)

    def multiply(yy, xx, hh):
        columns = pl.ds(pl.multiple_of(xx * 512 + hh * 256, 256), 256)
        lhs = nb[:, :, yy, :, columns].reshape(4 * rows, 256)
        acc[...] += jnp.dot(lhs, wb[yy * 4 + xx, hh], preferred_element_type=jnp.float32)

    multiply(y, x, 0)
    multiply(y, x, 1)
    for j in order:
        multiply(y, back(x, j), 0)
        multiply(back(y, j), x, 1)
    for k in (1, 3, 2):
        for j in (0, 1, 3, 2):
            ya, xa = back(y, k), back(x, j)
            yb, xb = back(y, j), back(x, k)
            if k == 2:
                far_arrived((a2(2, j), 62 + j), (ya, xa, 0))
            multiply(ya, xa, 0)
            if k == 2:
                far_arrived((b2(2, j), 66 + j), (yb, xb, 1))
            multiply(yb, xb, 1)

    arrived(59, begins.at[1 - c])
    pair = 2 * rows
    rows_g = pl.ds(pl.multiple_of(group * pair, pair), pair)
    lane = lax.broadcasted_iota(jnp.int32, (pair, HD), 1)
    for cc in (0, 1):
        first_token = (me.s - c + cc) * BLK + group * pair
        token = first_token + lax.broadcasted_iota(jnp.int32, (pair, HD), 0)
        angle = (token.astype(jnp.float32) - begins[cc, rows_g, :]) * freq_ref[0:1, :]
        sine = jnp.sin(angle)
        sine = jnp.where(lane < HD // 2, -sine, sine)
        keys = acc[cc * pair : (cc + 1) * pair, 0:HD]
        swapped = jnp.concatenate([keys[:, HD // 2 :], keys[:, : HD // 2]], axis=1)
        turned = keys * jnp.cos(angle) + swapped * sine
        res[cc, :, 0:HD] = turned.astype(jnp.bfloat16)
        res[cc, :, HD:] = acc[cc * pair : (cc + 1) * pair, HD:].astype(jnp.bfloat16)

    def part(zz, cc, g):
        return buf.at[0, 0, zz, cc, pl.ds(pl.multiple_of(g * pair, pair), pair)]

    def result_to(zz, cc, ff, index, recv):
        return remote(
            res.at[cc], part(z, cc, group), ss.at[index], rs.at[recv + group], near(zz, cc, ff)
        )

    @pl.when(home)
    def _():
        result_to(z, 1 - c, f, 55, 55).start()
        result_to(1 - z, 0, f, 57, 57).start()
        result_to(1 - z, 1, f, 58, 57).start()
        buf[0, 0, z, c, rows_g, :] = res[c]

    @pl.when(jnp.logical_not(home))
    def _():
        result_to(z, 0, twin, 55, 55).start()
        result_to(z, 1, twin, 56, 55).start()
        result_to(1 - z, 0, twin, 57, 57).start()
        result_to(1 - z, 1, twin, 58, 57).start()

    for g in (0, 1):

        @pl.when(jnp.logical_not(jnp.logical_and(home, group == g)))
        def _():
            arrived(55 + g, part(z, c, g))

    def opposite_arrived():
        for g in (0, 1):
            arrived(57 + g, part(1 - z, c, g))

    def finish():
        for copy in started:
            copy.wait_send()

        @pl.when(home)
        def _():
            result_to(z, 1 - c, f, 55, 55).wait_send()

        @pl.when(jnp.logical_not(home))
        def _():
            seed_to_core().wait_send()
            result_to(z, 0, twin, 55, 55).wait_send()
            result_to(z, 1, twin, 56, 55).wait_send()

        result_to(1 - z, 0, f, 57, 57).wait_send()
        result_to(1 - z, 1, f, 58, 57).wait_send()

    return finish, opposite_arrived


def layer_kernel(
    hid_hbm, gain_ref, w_ref, first_ref, q_hbm, qseg_ref, freq_ref, target_ref,
    out_ref, cache_ref,
    hid, q, nb, wb, fb, proj, res, begins, ass, ars, local,
    buf, pages, pages_ref, qa, m_ref, l_ref, acc_ref, ss, rs
):
    me = Place()
    c, z, x = me.c, me.z, me.x
    heads = q.shape[1] // HD
    owners = pages_ref.shape[0]
    scale2 = (HD ** (-0.5)) * LOG2E
    core = me.at(other_core=True)
    load_hidden = pltpu.make_async_copy(hid_hbm, hid, local.at[0])
    load_queries = pltpu.make_async_copy(q_hbm, q, local.at[1])
    load_hidden.start()
    load_queries.start()

    def peer(distance):
        return (wrap(me.s + distance, owners), me.f)

    def enter(others):
        barrier = pltpu.get_barrier_semaphore()

        def greet(distance, carry):
            pl.semaphore_signal(barrier, inc=1, device_id=peer(distance), device_id_type=MESH)
            return carry

        for other in others:
            pl.semaphore_signal(barrier, inc=1, device_id=other, device_id_type=MESH)
        lax.fori_loop(1, owners, greet, 0)
        pl.semaphore_wait(barrier, owners - 1 + len(others))
        load_hidden.wait()

    def idle():
        load_queries.wait()
        for h in range(heads):
            qa[h * BLK : (h + 1) * BLK, 0:HD] = q[:, h * HD : (h + 1) * HD]
            qa[h * BLK : (h + 1) * BLK, HD : 2 * HD] = qseg_ref[...]
        m_ref[...] = jnp.full_like(m_ref, NEGATIVE)
        l_ref[...] = jnp.zeros_like(l_ref)
        acc_ref[...] = jnp.zeros_like(acc_ref)

    finish, opposite_arrived = project_part(
        me, hid, gain_ref, w_ref, first_ref, qseg_ref, freq_ref,
        nb, wb, fb, proj, res, begins, buf, ass, ars, local.at[2], enter, idle,
    )
    bounds = fb[11]
    low = bounds[0:1, :]
    high = bounds[1:2, :]
    kv_ref = buf.at[0, 0, z, c]

    def send(index, src, dst, target):
        remote(src, dst, ss.at[index], rs.at[index], target).start()

    def arrived(index, dst):
        remote(dst, dst, ss.at[index], rs.at[index], core).wait_recv()

    def block(rx, k, zi, cc):
        return buf.at[rx, k, wrap(z + zi, 2), cc]

    def mine(rx, k, zi):
        return block(rx, k, zi, c)

    order = (1, 3, 2)
    out_wrap = {rx: (x + rx >= 4).astype(jnp.int32) for rx in order}
    in_wrap = {rx: (x < rx).astype(jnp.int32) for rx in order}
    x1 = lambda rx, zi: 11 + 2 * (rx - 1) + zi
    x2 = lambda rx, zi: 17 + 2 * (rx - 1) + zi

    def second(rx, zi):
        w = out_wrap[rx]
        return remote(
            mine(0, 2 * w, zi), mine(rx, w, zi), ss.at[x2(rx, zi)], rs.at[x2(rx, zi)], me.at(dx=rx)
        )

    def send_second(zi, wraps):
        for rx in order:

            @pl.when(out_wrap[rx] == wraps)
            def _():
                second(rx, zi).start()

    def send_y(zi):
        send(3 + zi, mine(0, 0, zi), mine(0, 1, zi), me.at(dy=1))
        send(5 + zi, mine(0, 0, zi), mine(0, 2, zi), me.at(dy=2))
        send_second(zi, 0)

    def send_first(zi):
        for rx in order:
            send(x1(rx, zi), mine(0, 1, zi), mine(rx, 1 - out_wrap[rx], zi), me.at(dx=rx))

    def forward(first, then, rx, k, zi):
        arrived(first, mine(rx, k, zi))
        send(then, mine(rx, k, zi), mine(rx, k, zi), core)

    units = [
        (0, 0, 0, None, 0),
        (0, 1, 0, 3, 7),
        (0, 2, 0, 5, 9),
        (0, 0, 1, None, 2),
        (0, 1, 1, 4, 8),
        (0, 2, 1, 6, 10),
    ]
    for zi in (0, 1):
        units += [(rx, 1 - in_wrap[rx], zi, x1(rx, zi), x1(rx, zi) + 12) for rx in order]
        units += [(rx, in_wrap[rx], zi, x2(rx, zi), x2(rx, zi) + 12) for rx in order]
    turn = [0, 3, 1, 2, 4, 5, 6, 7, 8, 9, 10, 11, 12, 13, 14, 15, 16, 17]
    units = [units[i] for i in turn]

    send(0, kv_ref, block(0, 0, 0, c), core)
    send_y(0)

    row = lax.broadcasted_iota(jnp.int32, (owners * 8, BLK), 0)
    select = (row == target_ref[0:1, :]).astype(jnp.bfloat16)
    chosen_pages = jnp.dot(select, kv_ref[...], preferred_element_type=jnp.float32)
    pages_ref[...] = chosen_pages.astype(jnp.bfloat16).reshape(pages_ref.shape)
    pages[me.s] = pages_ref[me.s]

    quad_first = (me.y * 4 + x) * 4 * BLK
    place = 2 * z + c

    def step(source, first_key, causal):
        key = first_key + lax.broadcasted_iota(jnp.int32, (BLK, HD), 0)
        inside = (key >= low) & (key < high)
        bias = jnp.where(inside, 0.0, NEGATIVE).astype(jnp.bfloat16)
        keys = jnp.concatenate([source[:, 0:HD], bias], axis=1)
        scores = lax.dot_general(
            qa[...], keys, (((1,), (1,)), ((), ())), preferred_element_type=jnp.float32
        )
        if causal:
            row = lax.broadcasted_iota(jnp.int32, scores.shape, 0) & (BLK - 1)
            column = lax.broadcasted_iota(jnp.int32, scores.shape, 1)
            scores = jnp.where(column <= row, scores, NEGATIVE)
        old = m_ref[...]
        new = jnp.maximum(old, jnp.max(scores, axis=1, keepdims=True))
        offset = new * scale2
        weights = jnp.exp2(scores * scale2 - jnp.concatenate([offset, offset], axis=1))
        factor = jnp.exp2((old - new) * scale2)
        m_ref[...] = new
        l_ref[...] = l_ref[...] * factor + (weights[:, 0:HD] + weights[:, HD : 2 * HD])
        update = jnp.dot(
            weights.astype(jnp.bfloat16), source[:, HD : 2 * HD], preferred_element_type=jnp.float32
        )
        acc_ref[...] = acc_ref[...] * factor + update

    step(block(0, 0, 0, c), quad_first + place * BLK, True)

    def chosen(n, field):
        value = 0
        for i, unit in enumerate(units):
            value = value + (n == i).astype(jnp.int32) * unit[field]
        return value

    def serve(i):
        rx, k, zi, first, then = units[i]
        if first is None:
            opposite_arrived()
            send(then, mine(rx, k, zi), mine(rx, k, zi), core)
        else:
            forward(first, then, rx, k, zi)
        if (rx, k) == (0, 1):
            send_first(zi)
        if (rx, k) == (0, 2):
            send_second(zi, 1)
        if (rx, k) == (0, 0):
            send_y(1)

    def one_unit(n, carry):
        for i in range(1, len(units)):

            @pl.when(n == i - 1)
            def _():
                serve(i)

        rx, k, zi, then = (chosen(n, field) for field in (0, 1, 2, 4))

        @pl.when(n < 8)
        def _():
            for i in range(8):

                @pl.when(n * 8 + i > 0)
                def _():
                    to = peer(n * 8 + i)
                    remote(pages_ref.at[to[0]], pages.at[me.s], ss.at[35], rs.at[35], to).start()

        def one_core(j, inner):
            cc = wrap(c + j, 2)
            source = block(rx, k, zi, cc)
            where = 2 * wrap(z + zi, 2) + cc

            @pl.when(j == 1)
            def _():
                arrived(then, source)

            distance = rx + 4 * k
            first_key = quad_first - distance * 4 * BLK + where * BLK
            skip = ((distance == 0) & (where >= place)) | ((distance == 8) & (where < place))

            @pl.when(jnp.logical_not(skip) & (first_key >= 0))
            def _():
                step(source, first_key, False)

            return inner

        return lax.fori_loop(0, 2, one_core, carry)

    lax.fori_loop(0, len(units), one_unit, 0)

    for h in range(heads):
        rows = slice(h * BLK, (h + 1) * BLK)
        total = jnp.sum(l_ref[rows, :], axis=1, keepdims=True)
        out_ref[:, h * HD : (h + 1) * HD] = (acc_ref[rows, :] / total).astype(out_ref.dtype)

    others = pl.ds(0, owners - 1)
    exchange = remote(pages_ref.at[others], pages.at[others], ss.at[35], rs.at[35], core)
    exchange.wait_recv()
    cache_ref[...] = pages[...]
    exchange.wait_send()
    for index in [0] + list(range(2, 35)):
        remote(kv_ref, block(0, 0, 0, c), ss.at[index], rs.at[index], core).wait_send()
    finish()


def layer(hidden, gain, weight, firsts, queries, query_onehot, freq, target):
    heads = queries.shape[1] // HD
    rows, width = hidden.shape
    columns = weight.shape[1]
    owners = lax.axis_size("seq")
    away = pl.BlockSpec(memory_space=pl.ANY)
    vmem = pl.BlockSpec(memory_space=pltpu.VMEM)
    return pl.pallas_call(
        layer_kernel,
        out_shape=(
            jax.ShapeDtypeStruct(queries.shape, jnp.bfloat16),
            jax.ShapeDtypeStruct((owners, 8, columns), jnp.bfloat16),
        ),
        in_specs=[away, vmem, away, vmem, away, vmem, vmem, vmem],
        out_specs=(vmem, vmem),
        scratch_shapes=[
            pltpu.VMEM(hidden.shape, jnp.bfloat16),
            pltpu.VMEM(queries.shape, jnp.bfloat16),
            pltpu.VMEM((2, 2, 4, rows, width // 4), jnp.bfloat16),
            pltpu.VMEM((16, 2, width // 32, columns), jnp.bfloat16),
            pltpu.VMEM((12, 8, HD), jnp.int32),
            pltpu.VMEM((4 * rows, columns), jnp.float32),
            pltpu.VMEM((2, 2 * rows, columns), jnp.bfloat16),
            pltpu.VMEM((2, 4 * rows, HD), jnp.float32),
            pltpu.SemaphoreType.DMA((70,)),
            pltpu.SemaphoreType.DMA((70,)),
            pltpu.SemaphoreType.DMA((3,)),
            pltpu.VMEM((4, 3, 2, 2, BLK, 2 * HD), jnp.bfloat16),
            pltpu.VMEM((owners, 8, columns), jnp.bfloat16),
            pltpu.VMEM((owners, 8, columns), jnp.bfloat16),
            pltpu.VMEM((heads * BLK, 2 * HD), jnp.bfloat16),
            pltpu.VMEM((heads * BLK, HD), jnp.float32),
            pltpu.VMEM((heads * BLK, HD), jnp.float32),
            pltpu.VMEM((heads * BLK, HD), jnp.float32),
            pltpu.SemaphoreType.DMA((36,)),
            pltpu.SemaphoreType.DMA((36,)),
        ],
        compiler_params=pltpu.CompilerParams(
            collective_id=0, has_side_effects=True, vmem_limit_bytes=52 << 20
        ),
        cost_estimate=pl.CostEstimate(
            flops=10_000_000_000, bytes_accessed=4_000_000, transcendentals=17_000_000
        ),
    )(hidden, gain, weight, firsts, queries, query_onehot, freq, target)


def on_device(hidden, norm_gain, kv_weight, queries, segment_ids, page_owner):
    seq_count = lax.axis_size("seq")
    seq_place = lax.axis_index("seq")
    block_rows = segment_ids.shape[0]
    stream_rows = block_rows * seq_count
    token_index = seq_place * block_rows + jnp.arange(block_rows, dtype=jnp.int32)
    lanes = jnp.arange(HD, dtype=jnp.int32)
    member = segment_ids[:, None] == lanes[None, :]
    wanted = jnp.stack([lanes, lanes + 1])
    hit = segment_ids[None, None, :] == wanted[:, :, None]
    firsts = jnp.min(jnp.where(hit, token_index[None, None, :], stream_rows), axis=2)
    first_tile = jnp.pad(firsts, ((0, 6), (0, 0)))
    freq = 10000.0 ** (-jnp.arange(HD // 2, dtype=jnp.float32) * 2.0 / HD)
    freq_tile = jnp.broadcast_to(jnp.concatenate([freq, freq])[None, :], (8, HD))

    pages_block = page_owner.shape[0]
    page_rows = block_rows // pages_block
    capacity = max(2, 2 * pages_block // seq_count)
    owners = page_owner[:, 0]
    order = jnp.arange(pages_block, dtype=jnp.int32)
    earlier = (owners[None, :] == owners[:, None]) & (order[None, :] < order[:, None])
    rank = jnp.sum(earlier.astype(jnp.int32), axis=1)
    slot = (owners * capacity + rank) * page_rows
    target = (slot[:, None] + jnp.arange(page_rows, dtype=jnp.int32)[None, :]).reshape(1, block_rows)
    target_tile = jnp.broadcast_to(target, (8, block_rows))

    attended, arrived = layer(
        hidden,
        norm_gain[None, :],
        kv_weight,
        first_tile,
        queries,
        member.astype(jnp.bfloat16),
        freq_tile,
        target_tile,
    )
    kv_cache = arrived.reshape(1, seq_count, capacity, page_rows, arrived.shape[2])
    return (attended, kv_cache)


def solution(mesh):
    placed = (P(("seq", "fs"), None), P(), P("seq", "fs"), P("seq", "fs"), P("seq"), P("seq", None))
    return jax.shard_map(
        on_device,
        mesh=mesh,
        in_specs=placed,
        out_specs=(P("seq", "fs"), P("seq", None, None, None, "fs")),
        check_vma=False,
    )
```

```python
import functools

import jax
import jax.numpy as jnp
from jax import lax
from jax.experimental import pallas as pl
from jax.experimental.pallas import tpu as pltpu
from jax.sharding import PartitionSpec as P

HD = 128
SEGS = 4
EPSILON = 1e-05
NEGATIVE = -1e30
LOG2E = 1.4426950408889634
MESH = pl.DeviceIdType.MESH
BLK = 256


def wrap(value, count):
    return value - count * (value >= count).astype(jnp.int32)


class Place:
    def __init__(self):
        s = lax.axis_index("seq")
        self.s = s
        self.f = lax.axis_index("fs")
        self.c = lax.rem(s, 2)
        self.z = lax.rem(lax.div(s, 2), 2)
        self.x = lax.rem(lax.div(s, 4), 4)
        self.y = lax.div(s, 16)

    def at(self, dy=0, dx=0, other_z=False, other_core=False):
        y = wrap(self.y + dy, 4)
        x = wrap(self.x + dx, 4)
        z = 1 - self.z if other_z else self.z
        c = 1 - self.c if other_core else self.c
        return (((y * 4 + x) * 2 + z) * 2 + c, self.f)


def remote(src, dst, send, recv, target):
    return pltpu.make_async_remote_copy(
        src_ref=src, dst_ref=dst, send_sem=send, recv_sem=recv, device_id=target, device_id_type=MESH
    )


def project_part(
    me, hid_ref, gain_ref, w_ref, first_ref, qseg_ref, freq_ref,
    nb, wb, fb, acc, res, begins, buf, ss, rs, local, enter, idle
):
    c, z, x, y, f = me.c, me.z, me.x, me.y, me.f
    parity, group = lax.rem(f, 2), lax.div(f, 2)
    head = parity + 2 * c
    twin = lax.rem(f + 2, 4)
    mate = f + 1 - 2 * parity
    home = c == group
    chunks, rows, cols = nb.shape[2], nb.shape[3], nb.shape[4]

    def near(zz, cc, ff):
        return (((y * 4 + x) * 2 + zz) * 2 + cc, ff)

    core = near(z, 1 - c, f)
    ring_x = {k: me.at(dx=k) for k in (1, 2, 3)}
    ring_y = {k: me.at(dy=k) for k in (1, 2, 3)}
    enter([near(zz, cc, twin) for zz in (z, 1 - z) for cc in (c, 1 - c)] + [near(z, c, mate)])

    started = []

    def send(index, src, dst, target, recv=None):
        recv = index if recv is None else recv
        copy = remote(src, dst, ss.at[index], rs.at[recv], target)
        copy.start()
        started.append(copy)

    def arrived(index, dst):
        remote(dst, dst, ss.at[index], rs.at[index], core).wait_recv()

    quad = y * 4 + x
    shard = 2 * z + c
    rows_w = w_ref.shape[0]

    def piece(zz, cc):
        return wb.at[quad, zz, pl.ds(pl.multiple_of(cc * rows_w, rows_w), rows_w)]

    def seed_to_core():
        return remote(w_ref, piece(z, c), ss.at[0], rs.at[shard], core)

    @pl.when(home)
    def _():
        pltpu.make_async_copy(w_ref, piece(z, c), local).start()

    @pl.when(jnp.logical_not(home))
    def _():
        seed_to_core().start()

    send(1, w_ref, piece(z, c), near(z, group, twin), shard)
    send(2, w_ref, piece(z, c), near(1 - z, group, f), shard)
    send(3, w_ref, piece(z, c), near(1 - z, group, twin), shard)
    send(4, first_ref, fb.at[0], core)
    send(5, first_ref, fb.at[1], near(1 - z, c, f))
    send(6, first_ref, fb.at[2], near(1 - z, 1 - c, f))

    total = jnp.zeros((rows, 1), jnp.float32)
    for i in range(chunks):
        wide = hid_ref[:, i * cols : (i + 1) * cols].astype(jnp.float32)
        total = total + jnp.sum(wide * wide, axis=1, keepdims=True)
    factor = lax.rsqrt(total / (chunks * cols) + EPSILON)
    for i in range(chunks):
        wide = hid_ref[:, i * cols : (i + 1) * cols].astype(jnp.float32)
        gain = gain_ref[:, i * cols : (i + 1) * cols].astype(jnp.float32)
        nb[c, parity, i] = (wide * factor * gain).astype(jnp.bfloat16)
        send(13 + i, nb.at[c, parity, i], nb.at[c, parity, i], near(z, c, mate))
        send(17 + i, nb.at[c, parity, i], nb.at[c, parity, i], core)

    def seed_arrived(zz):
        for cc in (0, 1):
            own = jnp.logical_and(home, shard == 2 * zz + cc)

            @pl.when(own)
            def _():
                pltpu.make_async_copy(w_ref, piece(zz, cc), local).wait()

            @pl.when(jnp.logical_not(own))
            def _():
                arrived(2 * zz + cc, piece(zz, cc))

    half = lambda yy, xx, hh: wb.at[yy * 4 + xx, hh]
    back = lambda v, k: lax.rem(v + 4 - k, 4)
    order = (1, 3, 2)
    seed_arrived(0)
    for k in (1, 3):
        send(24 + k, half(y, x, 0), half(y, x, 0), ring_x[k])
    seed_arrived(1)
    for k in (1, 3):
        send(27 + k, half(y, x, 1), half(y, x, 1), ring_y[k])

    a2 = lambda k, j: 31 + (k - 1) * 4 + j
    b2 = lambda k, j: 43 + (k - 1) * 4 + j

    cut = wb.shape[2] // 2
    lower = lambda yy, xx, hh: wb.at[yy * 4 + xx, hh, 0:cut]
    upper = lambda yy, xx, hh: wb.at[yy * 4 + xx, hh, cut : 2 * cut]

    def spread(j):
        ya, xa = y, back(x, j)
        yb, xb = back(y, j), x
        for k in (1, 3):
            send(a2(k, j), half(ya, xa, 0), half(ya, xa, 0), ring_y[k])
            send(b2(k, j), half(yb, xb, 1), half(yb, xb, 1), ring_x[k])

    def pass_on(firsts, halves, near_by, ring):
        arrived(firsts[0], half(*near_by(1)))
        send(halves[0], lower(*near_by(1)), lower(*near_by(1)), ring[1])
        arrived(firsts[1], half(*near_by(3)))
        send(halves[1], upper(*near_by(3)), upper(*near_by(3)), ring[3])

    def far_arrived(halves, at):
        arrived(halves[0], lower(*at))
        arrived(halves[1], upper(*at))

    def relay_first():
        pass_on((25, 27), (26, 60), lambda k: (y, back(x, k), 0), ring_x)
        pass_on((28, 30), (29, 61), lambda k: (back(y, k), x, 1), ring_y)

    def relay(j):
        pass_on(
            (a2(1, j), a2(3, j)), (a2(2, j), 62 + j), lambda k: (back(y, k), back(x, j), 0), ring_y
        )
        pass_on(
            (b2(1, j), b2(3, j)), (b2(2, j), 66 + j), lambda k: (back(y, j), back(x, k), 1), ring_x
        )

    def forward(i):
        arrived(13 + i, nb.at[c, 1 - parity, i])
        send(21 + i, nb.at[c, 1 - parity, i], nb.at[c, 1 - parity, i], core)

    spread(0)
    idle()
    for i in range(3):
        arrived(4 + i, fb.at[i])
    fb[3] = jnp.minimum(jnp.minimum(first_ref[...], fb[0]), jnp.minimum(fb[1], fb[2]))
    for k in order:
        send(6 + k, fb.at[3], fb.at[3 + k], ring_x[k])
    forward(0)
    relay_first()
    spread(1)
    spread(3)
    far_arrived((26, 60), (y, back(x, 2), 0))
    far_arrived((29, 61), (back(y, 2), x, 1))
    spread(2)
    forward(1)
    relay(0)
    for k in order:
        arrived(6 + k, fb.at[3 + k])
    fb[7] = jnp.minimum(jnp.minimum(fb[3], fb[4]), jnp.minimum(fb[5], fb[6]))
    for k in order:
        send(9 + k, fb.at[7], fb.at[7 + k], ring_y[k])
    relay(1)
    forward(2)
    relay(3)
    relay(2)
    forward(3)
    for k in order:
        arrived(9 + k, fb.at[7 + k])
    fb[11] = jnp.minimum(jnp.minimum(fb[7], fb[8]), jnp.minimum(fb[9], fb[10]))
    first_row = fb[11][0:1, :].astype(jnp.float32)
    begin = jnp.sum(qseg_ref[...].astype(jnp.float32) * first_row, axis=1, keepdims=True)
    begins[c] = jnp.broadcast_to(begin, begins.shape[1:])
    send(59, begins.at[c], begins.at[c], core)
    for i in range(chunks):
        arrived(17 + i, nb.at[1 - c, parity, i])
        arrived(21 + i, nb.at[1 - c, 1 - parity, i])

    acc[...] = jnp.zeros_like(acc)

    def multiply(yy, xx, hh):
        columns = pl.ds(pl.multiple_of(xx * 512 + hh * 256, 256), 256)
        lhs = nb[:, :, yy, :, columns].reshape(4 * rows, 256)
        acc[...] += jnp.dot(lhs, wb[yy * 4 + xx, hh], preferred_element_type=jnp.float32)

    multiply(y, x, 0)
    multiply(y, x, 1)
    for j in order:
        multiply(y, back(x, j), 0)
        multiply(back(y, j), x, 1)
    for k in (1, 3, 2):
        for j in (0, 1, 3, 2):
            ya, xa = back(y, k), back(x, j)
            yb, xb = back(y, j), back(x, k)
            if k == 2:
                far_arrived((a2(2, j), 62 + j), (ya, xa, 0))
            multiply(ya, xa, 0)
            if k == 2:
                far_arrived((b2(2, j), 66 + j), (yb, xb, 1))
            multiply(yb, xb, 1)

    arrived(59, begins.at[1 - c])
    pair = 2 * rows
    rows_g = pl.ds(pl.multiple_of(group * pair, pair), pair)
    lane = lax.broadcasted_iota(jnp.int32, (pair, HD), 1)
    for cc in (0, 1):
        first_token = (me.s - c + cc) * BLK + group * pair
        token = first_token + lax.broadcasted_iota(jnp.int32, (pair, HD), 0)
        angle = (token.astype(jnp.float32) - begins[cc, rows_g, :]) * freq_ref[0:1, :]
        sine = jnp.sin(angle)
        sine = jnp.where(lane < HD // 2, -sine, sine)
        keys = acc[cc * pair : (cc + 1) * pair, 0:HD]
        swapped = jnp.concatenate([keys[:, HD // 2 :], keys[:, : HD // 2]], axis=1)
        turned = keys * jnp.cos(angle) + swapped * sine
        res[cc, :, 0:HD] = turned.astype(jnp.bfloat16)
        res[cc, :, HD:] = acc[cc * pair : (cc + 1) * pair, HD:].astype(jnp.bfloat16)

    def part(zz, cc, g):
        return buf.at[0, 0, zz, cc, pl.ds(pl.multiple_of(g * pair, pair), pair)]

    def result_to(zz, cc, ff, index, recv):
        return remote(
            res.at[cc], part(z, cc, group), ss.at[index], rs.at[recv + group], near(zz, cc, ff)
        )

    @pl.when(home)
    def _():
        result_to(z, 1 - c, f, 55, 55).start()
        result_to(1 - z, 0, f, 57, 57).start()
        result_to(1 - z, 1, f, 58, 57).start()
        buf[0, 0, z, c, rows_g, :] = res[c]

    @pl.when(jnp.logical_not(home))
    def _():
        result_to(z, 0, twin, 55, 55).start()
        result_to(z, 1, twin, 56, 55).start()
        result_to(1 - z, 0, twin, 57, 57).start()
        result_to(1 - z, 1, twin, 58, 57).start()

    for g in (0, 1):

        @pl.when(jnp.logical_not(jnp.logical_and(home, group == g)))
        def _():
            arrived(55 + g, part(z, c, g))

    def opposite_arrived():
        for g in (0, 1):
            arrived(57 + g, part(1 - z, c, g))

    def finish():
        for copy in started:
            copy.wait_send()

        @pl.when(home)
        def _():
            result_to(z, 1 - c, f, 55, 55).wait_send()

        @pl.when(jnp.logical_not(home))
        def _():
            seed_to_core().wait_send()
            result_to(z, 0, twin, 55, 55).wait_send()
            result_to(z, 1, twin, 56, 55).wait_send()

        result_to(1 - z, 0, f, 57, 57).wait_send()
        result_to(1 - z, 1, f, 58, 57).wait_send()

    return finish, opposite_arrived


def layer_kernel(
    hid_hbm, gain_ref, w_ref, first_ref, q_hbm, qseg_ref, freq_ref, target_ref,
    out_ref, cache_ref,
    hid, q, nb, wb, fb, proj, res, begins, ass, ars, local,
    buf, pages, pages_ref, qa, m_ref, l_ref, acc_ref, ss, rs
):
    me = Place()
    c, z, x = me.c, me.z, me.x
    heads = q.shape[1] // HD
    owners = pages_ref.shape[0]
    scale2 = (HD ** (-0.5)) * LOG2E
    core = me.at(other_core=True)
    load_hidden = pltpu.make_async_copy(hid_hbm, hid, local.at[0])
    load_queries = pltpu.make_async_copy(q_hbm, q, local.at[1])
    load_hidden.start()
    load_queries.start()

    def peer(distance):
        return (wrap(me.s + distance, owners), me.f)

    def enter(others):
        barrier = pltpu.get_barrier_semaphore()

        def greet(distance, carry):
            pl.semaphore_signal(barrier, inc=1, device_id=peer(distance), device_id_type=MESH)
            return carry

        for other in others:
            pl.semaphore_signal(barrier, inc=1, device_id=other, device_id_type=MESH)
        lax.fori_loop(1, owners, greet, 0)
        pl.semaphore_wait(barrier, owners - 1 + len(others))
        load_hidden.wait()

    def idle():
        load_queries.wait()
        for h in range(heads):
            qa[h * BLK : (h + 1) * BLK, 0:HD] = q[:, h * HD : (h + 1) * HD]
            qa[h * BLK : (h + 1) * BLK, HD : 2 * HD] = qseg_ref[...]
        m_ref[...] = jnp.full_like(m_ref, NEGATIVE)
        l_ref[...] = jnp.zeros_like(l_ref)
        acc_ref[...] = jnp.zeros_like(acc_ref)

    finish, opposite_arrived = project_part(
        me, hid, gain_ref, w_ref, first_ref, qseg_ref, freq_ref,
        nb, wb, fb, proj, res, begins, buf, ass, ars, local.at[2], enter, idle,
    )
    bounds = fb[11]
    low = bounds[0:1, :]
    high = bounds[1:2, :]
    kv_ref = buf.at[0, 0, z, c]

    def send(index, src, dst, target):
        remote(src, dst, ss.at[index], rs.at[index], target).start()

    def arrived(index, dst):
        remote(dst, dst, ss.at[index], rs.at[index], core).wait_recv()

    def block(rx, k, zi, cc):
        return buf.at[rx, k, wrap(z + zi, 2), cc]

    def mine(rx, k, zi):
        return block(rx, k, zi, c)

    order = (1, 3, 2)
    out_wrap = {rx: (x + rx >= 4).astype(jnp.int32) for rx in order}
    in_wrap = {rx: (x < rx).astype(jnp.int32) for rx in order}
    x1 = lambda rx, zi: 11 + 2 * (rx - 1) + zi
    x2 = lambda rx, zi: 17 + 2 * (rx - 1) + zi

    def second(rx, zi):
        w = out_wrap[rx]
        return remote(
            mine(0, 2 * w, zi), mine(rx, w, zi), ss.at[x2(rx, zi)], rs.at[x2(rx, zi)], me.at(dx=rx)
        )

    def send_second(zi, wraps):
        for rx in order:

            @pl.when(out_wrap[rx] == wraps)
            def _():
                second(rx, zi).start()

    def send_y(zi):
        send(3 + zi, mine(0, 0, zi), mine(0, 1, zi), me.at(dy=1))
        send(5 + zi, mine(0, 0, zi), mine(0, 2, zi), me.at(dy=2))
        send_second(zi, 0)

    def send_first(zi):
        for rx in order:
            send(x1(rx, zi), mine(0, 1, zi), mine(rx, 1 - out_wrap[rx], zi), me.at(dx=rx))

    def forward(first, then, rx, k, zi):
        arrived(first, mine(rx, k, zi))
        send(then, mine(rx, k, zi), mine(rx, k, zi), core)

    units = [
        (0, 0, 0, None, 0),
        (0, 1, 0, 3, 7),
        (0, 2, 0, 5, 9),
        (0, 0, 1, None, 2),
        (0, 1, 1, 4, 8),
        (0, 2, 1, 6, 10),
    ]
    for zi in (0, 1):
        units += [(rx, 1 - in_wrap[rx], zi, x1(rx, zi), x1(rx, zi) + 12) for rx in order]
        units += [(rx, in_wrap[rx], zi, x2(rx, zi), x2(rx, zi) + 12) for rx in order]
    turn = [0, 3, 1, 2, 4, 5, 6, 7, 8, 9, 10, 11, 12, 13, 14, 15, 16, 17]
    units = [units[i] for i in turn]

    send(0, kv_ref, block(0, 0, 0, c), core)
    send_y(0)

    row = lax.broadcasted_iota(jnp.int32, (owners * 8, BLK), 0)
    select = (row == target_ref[0:1, :]).astype(jnp.bfloat16)
    chosen_pages = jnp.dot(select, kv_ref[...], preferred_element_type=jnp.float32)
    pages_ref[...] = chosen_pages.astype(jnp.bfloat16).reshape(pages_ref.shape)
    pages[me.s] = pages_ref[me.s]

    quad_first = (me.y * 4 + x) * 4 * BLK
    place = 2 * z + c

    def step(source, first_key, causal):
        key = first_key + lax.broadcasted_iota(jnp.int32, (BLK, HD), 0)
        inside = (key >= low) & (key < high)
        bias = jnp.where(inside, 0.0, NEGATIVE).astype(jnp.bfloat16)
        keys = jnp.concatenate([source[:, 0:HD], bias], axis=1)
        scores = lax.dot_general(
            qa[...], keys, (((1,), (1,)), ((), ())), preferred_element_type=jnp.float32
        )
        if causal:
            row = lax.broadcasted_iota(jnp.int32, scores.shape, 0) & (BLK - 1)
            column = lax.broadcasted_iota(jnp.int32, scores.shape, 1)
            scores = jnp.where(column <= row, scores, NEGATIVE)
        old = m_ref[...]
        top = jnp.maximum(scores[:, 0:HD], scores[:, HD : 2 * HD])
        new = jnp.maximum(old, jnp.max(top, axis=1, keepdims=True) * scale2)
        weights = jnp.exp2(scores * scale2 - jnp.concatenate([new, new], axis=1))
        factor = jnp.exp2(old - new)
        m_ref[...] = new
        l_ref[...] = l_ref[...] * factor + (weights[:, 0:HD] + weights[:, HD : 2 * HD])
        update = jnp.dot(
            weights.astype(jnp.bfloat16), source[:, HD : 2 * HD], preferred_element_type=jnp.float32
        )
        acc_ref[...] = acc_ref[...] * factor + update

    step(block(0, 0, 0, c), quad_first + place * BLK, True)

    def chosen(n, field):
        value = 0
        for i, unit in enumerate(units):
            value = value + (n == i).astype(jnp.int32) * unit[field]
        return value

    def serve(i):
        rx, k, zi, first, then = units[i]
        if first is None:
            opposite_arrived()
            send(then, mine(rx, k, zi), mine(rx, k, zi), core)
        else:
            forward(first, then, rx, k, zi)
        if (rx, k) == (0, 1):
            send_first(zi)
        if (rx, k) == (0, 2):
            send_second(zi, 1)
        if (rx, k) == (0, 0):
            send_y(1)

    def one_unit(n, carry):
        for i in range(1, len(units)):

            @pl.when(n == i - 1)
            def _():
                serve(i)

        rx, k, zi, then = (chosen(n, field) for field in (0, 1, 2, 4))

        @pl.when(n < 8)
        def _():
            for i in range(8):

                @pl.when(n * 8 + i > 0)
                def _():
                    to = peer(n * 8 + i)
                    remote(pages_ref.at[to[0]], pages.at[me.s], ss.at[35], rs.at[35], to).start()

        def one_core(j, inner):
            cc = wrap(c + j, 2)
            source = block(rx, k, zi, cc)
            where = 2 * wrap(z + zi, 2) + cc

            @pl.when(j == 1)
            def _():
                arrived(then, source)

            distance = rx + 4 * k
            first_key = quad_first - distance * 4 * BLK + where * BLK
            skip = ((distance == 0) & (where >= place)) | ((distance == 8) & (where < place))

            @pl.when(jnp.logical_not(skip) & (first_key >= 0))
            def _():
                step(source, first_key, False)

            return inner

        return lax.fori_loop(0, 2, one_core, carry)

    lax.fori_loop(0, len(units), one_unit, 0)

    for h in range(heads):
        rows = slice(h * BLK, (h + 1) * BLK)
        total = jnp.sum(l_ref[rows, :], axis=1, keepdims=True)
        out_ref[:, h * HD : (h + 1) * HD] = (acc_ref[rows, :] / total).astype(out_ref.dtype)

    others = pl.ds(0, owners - 1)
    exchange = remote(pages_ref.at[others], pages.at[others], ss.at[35], rs.at[35], core)
    exchange.wait_recv()
    cache_ref[...] = pages[...]
    exchange.wait_send()
    for index in [0] + list(range(2, 35)):
        remote(kv_ref, block(0, 0, 0, c), ss.at[index], rs.at[index], core).wait_send()
    finish()


def layer(hidden, gain, weight, firsts, queries, query_onehot, freq, target):
    heads = queries.shape[1] // HD
    rows, width = hidden.shape
    columns = weight.shape[1]
    owners = lax.axis_size("seq")
    away = pl.BlockSpec(memory_space=pl.ANY)
    vmem = pl.BlockSpec(memory_space=pltpu.VMEM)
    return pl.pallas_call(
        layer_kernel,
        out_shape=(
            jax.ShapeDtypeStruct(queries.shape, jnp.bfloat16),
            jax.ShapeDtypeStruct((owners, 8, columns), jnp.bfloat16),
        ),
        in_specs=[away, vmem, away, vmem, away, vmem, vmem, vmem],
        out_specs=(vmem, vmem),
        scratch_shapes=[
            pltpu.VMEM(hidden.shape, jnp.bfloat16),
            pltpu.VMEM(queries.shape, jnp.bfloat16),
            pltpu.VMEM((2, 2, 4, rows, width // 4), jnp.bfloat16),
            pltpu.VMEM((16, 2, width // 32, columns), jnp.bfloat16),
            pltpu.VMEM((12, 8, HD), jnp.int32),
            pltpu.VMEM((4 * rows, columns), jnp.float32),
            pltpu.VMEM((2, 2 * rows, columns), jnp.bfloat16),
            pltpu.VMEM((2, 4 * rows, HD), jnp.float32),
            pltpu.SemaphoreType.DMA((70,)),
            pltpu.SemaphoreType.DMA((70,)),
            pltpu.SemaphoreType.DMA((3,)),
            pltpu.VMEM((4, 3, 2, 2, BLK, 2 * HD), jnp.bfloat16),
            pltpu.VMEM((owners, 8, columns), jnp.bfloat16),
            pltpu.VMEM((owners, 8, columns), jnp.bfloat16),
            pltpu.VMEM((heads * BLK, 2 * HD), jnp.bfloat16),
            pltpu.VMEM((heads * BLK, HD), jnp.float32),
            pltpu.VMEM((heads * BLK, HD), jnp.float32),
            pltpu.VMEM((heads * BLK, HD), jnp.float32),
            pltpu.SemaphoreType.DMA((36,)),
            pltpu.SemaphoreType.DMA((36,)),
        ],
        compiler_params=pltpu.CompilerParams(
            collective_id=0, has_side_effects=True, vmem_limit_bytes=52 << 20
        ),
        cost_estimate=pl.CostEstimate(
            flops=10_000_000_000, bytes_accessed=4_000_000, transcendentals=17_000_000
        ),
    )(hidden, gain, weight, firsts, queries, query_onehot, freq, target)


def on_device(hidden, norm_gain, kv_weight, queries, segment_ids, page_owner):
    seq_count = lax.axis_size("seq")
    seq_place = lax.axis_index("seq")
    block_rows = segment_ids.shape[0]
    stream_rows = block_rows * seq_count
    token_index = seq_place * block_rows + jnp.arange(block_rows, dtype=jnp.int32)
    lanes = jnp.arange(HD, dtype=jnp.int32)
    member = segment_ids[:, None] == lanes[None, :]
    wanted = jnp.stack([lanes, lanes + 1])
    hit = segment_ids[None, None, :] == wanted[:, :, None]
    firsts = jnp.min(jnp.where(hit, token_index[None, None, :], stream_rows), axis=2)
    first_tile = jnp.pad(firsts, ((0, 6), (0, 0)))
    freq = 10000.0 ** (-jnp.arange(HD // 2, dtype=jnp.float32) * 2.0 / HD)
    freq_tile = jnp.broadcast_to(jnp.concatenate([freq, freq])[None, :], (8, HD))

    pages_block = page_owner.shape[0]
    page_rows = block_rows // pages_block
    capacity = max(2, 2 * pages_block // seq_count)
    owners = page_owner[:, 0]
    order = jnp.arange(pages_block, dtype=jnp.int32)
    earlier = (owners[None, :] == owners[:, None]) & (order[None, :] < order[:, None])
    rank = jnp.sum(earlier.astype(jnp.int32), axis=1)
    slot = (owners * capacity + rank) * page_rows
    target = (slot[:, None] + jnp.arange(page_rows, dtype=jnp.int32)[None, :]).reshape(1, block_rows)
    target_tile = jnp.broadcast_to(target, (8, block_rows))

    attended, arrived = layer(
        hidden,
        norm_gain[None, :],
        kv_weight,
        first_tile,
        queries,
        member.astype(jnp.bfloat16),
        freq_tile,
        target_tile,
    )
    kv_cache = arrived.reshape(1, seq_count, capacity, page_rows, arrived.shape[2])
    return (attended, kv_cache)


def solution(mesh):
    placed = (P(("seq", "fs"), None), P(), P("seq", "fs"), P("seq", "fs"), P("seq"), P("seq", None))
    return jax.shard_map(
        on_device,
        mesh=mesh,
        in_specs=placed,
        out_specs=(P("seq", "fs"), P("seq", None, None, None, "fs")),
        check_vma=False,
    )
```

```python
import functools

import jax
import jax.numpy as jnp
from jax import lax
from jax.experimental import pallas as pl
from jax.experimental.pallas import tpu as pltpu
from jax.sharding import PartitionSpec as P

HD = 128
SEGS = 4
EPSILON = 1e-05
NEGATIVE = -1e30
LOG2E = 1.4426950408889634
MESH = pl.DeviceIdType.MESH
BLK = 256


def wrap(value, count):
    return value - count * (value >= count).astype(jnp.int32)


class Place:
    def __init__(self):
        s = lax.axis_index("seq")
        self.s = s
        self.f = lax.axis_index("fs")
        self.c = lax.rem(s, 2)
        self.z = lax.rem(lax.div(s, 2), 2)
        self.x = lax.rem(lax.div(s, 4), 4)
        self.y = lax.div(s, 16)

    def at(self, dy=0, dx=0, other_z=False, other_core=False):
        y = wrap(self.y + dy, 4)
        x = wrap(self.x + dx, 4)
        z = 1 - self.z if other_z else self.z
        c = 1 - self.c if other_core else self.c
        return (((y * 4 + x) * 2 + z) * 2 + c, self.f)


def remote(src, dst, send, recv, target):
    return pltpu.make_async_remote_copy(
        src_ref=src, dst_ref=dst, send_sem=send, recv_sem=recv, device_id=target, device_id_type=MESH
    )


def project_part(
    me, hid_ref, gain_ref, w_ref, first_ref, qseg_ref, freq_ref,
    nb, wb, fb, acc, res, begins, buf, ss, rs, local, enter, idle
):
    c, z, x, y, f = me.c, me.z, me.x, me.y, me.f
    parity, group = lax.rem(f, 2), lax.div(f, 2)
    head = parity + 2 * c
    twin = lax.rem(f + 2, 4)
    mate = f + 1 - 2 * parity
    home = c == group
    chunks, rows, cols = nb.shape[2], nb.shape[3], nb.shape[4]

    def near(zz, cc, ff):
        return (((y * 4 + x) * 2 + zz) * 2 + cc, ff)

    core = near(z, 1 - c, f)
    ring_x = {k: me.at(dx=k) for k in (1, 2, 3)}
    ring_y = {k: me.at(dy=k) for k in (1, 2, 3)}
    enter([near(zz, cc, twin) for zz in (z, 1 - z) for cc in (c, 1 - c)] + [near(z, c, mate)])

    started = []

    def send(index, src, dst, target, recv=None):
        recv = index if recv is None else recv
        copy = remote(src, dst, ss.at[index], rs.at[recv], target)
        copy.start()
        started.append(copy)

    def arrived(index, dst):
        remote(dst, dst, ss.at[index], rs.at[index], core).wait_recv()

    quad = y * 4 + x
    shard = 2 * z + c
    rows_w = w_ref.shape[0]

    def piece(zz, cc):
        return wb.at[quad, zz, pl.ds(pl.multiple_of(cc * rows_w, rows_w), rows_w)]

    def seed_to_core():
        return remote(w_ref, piece(z, c), ss.at[0], rs.at[shard], core)

    @pl.when(home)
    def _():
        pltpu.make_async_copy(w_ref, piece(z, c), local).start()

    @pl.when(jnp.logical_not(home))
    def _():
        seed_to_core().start()

    send(1, w_ref, piece(z, c), near(z, group, twin), shard)
    send(2, w_ref, piece(z, c), near(1 - z, group, f), shard)
    send(3, w_ref, piece(z, c), near(1 - z, group, twin), shard)
    send(4, first_ref, fb.at[0], core)
    send(5, first_ref, fb.at[1], near(1 - z, c, f))
    send(6, first_ref, fb.at[2], near(1 - z, 1 - c, f))

    total = jnp.zeros((rows, 1), jnp.float32)
    for i in range(chunks):
        wide = hid_ref[:, i * cols : (i + 1) * cols].astype(jnp.float32)
        total = total + jnp.sum(wide * wide, axis=1, keepdims=True)
    factor = lax.rsqrt(total / (chunks * cols) + EPSILON)
    for i in range(chunks):
        wide = hid_ref[:, i * cols : (i + 1) * cols].astype(jnp.float32)
        gain = gain_ref[:, i * cols : (i + 1) * cols].astype(jnp.float32)
        nb[c, parity, i] = (wide * factor * gain).astype(jnp.bfloat16)
        send(13 + i, nb.at[c, parity, i], nb.at[c, parity, i], near(z, c, mate))
        send(17 + i, nb.at[c, parity, i], nb.at[c, parity, i], core)

    def seed_arrived(zz):
        for cc in (0, 1):
            own = jnp.logical_and(home, shard == 2 * zz + cc)

            @pl.when(own)
            def _():
                pltpu.make_async_copy(w_ref, piece(zz, cc), local).wait()

            @pl.when(jnp.logical_not(own))
            def _():
                arrived(2 * zz + cc, piece(zz, cc))

    half = lambda yy, xx, hh: wb.at[yy * 4 + xx, hh]
    back = lambda v, k: lax.rem(v + 4 - k, 4)
    order = (1, 3, 2)
    seed_arrived(0)
    for k in (1, 3):
        send(24 + k, half(y, x, 0), half(y, x, 0), ring_x[k])
    seed_arrived(1)
    for k in (1, 3):
        send(27 + k, half(y, x, 1), half(y, x, 1), ring_y[k])

    a2 = lambda k, j: 31 + (k - 1) * 4 + j
    b2 = lambda k, j: 43 + (k - 1) * 4 + j

    cut = wb.shape[2] // 2
    lower = lambda yy, xx, hh: wb.at[yy * 4 + xx, hh, 0:cut]
    upper = lambda yy, xx, hh: wb.at[yy * 4 + xx, hh, cut : 2 * cut]

    def spread(j):
        ya, xa = y, back(x, j)
        yb, xb = back(y, j), x
        for k in (1, 3):
            send(a2(k, j), half(ya, xa, 0), half(ya, xa, 0), ring_y[k])
            send(b2(k, j), half(yb, xb, 1), half(yb, xb, 1), ring_x[k])

    def pass_on(firsts, halves, near_by, ring):
        arrived(firsts[0], half(*near_by(1)))
        send(halves[0], lower(*near_by(1)), lower(*near_by(1)), ring[1])
        arrived(firsts[1], half(*near_by(3)))
        send(halves[1], upper(*near_by(3)), upper(*near_by(3)), ring[3])

    def far_arrived(halves, at):
        arrived(halves[0], lower(*at))
        arrived(halves[1], upper(*at))

    def relay_first():
        pass_on((25, 27), (26, 60), lambda k: (y, back(x, k), 0), ring_x)
        pass_on((28, 30), (29, 61), lambda k: (back(y, k), x, 1), ring_y)

    def relay(j):
        pass_on(
            (a2(1, j), a2(3, j)), (a2(2, j), 62 + j), lambda k: (back(y, k), back(x, j), 0), ring_y
        )
        pass_on(
            (b2(1, j), b2(3, j)), (b2(2, j), 66 + j), lambda k: (back(y, j), back(x, k), 1), ring_x
        )

    def forward(i):
        arrived(13 + i, nb.at[c, 1 - parity, i])
        send(21 + i, nb.at[c, 1 - parity, i], nb.at[c, 1 - parity, i], core)

    spread(0)
    idle()
    for i in range(3):
        arrived(4 + i, fb.at[i])
    fb[3] = jnp.minimum(jnp.minimum(first_ref[...], fb[0]), jnp.minimum(fb[1], fb[2]))
    for k in order:
        send(6 + k, fb.at[3], fb.at[3 + k], ring_x[k])
    forward(0)
    relay_first()
    spread(1)
    spread(3)
    far_arrived((26, 60), (y, back(x, 2), 0))
    far_arrived((29, 61), (back(y, 2), x, 1))
    spread(2)
    forward(1)
    relay(0)
    for k in order:
        arrived(6 + k, fb.at[3 + k])
    fb[7] = jnp.minimum(jnp.minimum(fb[3], fb[4]), jnp.minimum(fb[5], fb[6]))
    for k in order:
        send(9 + k, fb.at[7], fb.at[7 + k], ring_y[k])
    relay(1)
    forward(2)
    relay(3)
    relay(2)
    forward(3)
    for k in order:
        arrived(9 + k, fb.at[7 + k])
    fb[11] = jnp.minimum(jnp.minimum(fb[7], fb[8]), jnp.minimum(fb[9], fb[10]))
    first_row = fb[11][0:1, :].astype(jnp.float32)
    begin = jnp.sum(qseg_ref[...].astype(jnp.float32) * first_row, axis=1, keepdims=True)
    begins[c] = jnp.broadcast_to(begin, begins.shape[1:])
    send(59, begins.at[c], begins.at[c], core)
    for i in range(chunks):
        arrived(17 + i, nb.at[1 - c, parity, i])
        arrived(21 + i, nb.at[1 - c, 1 - parity, i])

    acc[...] = jnp.zeros_like(acc)

    def multiply(yy, xx, hh):
        columns = pl.ds(pl.multiple_of(xx * 512 + hh * 256, 256), 256)
        lhs = nb[:, :, yy, :, columns].reshape(4 * rows, 256)
        acc[...] += jnp.dot(lhs, wb[yy * 4 + xx, hh], preferred_element_type=jnp.float32)

    multiply(y, x, 0)
    multiply(y, x, 1)
    for j in order:
        multiply(y, back(x, j), 0)
        multiply(back(y, j), x, 1)
    for k in (1, 3, 2):
        for j in (0, 1, 3, 2):
            ya, xa = back(y, k), back(x, j)
            yb, xb = back(y, j), back(x, k)
            if k == 2:
                far_arrived((a2(2, j), 62 + j), (ya, xa, 0))
            multiply(ya, xa, 0)
            if k == 2:
                far_arrived((b2(2, j), 66 + j), (yb, xb, 1))
            multiply(yb, xb, 1)

    arrived(59, begins.at[1 - c])
    pair = 2 * rows
    rows_g = pl.ds(pl.multiple_of(group * pair, pair), pair)
    lane = lax.broadcasted_iota(jnp.int32, (pair, HD), 1)
    for cc in (0, 1):
        first_token = (me.s - c + cc) * BLK + group * pair
        token = first_token + lax.broadcasted_iota(jnp.int32, (pair, HD), 0)
        angle = (token.astype(jnp.float32) - begins[cc, rows_g, :]) * freq_ref[0:1, :]
        sine = jnp.sin(angle)
        sine = jnp.where(lane < HD // 2, -sine, sine)
        keys = acc[cc * pair : (cc + 1) * pair, 0:HD]
        swapped = jnp.concatenate([keys[:, HD // 2 :], keys[:, : HD // 2]], axis=1)
        turned = keys * jnp.cos(angle) + swapped * sine
        res[cc, :, 0:HD] = turned.astype(jnp.bfloat16)
        res[cc, :, HD:] = acc[cc * pair : (cc + 1) * pair, HD:].astype(jnp.bfloat16)

    def part(zz, cc, g):
        return buf.at[0, 0, zz, cc, pl.ds(pl.multiple_of(g * pair, pair), pair)]

    def result_to(zz, cc, ff, index, recv):
        return remote(
            res.at[cc], part(z, cc, group), ss.at[index], rs.at[recv + group], near(zz, cc, ff)
        )

    @pl.when(home)
    def _():
        result_to(z, 1 - c, f, 55, 55).start()
        result_to(1 - z, 0, f, 57, 57).start()
        result_to(1 - z, 1, f, 58, 57).start()
        buf[0, 0, z, c, rows_g, :] = res[c]

    @pl.when(jnp.logical_not(home))
    def _():
        result_to(z, 0, twin, 55, 55).start()
        result_to(z, 1, twin, 56, 55).start()
        result_to(1 - z, 0, twin, 57, 57).start()
        result_to(1 - z, 1, twin, 58, 57).start()

    for g in (0, 1):

        @pl.when(jnp.logical_not(jnp.logical_and(home, group == g)))
        def _():
            arrived(55 + g, part(z, c, g))

    def opposite_arrived():
        for g in (0, 1):
            arrived(57 + g, part(1 - z, c, g))

    def finish():
        for copy in started:
            copy.wait_send()

        @pl.when(home)
        def _():
            result_to(z, 1 - c, f, 55, 55).wait_send()

        @pl.when(jnp.logical_not(home))
        def _():
            seed_to_core().wait_send()
            result_to(z, 0, twin, 55, 55).wait_send()
            result_to(z, 1, twin, 56, 55).wait_send()

        result_to(1 - z, 0, f, 57, 57).wait_send()
        result_to(1 - z, 1, f, 58, 57).wait_send()

    return finish, opposite_arrived


def layer_kernel(
    hid_hbm, gain_ref, w_ref, first_ref, q_hbm, qseg_ref, freq_ref, target_ref,
    out_ref, cache_ref,
    hid, q, nb, wb, fb, proj, res, begins, ass, ars, local,
    buf, pages, pages_ref, qa, m_ref, l_ref, acc_ref, ss, rs
):
    me = Place()
    c, z, x = me.c, me.z, me.x
    heads = q.shape[1] // HD
    owners = pages_ref.shape[0]
    scale2 = (HD ** (-0.5)) * LOG2E
    core = me.at(other_core=True)
    load_hidden = pltpu.make_async_copy(hid_hbm, hid, local.at[0])
    load_queries = pltpu.make_async_copy(q_hbm, q, local.at[1])
    load_hidden.start()
    load_queries.start()

    def peer(distance):
        return (wrap(me.s + distance, owners), me.f)

    def enter(others):
        barrier = pltpu.get_barrier_semaphore()

        def greet(distance, carry):
            pl.semaphore_signal(barrier, inc=1, device_id=peer(distance), device_id_type=MESH)
            return carry

        for other in others:
            pl.semaphore_signal(barrier, inc=1, device_id=other, device_id_type=MESH)
        lax.fori_loop(1, owners, greet, 0)
        pl.semaphore_wait(barrier, owners - 1 + len(others))
        load_hidden.wait()

    def idle():
        load_queries.wait()
        for h in range(heads):
            qa[h * BLK : (h + 1) * BLK, 0:HD] = q[:, h * HD : (h + 1) * HD]
            qa[h * BLK : (h + 1) * BLK, HD : 2 * HD] = qseg_ref[...]
        m_ref[...] = jnp.full_like(m_ref, NEGATIVE)
        l_ref[...] = jnp.zeros_like(l_ref)
        acc_ref[...] = jnp.zeros_like(acc_ref)

    finish, opposite_arrived = project_part(
        me, hid, gain_ref, w_ref, first_ref, qseg_ref, freq_ref,
        nb, wb, fb, proj, res, begins, buf, ass, ars, local.at[2], enter, idle,
    )
    bounds = fb[11]
    low = bounds[0:1, :]
    high = bounds[1:2, :]
    kv_ref = buf.at[0, 0, z, c]

    def send(index, src, dst, target):
        remote(src, dst, ss.at[index], rs.at[index], target).start()

    def arrived(index, dst):
        remote(dst, dst, ss.at[index], rs.at[index], core).wait_recv()

    def block(rx, k, zi, cc):
        return buf.at[rx, k, wrap(z + zi, 2), cc]

    def mine(rx, k, zi):
        return block(rx, k, zi, c)

    order = (1, 3, 2)
    out_wrap = {rx: (x + rx >= 4).astype(jnp.int32) for rx in order}
    in_wrap = {rx: (x < rx).astype(jnp.int32) for rx in order}
    x1 = lambda rx, zi: 11 + 2 * (rx - 1) + zi
    x2 = lambda rx, zi: 17 + 2 * (rx - 1) + zi

    def second(rx, zi):
        w = out_wrap[rx]
        return remote(
            mine(0, 2 * w, zi), mine(rx, w, zi), ss.at[x2(rx, zi)], rs.at[x2(rx, zi)], me.at(dx=rx)
        )

    def send_second(zi, wraps):
        for rx in order:

            @pl.when(out_wrap[rx] == wraps)
            def _():
                second(rx, zi).start()

    def send_y(zi):
        send(3 + zi, mine(0, 0, zi), mine(0, 1, zi), me.at(dy=1))
        send(5 + zi, mine(0, 0, zi), mine(0, 2, zi), me.at(dy=2))
        send_second(zi, 0)

    def send_first(zi):
        for rx in order:
            send(x1(rx, zi), mine(0, 1, zi), mine(rx, 1 - out_wrap[rx], zi), me.at(dx=rx))

    def forward(first, then, rx, k, zi):
        arrived(first, mine(rx, k, zi))
        send(then, mine(rx, k, zi), mine(rx, k, zi), core)

    units = [
        (0, 0, 0, None, 0),
        (0, 1, 0, 3, 7),
        (0, 2, 0, 5, 9),
        (0, 0, 1, None, 2),
        (0, 1, 1, 4, 8),
        (0, 2, 1, 6, 10),
    ]
    for zi in (0, 1):
        units += [(rx, 1 - in_wrap[rx], zi, x1(rx, zi), x1(rx, zi) + 12) for rx in order]
        units += [(rx, in_wrap[rx], zi, x2(rx, zi), x2(rx, zi) + 12) for rx in order]
    turn = [0, 3, 1, 2, 4, 5, 6, 7, 8, 9, 10, 11, 12, 13, 14, 15, 16, 17]
    units = [units[i] for i in turn]
    served_at = [0, 0, 0, 1, 1, 2] + [i - 1 for i in range(6, len(units))]

    send(0, kv_ref, block(0, 0, 0, c), core)
    send_y(0)

    row = lax.broadcasted_iota(jnp.int32, (owners * 8, BLK), 0)
    select = (row == target_ref[0:1, :]).astype(jnp.bfloat16)
    chosen_pages = jnp.dot(select, kv_ref[...], preferred_element_type=jnp.float32)
    pages_ref[...] = chosen_pages.astype(jnp.bfloat16).reshape(pages_ref.shape)
    pages[me.s] = pages_ref[me.s]

    quad_first = (me.y * 4 + x) * 4 * BLK
    place = 2 * z + c

    def step(source, first_key, causal):
        key = first_key + lax.broadcasted_iota(jnp.int32, (BLK, HD), 0)
        inside = (key >= low) & (key < high)
        bias = jnp.where(inside, 0.0, NEGATIVE).astype(jnp.bfloat16)
        keys = jnp.concatenate([source[:, 0:HD], bias], axis=1)
        scores = lax.dot_general(
            qa[...], keys, (((1,), (1,)), ((), ())), preferred_element_type=jnp.float32
        )
        if causal:
            row = lax.broadcasted_iota(jnp.int32, scores.shape, 0) & (BLK - 1)
            column = lax.broadcasted_iota(jnp.int32, scores.shape, 1)
            scores = jnp.where(column <= row, scores, NEGATIVE)
        old = m_ref[...]
        top = jnp.maximum(scores[:, 0:HD], scores[:, HD : 2 * HD])
        new = jnp.maximum(old, jnp.max(top, axis=1, keepdims=True) * scale2)
        weights = jnp.exp2(scores * scale2 - jnp.concatenate([new, new], axis=1))
        factor = jnp.exp2(old - new)
        m_ref[...] = new
        l_ref[...] = l_ref[...] * factor + (weights[:, 0:HD] + weights[:, HD : 2 * HD])
        update = jnp.dot(
            weights.astype(jnp.bfloat16), source[:, HD : 2 * HD], preferred_element_type=jnp.float32
        )
        acc_ref[...] = acc_ref[...] * factor + update

    step(block(0, 0, 0, c), quad_first + place * BLK, True)

    def chosen(n, field):
        value = 0
        for i, unit in enumerate(units):
            value = value + (n == i).astype(jnp.int32) * unit[field]
        return value

    def serve(i):
        rx, k, zi, first, then = units[i]
        if first is None:
            opposite_arrived()
            send(then, mine(rx, k, zi), mine(rx, k, zi), core)
        else:
            forward(first, then, rx, k, zi)
        if (rx, k) == (0, 1):
            send_first(zi)
        if (rx, k) == (0, 2):
            send_second(zi, 1)
        if (rx, k) == (0, 0):
            send_y(1)

    def one_unit(n, carry):
        for i in range(1, len(units)):

            @pl.when(n == served_at[i])
            def _():
                serve(i)

        rx, k, zi, then = (chosen(n, field) for field in (0, 1, 2, 4))

        @pl.when(n < 8)
        def _():
            for i in range(8):

                @pl.when(n * 8 + i > 0)
                def _():
                    to = peer(n * 8 + i)
                    remote(pages_ref.at[to[0]], pages.at[me.s], ss.at[35], rs.at[35], to).start()

        def one_core(j, inner):
            cc = wrap(c + j, 2)
            source = block(rx, k, zi, cc)
            where = 2 * wrap(z + zi, 2) + cc

            @pl.when(j == 1)
            def _():
                arrived(then, source)

            distance = rx + 4 * k
            first_key = quad_first - distance * 4 * BLK + where * BLK
            skip = ((distance == 0) & (where >= place)) | ((distance == 8) & (where < place))

            @pl.when(jnp.logical_not(skip) & (first_key >= 0))
            def _():
                step(source, first_key, False)

            return inner

        return lax.fori_loop(0, 2, one_core, carry)

    lax.fori_loop(0, len(units), one_unit, 0)

    for h in range(heads):
        rows = slice(h * BLK, (h + 1) * BLK)
        total = jnp.sum(l_ref[rows, :], axis=1, keepdims=True)
        out_ref[:, h * HD : (h + 1) * HD] = (acc_ref[rows, :] / total).astype(out_ref.dtype)

    others = pl.ds(0, owners - 1)
    exchange = remote(pages_ref.at[others], pages.at[others], ss.at[35], rs.at[35], core)
    exchange.wait_recv()
    cache_ref[...] = pages[...]
    exchange.wait_send()
    for index in [0] + list(range(2, 35)):
        remote(kv_ref, block(0, 0, 0, c), ss.at[index], rs.at[index], core).wait_send()
    finish()


def layer(hidden, gain, weight, firsts, queries, query_onehot, freq, target):
    heads = queries.shape[1] // HD
    rows, width = hidden.shape
    columns = weight.shape[1]
    owners = lax.axis_size("seq")
    away = pl.BlockSpec(memory_space=pl.ANY)
    vmem = pl.BlockSpec(memory_space=pltpu.VMEM)
    return pl.pallas_call(
        layer_kernel,
        out_shape=(
            jax.ShapeDtypeStruct(queries.shape, jnp.bfloat16),
            jax.ShapeDtypeStruct((owners, 8, columns), jnp.bfloat16),
        ),
        in_specs=[away, vmem, away, vmem, away, vmem, vmem, vmem],
        out_specs=(vmem, vmem),
        scratch_shapes=[
            pltpu.VMEM(hidden.shape, jnp.bfloat16),
            pltpu.VMEM(queries.shape, jnp.bfloat16),
            pltpu.VMEM((2, 2, 4, rows, width // 4), jnp.bfloat16),
            pltpu.VMEM((16, 2, width // 32, columns), jnp.bfloat16),
            pltpu.VMEM((12, 8, HD), jnp.int32),
            pltpu.VMEM((4 * rows, columns), jnp.float32),
            pltpu.VMEM((2, 2 * rows, columns), jnp.bfloat16),
            pltpu.VMEM((2, 4 * rows, HD), jnp.float32),
            pltpu.SemaphoreType.DMA((70,)),
            pltpu.SemaphoreType.DMA((70,)),
            pltpu.SemaphoreType.DMA((3,)),
            pltpu.VMEM((4, 3, 2, 2, BLK, 2 * HD), jnp.bfloat16),
            pltpu.VMEM((owners, 8, columns), jnp.bfloat16),
            pltpu.VMEM((owners, 8, columns), jnp.bfloat16),
            pltpu.VMEM((heads * BLK, 2 * HD), jnp.bfloat16),
            pltpu.VMEM((heads * BLK, HD), jnp.float32),
            pltpu.VMEM((heads * BLK, HD), jnp.float32),
            pltpu.VMEM((heads * BLK, HD), jnp.float32),
            pltpu.SemaphoreType.DMA((36,)),
            pltpu.SemaphoreType.DMA((36,)),
        ],
        compiler_params=pltpu.CompilerParams(
            collective_id=0, has_side_effects=True, vmem_limit_bytes=52 << 20
        ),
        cost_estimate=pl.CostEstimate(
            flops=10_000_000_000, bytes_accessed=4_000_000, transcendentals=17_000_000
        ),
    )(hidden, gain, weight, firsts, queries, query_onehot, freq, target)


def on_device(hidden, norm_gain, kv_weight, queries, segment_ids, page_owner):
    seq_count = lax.axis_size("seq")
    seq_place = lax.axis_index("seq")
    block_rows = segment_ids.shape[0]
    stream_rows = block_rows * seq_count
    token_index = seq_place * block_rows + jnp.arange(block_rows, dtype=jnp.int32)
    lanes = jnp.arange(HD, dtype=jnp.int32)
    member = segment_ids[:, None] == lanes[None, :]
    wanted = jnp.stack([lanes, lanes + 1])
    hit = segment_ids[None, None, :] == wanted[:, :, None]
    firsts = jnp.min(jnp.where(hit, token_index[None, None, :], stream_rows), axis=2)
    first_tile = jnp.pad(firsts, ((0, 6), (0, 0)))
    freq = 10000.0 ** (-jnp.arange(HD // 2, dtype=jnp.float32) * 2.0 / HD)
    freq_tile = jnp.broadcast_to(jnp.concatenate([freq, freq])[None, :], (8, HD))

    pages_block = page_owner.shape[0]
    page_rows = block_rows // pages_block
    capacity = max(2, 2 * pages_block // seq_count)
    owners = page_owner[:, 0]
    order = jnp.arange(pages_block, dtype=jnp.int32)
    earlier = (owners[None, :] == owners[:, None]) & (order[None, :] < order[:, None])
    rank = jnp.sum(earlier.astype(jnp.int32), axis=1)
    slot = (owners * capacity + rank) * page_rows
    target = (slot[:, None] + jnp.arange(page_rows, dtype=jnp.int32)[None, :]).reshape(1, block_rows)
    target_tile = jnp.broadcast_to(target, (8, block_rows))

    attended, arrived = layer(
        hidden,
        norm_gain[None, :],
        kv_weight,
        first_tile,
        queries,
        member.astype(jnp.bfloat16),
        freq_tile,
        target_tile,
    )
    kv_cache = arrived.reshape(1, seq_count, capacity, page_rows, arrived.shape[2])
    return (attended, kv_cache)


def solution(mesh):
    placed = (P(("seq", "fs"), None), P(), P("seq", "fs"), P("seq", "fs"), P("seq"), P("seq", None))
    return jax.shard_map(
        on_device,
        mesh=mesh,
        in_specs=placed,
        out_specs=(P("seq", "fs"), P("seq", None, None, None, "fs")),
        check_vma=False,
    )
```
